32 devices in a mesh: dp: 8 (over z, y), expert: 4 (over x, core).
Axes of the slice: x: 2, y: 2, z: 4, core: 2. Of those that a mesh axis runs over, the one named last changes fastest.
Arguments:
- tokens: bfloat16 [2, 2048, 1536], P(None, ('dp', 'expert')), may hold values from -6 to 6
- cotangent: bfloat16 [2, 2048, 1536], P(None, ('dp', 'expert')), may hold values from -6 to 6
- attn_gain: bfloat16 [1536], P(('dp', 'expert')), may hold values from 0.099609375 to 1.8984375
- mlp_gain: bfloat16 [1536], P(('dp', 'expert')), may hold values from 0.099609375 to 1.8984375
- w_query: bfloat16 [1536, 1536], P(('dp', 'expert')), may hold values from -1.25 to 1.25
- w_key: bfloat16 [1536, 512], P(('dp', 'expert')), may hold values from -1.25 to 1.25
- w_value: bfloat16 [1536, 512], P(('dp', 'expert')), may hold values from -0.15625 to 0.15625
- w_out: bfloat16 [1536, 1536], P(('dp', 'expert')), may hold values from -6 to 6
- w_router: bfloat16 [1536, 20], P(('dp', 'expert')), may hold values from -0.1875 to 0.1875
- w_gate: bfloat16 [20, 1536, 512], P('expert', 'dp'), may hold values from -0.15625 to 0.15625
- w_up: bfloat16 [20, 1536, 512], P('expert', 'dp'), may hold values from -0.15625 to 0.15625
- w_down: bfloat16 [20, 512, 1536], P('expert', 'dp'), may hold values from -6 to 6
- shuffle: int32 [2, 32, 64], P(None, ('dp', 'expert')), may hold values from 0 to 63, each once within a row
- routes: int32 [2, 2048, 8], P(None, ('dp', 'expert')), may hold values from 0 to 19, all different within a row; in each aligned block of 64 rows (0 to 63, 64 to 127, ..., all dimensions but the last counted through in order) at most 32 rows name the same one
- lengths: int32 [2, 8, 1], P(None, 'dp'), may hold values from 256 to 256, as said below
Outputs:
- output: bfloat16 [2, 2048, 1536], P(None, ('dp', 'expert'))
- grad_tokens: float32 [2, 2048, 1536], P(None, ('dp', 'expert'))
- grad_attn_gain: float32 [1536], P(('dp', 'expert'))
- grad_mlp_gain: float32 [1536], P(('dp', 'expert'))
- grad_w_query: float32 [1536, 1536], P(('dp', 'expert'))
- grad_w_key: float32 [1536, 512], P(('dp', 'expert'))
- grad_w_value: float32 [1536, 512], P(('dp', 'expert'))
- grad_w_out: float32 [1536, 1536], P(('dp', 'expert'))
- grad_w_router: float32 [1536, 20], P(('dp', 'expert'))
- grad_w_gate: float32 [20, 1536, 512], P('expert', 'dp')
- grad_w_up: float32 [20, 1536, 512], P('expert', 'dp')
- grad_w_down: float32 [20, 512, 1536], P('expert', 'dp')
The draws below stay inside these ranges and needn't reach their ends.
Inputs may be any that keep to these rules, and one draw needn't show every extreme that they name: `shuffle`: each device's entries are each number once. `routes`: each row names 8 different experts. In the dealt rows of one device (aligned blocks of 64 rows) no expert is named by more than 32 rows, a bound that some block reaches. `lengths`: A group's entries sum to 256; its documents come first, each of 256 tokens or more, and the entries after them are 0. Group 0 of every micro-batch is one document of 256 tokens.
All inputs are finite; a program needn't handle non-finite values.
Results may differ from the reference program's by a relative error of at most 0.018.
The reference program's roundings to bfloat16 on the way count: a program that leaves them out, or rounds other values in their place, can miss the bound.
Values may be sent and summed in bfloat16 or wider, within the bound.
No kernel may reach another device: no remote copies, remote signals or barrier semaphores. Data moves between devices by JAX's collectives and lax.ppermute only.
A program may use at most 192 MiB of HBM per device.

```python
import math
import jax
import jax.numpy as jnp
import numpy as np
from jax import lax

D = 1536
HEADS = 24
KV_HEADS = 8
HEAD_DIM = 64
FF = 512
TOP = 8
MICRO = 2
ROWS = 64
EXPERTS = 20
SHARDS = 32
TOKENS_MB = 2048
GROUP_TOK = 256
PEER_ROWS = 8
MIN_DOC = 256
DOCS = 1
CAP = 32
N_DP = 8
N_EXPERT = 4


def draw_lengths(key, part):
    count_key = jax.random.fold_in(key, 11)
    cut_key = jax.random.fold_in(key, 23)
    doc_count = jax.random.randint(count_key, (MICRO, N_DP), 1, DOCS + 1).astype(jnp.int32)
    group_iota = jnp.arange(N_DP, dtype=jnp.int32)
    doc_count = jnp.where(group_iota[None, :] == 0, 1, doc_count).astype(jnp.int32)
    spare = (GROUP_TOK - doc_count * MIN_DOC).astype(jnp.int32)
    cuts = jax.random.randint(cut_key, (MICRO, N_DP, DOCS - 1), 0, spare[:, :, None] + 1).astype(jnp.int32)
    cut_iota = jnp.arange(DOCS - 1, dtype=jnp.int32)
    cuts = jnp.where(cut_iota[None, None, :] < doc_count[:, :, None] - 1, cuts, spare[:, :, None])
    cuts = jnp.sort(cuts, -1)
    edges = jnp.concatenate([jnp.zeros((MICRO, N_DP, 1), jnp.int32), cuts, spare[:, :, None]], -1)
    extra = edges[:, :, 1:] - edges[:, :, :-1]
    doc_iota = jnp.arange(DOCS, dtype=jnp.int32)
    present = (doc_iota[None, None, :] < doc_count[:, :, None]).astype(jnp.int32)
    return (extra + MIN_DOC * present).astype(jnp.int32)


def block_scale(stream_key, shape, shards, low, top_value):
    level = 1.0
    for dim, shards_of in shards:
        steps = jax.random.uniform(jax.random.fold_in(jax.random.fold_in(stream_key, 6), dim), (shards_of,), jnp.float32, low / len(shards), top_value / len(shards))
        level = level * jnp.repeat(jnp.exp(steps), shape[dim] // shards_of).reshape((-1,) + (1,) * (len(shape) - 1 - dim))
    return level


def shared_out(own_key, own, number, rows, count, top, bound, skew):
    sequence = jax.random.permutation(own_key, count)
    packed, common = portions_of(count, rows * top, bound, skew, True), portions_of(count, rows * top, bound, skew, False)
    places = jnp.arange(count)

    def named(tallies, rotation):
        used = int((tallies > 0).sum())
        fixed = max(1, used // 4)
        shifted = fixed + (places - fixed + rotation * (used - fixed)) % max(1, count - fixed)
        return jnp.zeros((count,), jnp.int32).at[sequence[jnp.where(places < fixed, places, shifted)]].set(jnp.asarray(tallies, jnp.int32))

    tallies = jnp.where(number % 4 == 0, named(packed, number // 4), named(common, number - number // 4 - 1))
    mixed = jax.random.permutation(jax.random.fold_in(own, 3), count)
    donor, receiver = mixed[0:count // 2 * 2:2], mixed[1:count // 2 * 2:2]
    slack = jnp.minimum(tallies[donor] - 1, bound - tallies[receiver]) // 2
    slack = jnp.where((donor == sequence[0]) | (receiver == sequence[0]) | (tallies[receiver] == 0), 0, jnp.maximum(slack, 0))
    shifted = jax.random.randint(jax.random.fold_in(own, 4), (count // 2,), 0, 1 << 20) % (slack + 1)
    tallies = tallies.at[donor].add(-shifted).at[receiver].add(shifted)
    labels = jnp.searchsorted(jnp.cumsum(tallies), jnp.arange(rows * top), side="right").astype(jnp.int32)
    grid = labels.reshape(top, rows).T
    grid = grid[jax.random.permutation(jax.random.fold_in(own, 1), rows)]
    rotation = jax.random.randint(jax.random.fold_in(own, 2), (rows, 1), 0, top)
    return jnp.take_along_axis(grid, (jnp.arange(top)[None, :] + rotation) % top, axis=1)


def portions_of(number_of, total, bound, skew, full):
    weights = [(1 << 20) // math.isqrt(grade ** skew) + 1 for grade in range(1, number_of + 1)]
    largest = bound if full else min(bound, max(-(-total // number_of), total * weights[0] // sum(weights)))
    least = 1 if total - largest >= number_of - 1 else 0
    given, spare = [largest] + [least] * (number_of - 1), total - largest - least * (number_of - 1)
    while spare > 0:
        candidates = [i for i in range(1, number_of) if given[i] < largest] or [i for i in range(1, number_of) if given[i] < bound]
        pool, remaining = sum([weights[i] for i in candidates]), spare
        for i in candidates:
            addition = min(bound - given[i], max(1, remaining * weights[i] // pool), spare)
            given[i] = given[i] + addition
            spare = spare - addition
    return np.array(given)


def normal_values(key, extent, width, limit, pieces=(), kind=jnp.bfloat16):
    values = width * jax.random.normal(key, extent, jnp.float32)
    if pieces:
        values = values * block_scale(key, extent, pieces, -0.22, 0.18)
    return jnp.clip(values, -limit, limit).astype(kind)


def setup_inputs(seed: int = 0) -> dict:
    arg_keys = jax.random.split(jax.random.key(seed), 16)
    tokens = normal_values(arg_keys[0], (MICRO, TOKENS_MB, D), 1.0, 6.0, ((1, 32),))
    cotangent = normal_values(arg_keys[1], (MICRO, TOKENS_MB, D), 1.0, 6.0, ((1, 32),))
    attn_gain = jnp.clip(1.0 + 0.18 * jax.random.normal(arg_keys[2], (D,), jnp.float32), 0.099609375, 1.8984375).astype(jnp.bfloat16)
    mlp_gain = jnp.clip(1.0 + 0.18 * jax.random.normal(arg_keys[3], (D,), jnp.float32), 0.099609375, 1.8984375).astype(jnp.bfloat16)
    w_query = normal_values(arg_keys[4], (D, HEADS * HEAD_DIM), 0.09, 1.25, ((0, 32),))
    w_key = normal_values(arg_keys[5], (D, KV_HEADS * HEAD_DIM), 0.09, 1.25, ((0, 32),))
    w_value = normal_values(arg_keys[6], (D, KV_HEADS * HEAD_DIM), D ** -0.5, 0.15625, ((0, 32),))
    w_out = normal_values(arg_keys[7], (HEADS * HEAD_DIM, D), 0.5, 6.0, ((0, 32),))
    w_router = normal_values(arg_keys[8], (D, EXPERTS), 0.013, 0.1875, ((0, 32),))
    w_gate = normal_values(arg_keys[9], (EXPERTS, D, FF), D ** -0.5, 0.15625, ((0, 4), (1, 8)))
    w_up = normal_values(arg_keys[10], (EXPERTS, D, FF), D ** -0.5, 0.15625, ((0, 4), (1, 8)))
    w_down = normal_values(arg_keys[11], (EXPERTS, FF, D), 0.5, 6.0, ((0, 4), (1, 8)))
    shuffle = jax.vmap(lambda own: jax.random.permutation(own, ROWS))(jax.random.split(arg_keys[12], MICRO * (N_DP * N_EXPERT))).reshape((MICRO, N_DP * N_EXPERT, ROWS)).astype(jnp.int32)
    routes_keys = jax.random.split(jax.random.fold_in(arg_keys[13], 1), MICRO * TOKENS_MB // ROWS)
    routes_turns = jax.random.permutation(jax.random.fold_in(arg_keys[13], 3), MICRO * TOKENS_MB // ROWS)
    routes = jax.vmap(lambda own, number: shared_out(jax.random.fold_in(arg_keys[13], 2), own, number, ROWS, EXPERTS, TOP, CAP, 1))(routes_keys, routes_turns).reshape((MICRO, TOKENS_MB, TOP))
    lengths = draw_lengths(jax.random.fold_in(arg_keys[15], 71), 0)
    return dict(tokens=tokens, cotangent=cotangent, attn_gain=attn_gain, mlp_gain=mlp_gain, w_query=w_query, w_key=w_key, w_value=w_value, w_out=w_out, w_router=w_router, w_gate=w_gate, w_up=w_up, w_down=w_down, shuffle=shuffle, routes=routes, lengths=lengths)


EPSILON = 1e-06
ROPE_BASE = 10000.0
RESIDUAL_SCALE = 0.22
SCORE_SCALE = 1.0 / 64.0

@jax.custom_vjp
def low(v):
    return lax.optimization_barrier(v.astype(jnp.bfloat16)).astype(jnp.float32)

@jax.custom_vjp
def low_back(v):
    return v

def low_keep(v):
    return (low(v), None)

def low_pass(kept, grad):
    return (grad,)

def back_keep(v):
    return (v, None)

def back_low(kept, grad):
    return (low(grad),)
low.defvjp(low_keep, low_pass)
low_back.defvjp(back_keep, back_low)

def matmul_high(left_side, right_side):
    return jnp.dot(left_side, right_side, precision=lax.Precision.HIGHEST, preferred_element_type=jnp.float32)

def rms_norm(values, gain_row):
    return values * lax.rsqrt(lax.optimization_barrier(jnp.mean(values * values, -1, keepdims=True)) + EPSILON) * gain_row

def rope_tables(positions):
    half_dim = HEAD_DIM // 2
    inverse = ROPE_BASE ** (-(jnp.arange(half_dim, dtype=jnp.float32) * 2.0) / HEAD_DIM)
    angles = positions.astype(jnp.float32)[:, None] * inverse[None, :]
    return (jnp.cos(angles), jnp.sin(angles))

def rotate(values, cosine_table, sine_table):
    half_dim = values.shape[-1] // 2
    first_part = values[..., :half_dim]
    second_part = values[..., half_dim:]
    cosine_part = cosine_table[:, None, :]
    sine_part = sine_table[:, None, :]
    return jnp.concatenate([first_part * cosine_part - second_part * sine_part, second_part * cosine_part + first_part * sine_part], -1)

def doc_layout(doc_lengths):
    doc_ends = jnp.cumsum(doc_lengths, -1).astype(jnp.int32)
    doc_starts = doc_ends - doc_lengths
    group_iota = jnp.arange(GROUP_TOK, dtype=jnp.int32)
    segment_ids = lax.optimization_barrier(jnp.sum((group_iota[None, :, None] >= doc_ends[:, None, :]).astype(jnp.int32), -1))
    member_of = segment_ids[:, :, None] == jnp.arange(DOCS, dtype=jnp.int32)[None, None, :]
    position_ids = group_iota[None, :] - lax.optimization_barrier(jnp.sum(jnp.where(member_of, doc_starts[:, None, :], 0), -1))
    return (segment_ids.reshape(-1).astype(jnp.int32), position_ids.reshape(-1).astype(jnp.int32))

def deal_source(order_table):
    order_grid = order_table.reshape(N_DP, N_EXPERT, N_DP, PEER_ROWS)
    row_base = (jnp.arange(N_DP, dtype=jnp.int32)[:, None] * N_EXPERT + jnp.arange(N_EXPERT, dtype=jnp.int32)[None, :]) * ROWS
    source = order_grid + row_base[:, :, None, None]
    return jnp.transpose(source, (2, 1, 0, 3)).reshape(-1).astype(jnp.int32)

def attend_group(group_parts):
    query_rot, key_rot, value_rows, segment_ids = group_parts
    head_share = HEADS // KV_HEADS
    grouped = query_rot.reshape(GROUP_TOK, KV_HEADS, head_share, HEAD_DIM)
    raw_scores = low_back(jnp.einsum('qgjd,kgd->gjqk', grouped, key_rot, precision=lax.Precision.HIGHEST))
    scores = raw_scores * SCORE_SCALE
    group_iota = jnp.arange(GROUP_TOK, dtype=jnp.int32)
    allowed = (segment_ids[:, None] == segment_ids[None, :]) & (group_iota[None, :] <= group_iota[:, None])
    scores = jnp.where(allowed[None, None], scores, -jnp.inf)
    highest = lax.optimization_barrier(jnp.max(scores, -1, keepdims=True))
    exponent = jnp.exp(scores - highest)
    probabilities = exponent / lax.optimization_barrier(jnp.sum(exponent, -1, keepdims=True))
    weights = low(probabilities)
    attended = jnp.einsum('gjqk,kgd->qgjd', weights, value_rows, precision=lax.Precision.HIGHEST)
    return attended.reshape(GROUP_TOK, HEADS * HEAD_DIM)

def experts_apply(dealt_rows, gate_weights, route_flat, gate_all, up_all, down_all):
    padded = jnp.concatenate([dealt_rows, jnp.zeros((1, D), jnp.float32)], 0)
    gate_pad = jnp.concatenate([gate_weights.reshape(-1), jnp.zeros((1,), jnp.float32)], 0)

    def expert_step(running, inputs):
        expert_id, gate_one, up_one, down_one = inputs
        picked = jnp.nonzero(route_flat == expert_id, size=SHARDS * CAP, fill_value=TOKENS_MB * TOP)[0].astype(jnp.int32)
        token_id = picked // TOP
        rows_in = low_back(padded[token_id])
        gate_pre = low_back(matmul_high(rows_in, gate_one))
        up_pre = low_back(matmul_high(rows_in, up_one))
        activated = low(jax.nn.silu(gate_pre) * up_pre)
        expert_out = low_back(low(matmul_high(activated, down_one)))
        running = running.at[token_id].add(expert_out * gate_pad[picked][:, None])
        return (running, None)
    running, unused = lax.scan(jax.checkpoint(expert_step), jnp.zeros((TOKENS_MB + 1, D), jnp.float32), (jnp.arange(EXPERTS, dtype=jnp.int32), gate_all, up_all, down_all))
    return running[:TOKENS_MB]

def layer_forward(inputs, params, source, inverse, segment_ids, position_ids, route_rows, route_flat):
    gain_attn, gain_mlp, query_w, key_w, value_w, out_w, router_w, gate_all, up_all, down_all = params
    normed_first = low(rms_norm(inputs, gain_attn))
    cosine_table, sine_table = rope_tables(position_ids)
    query_pre = low_back(matmul_high(normed_first, query_w)).reshape(TOKENS_MB, HEADS, HEAD_DIM)
    key_pre = low_back(matmul_high(normed_first, key_w)).reshape(TOKENS_MB, KV_HEADS, HEAD_DIM)
    value_rows = low_back(low(matmul_high(normed_first, value_w))).reshape(TOKENS_MB, KV_HEADS, HEAD_DIM)
    query_rot = low(rotate(query_pre, cosine_table, sine_table))
    key_rot = low(rotate(key_pre, cosine_table, sine_table))
    attended = lax.map(jax.checkpoint(attend_group), (query_rot.reshape(N_DP, GROUP_TOK, HEADS, HEAD_DIM), key_rot.reshape(N_DP, GROUP_TOK, KV_HEADS, HEAD_DIM), value_rows.reshape(N_DP, GROUP_TOK, KV_HEADS, HEAD_DIM), segment_ids.reshape(N_DP, GROUP_TOK)))
    merged = low_back(low(attended.reshape(TOKENS_MB, HEADS * HEAD_DIM)))
    attn_out = low_back(matmul_high(merged, out_w))
    hidden = inputs + RESIDUAL_SCALE * attn_out
    normed_second = low_back(low(rms_norm(hidden, gain_mlp)))
    dealt_rows = normed_second[source]
    logits = low_back(matmul_high(dealt_rows, router_w))
    picked = jnp.take_along_axis(logits, route_rows, 1)
    gate_weights = jax.nn.softmax(picked, -1)
    mixed_rows = low_back(low(experts_apply(dealt_rows, gate_weights, route_flat, gate_all, up_all, down_all)))
    return hidden + RESIDUAL_SCALE * mixed_rows[inverse]

def reference(tokens, cotangent, attn_gain, mlp_gain, w_query, w_key, w_value, w_out, w_router, w_gate, w_up, w_down, shuffle, routes, lengths):
    floats = tuple((weight_array.astype(jnp.float32) for weight_array in (attn_gain, mlp_gain, w_query, w_key, w_value, w_out, w_router, w_gate, w_up, w_down)))
    outputs = []
    grad_inputs = []
    totals = None
    for step_index in range(MICRO):
        source = deal_source(shuffle[step_index])
        inverse = jnp.zeros((TOKENS_MB,), jnp.int32).at[source].set(jnp.arange(TOKENS_MB, dtype=jnp.int32))
        segment_ids, position_ids = doc_layout(lengths[step_index])
        route_rows = routes[step_index]
        route_flat = route_rows.reshape(-1)

        def forward(inputs, params):
            return layer_forward(inputs, params, source, inverse, segment_ids, position_ids, route_rows, route_flat)
        result, pullback = jax.vjp(forward, tokens[step_index].astype(jnp.float32), floats)
        grad_x, grad_params = pullback(cotangent[step_index].astype(jnp.float32))
        outputs.append(result.astype(jnp.bfloat16))
        grad_inputs.append(grad_x)
        totals = grad_params if totals is None else jax.tree.map(jnp.add, totals, grad_params)
    return (jnp.stack(outputs), jnp.stack(grad_inputs), totals[0], totals[1], totals[2], totals[3], totals[4], totals[5], totals[6], totals[7], totals[8], totals[9])
```

```python
import functools

import jax
import jax.numpy as jnp
from jax import lax
from jax.experimental import pallas as pl
from jax.experimental.pallas import tpu as pltpu
from jax.sharding import PartitionSpec as P

HEADS = 24
KV_HEADS = 8
HEAD_DIM = 64

EPSILON = 1e-06
ROPE_BASE = 10000.0
RESIDUAL_SCALE = 0.22
SCORE_SCALE = 1.0 / 64.0
NEGATIVE = -1e30
LANES = 128

BF16 = jnp.bfloat16
F32 = jnp.float32
ALL = ("dp", "expert")


def dot(a, b, dims=((1,), (0,))):
    return lax.dot_general(a, b, (dims, ((), ())), preferred_element_type=F32)


class Rings:
    def __init__(self, dp_count, expert_count):
        y_count = 1
        while dp_count % (2 * y_count) == 0 and 8 * y_count * y_count <= dp_count:
            y_count *= 2
        self.y, self.z = y_count, dp_count // y_count
        self.core = 2 if expert_count % 2 == 0 else 1
        self.x = expert_count // self.core
        zs, ys, xs, cs = range(self.z), range(self.y), range(self.x), range(self.core)
        self.z_groups = [[z * self.y + y for z in zs] for y in ys]
        self.table = {
            "z": ("dp", self.z, [(z * self.y + y, (z + 1) % self.z * self.y + y) for z in zs for y in ys]),
            "y": ("dp", self.y, [(z * self.y + y, z * self.y + (y + 1) % self.y) for z in zs for y in ys]),
            "x": (
                "expert",
                self.x,
                [(x * self.core + c, (x + 1) % self.x * self.core + c) for x in xs for c in cs],
            ),
            "c": (
                "expert",
                self.core,
                [(x * self.core + c, x * self.core + (c + 1) % self.core) for x in xs for c in cs],
            ),
        }
        d, e = lax.axis_index("dp"), lax.axis_index("expert")
        self.at = {"z": d // self.y, "y": d % self.y, "x": e // self.core, "c": e % self.core}

    def count(self, ring):
        return self.table[ring][1]

    def step(self, value, ring):
        axis, _, pairs = self.table[ring]
        return lax.ppermute(value, axis, pairs)

    def origin(self, ring, slot):
        return lax.rem(self.at[ring] + (self.count(ring) - slot), self.count(ring))

    def gather(self, value, ring):
        slots = [value]
        for _ in range(self.count(ring) - 1):
            slots.append(self.step(slots[-1], ring))
        return slots

    def reduce(self, parts, ring, wire=BF16):
        running = None
        for slot in range(1, self.count(ring)):
            term = parts[slot]
            if running is not None:
                term = term.astype(F32) + running.astype(F32)
            running = self.step(term.astype(wire), ring)
        own = parts[0].astype(F32)
        return own if running is None else own + running.astype(F32)

    def gather_two(self, value, first, second):
        columns = [self.gather(slot, second) for slot in self.gather(value, first)]
        return [[column[s] for column in columns] for s in range(self.count(second))]

    def reduce_two(self, parts, first, second, wire=BF16):
        partial = [
            self.reduce([parts[s][t] for s in range(self.count(second))], second, wire)
            for t in range(self.count(first))
        ]
        return self.reduce(partial, first, wire)


def in_order(slots, position_of, count):
    stacked = jnp.stack(slots)
    return [
        lax.dynamic_index_in_dim(stacked, lax.rem(position_of + (count - i), count), 0, False)
        for i in range(count)
    ]


def rotate_pairs(values, cosine, sine, direction):
    lane = lax.broadcasted_iota(jnp.int32, (values.shape[0], LANES), 1)
    low = (lane & (HEAD_DIM - 1)) < HEAD_DIM // 2
    pieces = []
    for start in range(0, values.shape[1], LANES):
        piece = values[:, start : start + LANES]
        partner = jnp.where(
            low,
            pltpu.roll(piece, LANES - HEAD_DIM // 2, 1),
            pltpu.roll(piece, HEAD_DIM // 2, 1),
        )
        turned = partner * sine
        pieces.append(piece * cosine + turned if direction > 0 else piece * cosine - turned)
    return jnp.concatenate(pieces, 1)


def attention_forward_kernel(
    heads, kv_heads, n1_ref, w_ref, wo_ref, cos_ref, sin_ref, bias_ref, out_ref, qkv_ref, merged_ref, lse_ref
):
    share = heads // kv_heads
    rotated = (heads + kv_heads) * HEAD_DIM
    pre = dot(n1_ref[0], w_ref[...])
    turned = rotate_pairs(pre[:, :rotated], cos_ref[0], sin_ref[0], 1)
    qkv_ref[0, :, :rotated] = turned.astype(BF16)
    qkv_ref[0, :, rotated:] = pre[:, rotated:].astype(BF16)
    bias = bias_ref[0]
    lane = lax.broadcasted_iota(jnp.int32, (pre.shape[0], LANES), 1)
    sums = jnp.zeros((pre.shape[0], LANES), F32)
    for head in range(heads):
        group = head // share
        key_at = (heads + group) * HEAD_DIM
        value_at = rotated + group * HEAD_DIM
        query = qkv_ref[0, :, head * HEAD_DIM : (head + 1) * HEAD_DIM]
        key = qkv_ref[0, :, key_at : key_at + HEAD_DIM]
        value = qkv_ref[0, :, value_at : value_at + HEAD_DIM]
        scores = dot(query, key, ((1,), (1,))) * SCORE_SCALE + bias
        highest = jnp.max(scores, -1, keepdims=True)
        exponent = jnp.exp(scores - highest)
        total = jnp.sum(exponent, -1, keepdims=True)
        weights = (exponent / total).astype(BF16)
        merged_ref[0, :, head * HEAD_DIM : (head + 1) * HEAD_DIM] = dot(weights, value).astype(BF16)
        sums = jnp.where(lane == head, highest + jnp.log(total), sums)
    lse_ref[0] = sums
    out_ref[0] = dot(merged_ref[0], wo_ref[...]).astype(BF16)


def attention_backward_kernel(
    heads,
    kv_heads,
    ga_ref,
    w_ref,
    wo_ref,
    cos_ref,
    sin_ref,
    bias_ref,
    qkv_ref,
    lse_ref,
    out_ref,
    dqkv_ref,
    turned_ref,
):
    share = heads // kv_heads
    rotated = (heads + kv_heads) * HEAD_DIM
    grad_merged = dot(ga_ref[0], wo_ref[...], ((1,), (1,))).astype(BF16)
    bias = bias_ref[0]
    for group in range(kv_heads):
        key_at = (heads + group) * HEAD_DIM
        value_at = rotated + group * HEAD_DIM
        key = qkv_ref[0, :, key_at : key_at + HEAD_DIM]
        value = qkv_ref[0, :, value_at : value_at + HEAD_DIM]
        grad_key, grad_value = None, None
        for head in range(group * share, (group + 1) * share):
            query = qkv_ref[0, :, head * HEAD_DIM : (head + 1) * HEAD_DIM]
            grad_rows = grad_merged[:, head * HEAD_DIM : (head + 1) * HEAD_DIM]
            scores = dot(query, key, ((1,), (1,))) * SCORE_SCALE + bias
            chance = jnp.exp(scores - lse_ref[0, :, head : head + 1])
            weights = chance.astype(BF16)
            grad_chance = dot(grad_rows, value, ((1,), (1,)))
            delta = jnp.sum(chance * grad_chance, -1, keepdims=True)
            grad_raw = (chance * (grad_chance - delta) * SCORE_SCALE).astype(BF16)
            turned_ref[:, head * HEAD_DIM : (head + 1) * HEAD_DIM] = dot(grad_raw, key)
            key_part = dot(grad_raw, query, ((0,), (0,)))
            value_part = dot(weights, grad_rows, ((0,), (0,)))
            grad_key = key_part if grad_key is None else grad_key + key_part
            grad_value = value_part if grad_value is None else grad_value + value_part
        turned_ref[:, key_at : key_at + HEAD_DIM] = grad_key
        dqkv_ref[0, :, value_at : value_at + HEAD_DIM] = grad_value.astype(BF16)
    back = rotate_pairs(turned_ref[...], cos_ref[0], sin_ref[0], -1)
    dqkv_ref[0, :, :rotated] = back.astype(BF16)
    out_ref[0] = dot(dqkv_ref[0], w_ref[...], ((1,), (1,))).astype(BF16)


def per_micro(shape):
    return pl.BlockSpec((1,) + tuple(shape[1:]), lambda m: (m,) + (0,) * (len(shape) - 1))


def whole(shape):
    return pl.BlockSpec(tuple(shape), lambda m: (0,) * len(shape))


def attention_forward(n1, w, wo, cosine, sine, bias, heads, kv_heads):
    micros, rows, width = n1.shape
    outs = [
        jax.ShapeDtypeStruct((micros, rows, width), BF16),
        jax.ShapeDtypeStruct((micros, rows, w.shape[1]), BF16),
        jax.ShapeDtypeStruct((micros, rows, heads * HEAD_DIM), BF16),
        jax.ShapeDtypeStruct((micros, rows, LANES), F32),
    ]
    return pl.pallas_call(
        functools.partial(attention_forward_kernel, heads, kv_heads),
        grid=(micros,),
        in_specs=[
            per_micro(n1.shape),
            whole(w.shape),
            whole(wo.shape),
            per_micro(cosine.shape),
            per_micro(sine.shape),
            per_micro(bias.shape),
        ],
        out_specs=[per_micro(o.shape) for o in outs],
        out_shape=outs,
        name="attention_forward",
    )(n1, w, wo, cosine, sine, bias)


def attention_backward(ga, w, wo, cosine, sine, bias, qkv, lse, heads, kv_heads):
    micros, rows, width = ga.shape
    outs = [
        jax.ShapeDtypeStruct((micros, rows, width), BF16),
        jax.ShapeDtypeStruct((micros, rows, w.shape[1]), BF16),
    ]
    return pl.pallas_call(
        functools.partial(attention_backward_kernel, heads, kv_heads),
        grid=(micros,),
        in_specs=[
            per_micro(ga.shape),
            whole(w.shape),
            whole(wo.shape),
            per_micro(cosine.shape),
            per_micro(sine.shape),
            per_micro(bias.shape),
            per_micro(qkv.shape),
            per_micro(lse.shape),
        ],
        out_specs=[per_micro(o.shape) for o in outs],
        out_shape=outs,
        scratch_shapes=[pltpu.VMEM((rows, (heads + kv_heads) * HEAD_DIM), F32)],
        name="attention_backward",
    )(ga, w, wo, cosine, sine, bias, qkv, lse)


def experts_kernel(
    experts_all,
    ids_ref,
    x_ref,
    gm_ref,
    mask_ref,
    wr_ref,
    wgu_ref,
    wd_ref,
    mixed_ref,
    dx_ref,
    gate_ref,
    gg_ref,
    act_ref,
    dgu_ref,
    mixed_acc,
    dx_acc,
):
    step = pl.program_id(1)
    rows = x_ref.shape[0]
    per_step, hidden = wd_ref.shape[0], wd_ref.shape[1]
    lane = lax.broadcasted_iota(jnp.int32, (rows, LANES), 1)

    @pl.when(step == 0)
    def _():
        named = mask_ref[...].astype(F32) > 0.5
        logits = jnp.where(named, dot(x_ref[...], wr_ref[...]), NEGATIVE)
        highest = jnp.max(logits, -1, keepdims=True)
        exponent = jnp.where(named, jnp.exp(logits - highest), 0.0)
        gate_ref[...] = exponent / jnp.sum(exponent, -1, keepdims=True)
        gg_ref[...] = jnp.zeros_like(gg_ref)
        mixed_acc[...] = jnp.zeros_like(mixed_acc)
        dx_acc[...] = jnp.zeros_like(dx_acc)

    x = x_ref[...]
    down = wd_ref[...].reshape(per_step * hidden, wd_ref.shape[2])
    grad_act = dot(gm_ref[...], down, ((1,), (1,)))
    gates = gate_ref[...]
    for i in range(per_step):
        mine = lane == ids_ref[step * per_step + i]
        gate = jnp.sum(jnp.where(mine, gates, 0.0), -1, keepdims=True)
        pre = dot(x, wgu_ref[i])
        gate_pre, up_pre = pre[:, :hidden], pre[:, hidden:]
        sig = jax.nn.sigmoid(gate_pre)
        silu = gate_pre * sig
        activated = (silu * up_pre).astype(BF16).astype(F32)
        grad_one = grad_act[:, i * hidden : (i + 1) * hidden]
        picked = jnp.sum(activated * grad_one, -1, keepdims=True)
        gg_ref[...] += jnp.where(mine, picked, 0.0)
        act_ref[:, i * hidden : (i + 1) * hidden] = (activated * gate).astype(BF16)
        grad_one = grad_one * gate
        grad_gate_pre = (grad_one * up_pre * sig * (1.0 + gate_pre * (1.0 - sig))).astype(BF16)
        grad_up_pre = (grad_one * silu).astype(BF16)
        base = 2 * hidden * i
        dgu_ref[:, base : base + hidden] = grad_gate_pre
        dgu_ref[:, base + hidden : base + 2 * hidden] = grad_up_pre
        dx_acc[...] += dot(dgu_ref[:, base : base + 2 * hidden], wgu_ref[i], ((1,), (1,)))
    mixed_acc[...] += dot(act_ref[...], down)

    @pl.when(step == pl.num_programs(1) - 1)
    def _():
        mixed_ref[...] = mixed_acc[...].astype(BF16)
        dx_ref[...] = dx_acc[...].astype(BF16)


def run_experts(ids, x, gm_mask, wr, wgu, wd, experts_all):
    rows, width = x.shape
    local, hidden = wd.shape[0], wd.shape[1]
    per_step = 2 if local % 2 == 0 else 1
    block = min(rows, 1024)
    outs = [
        jax.ShapeDtypeStruct((rows, width), BF16),
        jax.ShapeDtypeStruct((rows, width), BF16),
        jax.ShapeDtypeStruct((rows, LANES), F32),
        jax.ShapeDtypeStruct((rows, LANES), F32),
        jax.ShapeDtypeStruct((rows, local * hidden), BF16),
        jax.ShapeDtypeStruct((rows, 2 * local * hidden), BF16),
    ]
    once = pl.Buffered(1)
    return pl.pallas_call(
        functools.partial(experts_kernel, experts_all),
        grid_spec=pltpu.PrefetchScalarGridSpec(
            num_scalar_prefetch=1,
            grid=(rows // block, local // per_step),
            in_specs=[
                pl.BlockSpec((block, width), lambda r, s, ids: (r, 0)),
                pl.BlockSpec((block, width), lambda r, s, ids: (r, 0)),
                pl.BlockSpec((block, LANES), lambda r, s, ids: (r, width // LANES)),
                pl.BlockSpec((width, LANES), lambda r, s, ids: (0, 0), pipeline_mode=once),
                pl.BlockSpec((per_step, width, 2 * hidden), lambda r, s, ids: (s, 0, 0)),
                pl.BlockSpec((per_step, hidden, width), lambda r, s, ids: (s, 0, 0)),
            ],
            out_specs=[
                pl.BlockSpec((block, width), lambda r, s, ids: (r, 0)),
                pl.BlockSpec((block, width), lambda r, s, ids: (r, 0)),
                pl.BlockSpec((block, LANES), lambda r, s, ids: (r, 0)),
                pl.BlockSpec((block, LANES), lambda r, s, ids: (r, 0)),
                pl.BlockSpec((block, per_step * hidden), lambda r, s, ids: (r, s)),
                pl.BlockSpec((block, 2 * per_step * hidden), lambda r, s, ids: (r, s)),
            ],
            scratch_shapes=[pltpu.VMEM((block, width), F32), pltpu.VMEM((block, width), F32)],
        ),
        out_shape=outs,
        compiler_params=pltpu.CompilerParams(vmem_limit_bytes=60 << 20),
        name="experts",
    )(ids, x, gm_mask, gm_mask, wr, wgu, wd)


def per_device(
    tokens,
    cotangent,
    attn_gain,
    mlp_gain,
    w_query,
    w_key,
    w_value,
    w_out,
    w_router,
    w_gate,
    w_up,
    w_down,
    shuffle,
    routes,
    lengths,
):
    micros, rows, width = tokens.shape
    dp_count, members = lax.axis_size("dp"), lax.axis_size("expert")
    devices = dp_count * members
    rings = Rings(dp_count, members)
    zn, yn, xn, cn = rings.z, rings.y, rings.x, rings.core
    group_rows = rows * members
    experts_all = w_router.shape[1]
    own_experts, model_part, hidden_all = w_gate.shape
    hidden_part = hidden_all // zn
    heads, kv_heads = HEADS // members, KV_HEADS // members
    weight_rows = w_query.shape[0]
    home_rows = micros * rows

    small = jnp.concatenate([w_router.T, attn_gain[None], mlp_gain[None]], 0)
    small = lax.all_to_all(jnp.broadcast_to(small[None], (devices,) + small.shape), ALL, 0, 0)
    small = small.transpose(1, 0, 2).reshape(experts_all + 2, width)
    gain_first = small[experts_all].astype(F32)
    gain_second = small[experts_all + 1].astype(F32)
    router_rows = jnp.pad(small[:experts_all], ((0, LANES - experts_all), (0, 0)))
    router_cols = router_rows.T

    def by_member(w):
        return w.reshape(weight_rows, members, w.shape[1] // members)

    mine = jnp.concatenate([by_member(w_query), by_member(w_key), by_member(w_value)], 2)
    mine = lax.all_to_all(mine.transpose(1, 0, 2), "expert", 0, 0)
    qkv_cols = mine.shape[2]
    mine = mine.reshape(members * weight_rows, qkv_cols)
    to_heads = [(s, (s % dp_count) * members + s // dp_count) for s in range(devices)]
    to_home = [(t, s) for s, t in to_heads]
    out_mine = lax.ppermute(w_out, ALL, to_heads)
    merged_cols = width // members
    pack = out_mine.reshape(weight_rows, members, merged_cols).transpose(1, 0, 2)
    pack = jnp.concatenate([mine, pack.reshape(members * weight_rows, merged_cols)], 1)
    packs = rings.gather_two(pack, "z", "y")
    packs = [in_order(column, rings.at["z"], zn) for column in packs]
    packs = [in_order([packs[s][z] for s in range(yn)], rings.at["y"], yn) for z in range(zn)]
    packs = jnp.stack([packs[z][y] for z in range(zn) for y in range(yn)])
    w_qkv = packs[:, :, :qkv_cols].reshape(width, qkv_cols)
    w_merge = packs[:, :, qkv_cols:].reshape(dp_count, members, weight_rows, merged_cols)
    w_merge = w_merge.transpose(0, 2, 1, 3).reshape(dp_count * weight_rows, width)

    dealt = lax.all_to_all(
        routes.reshape(micros, dp_count, rows // dp_count, routes.shape[2]), "dp", 1, 1
    ).reshape(micros, rows, routes.shape[2])
    lane_ids = jnp.arange(LANES, dtype=jnp.int32)
    hot = jnp.sum((dealt[:, :, :, None] == lane_ids).astype(F32), 2).astype(BF16)
    place = (shuffle[:, 0, :, None] == jnp.arange(rows, dtype=jnp.int32)).astype(BF16)
    named = jnp.einsum("mir,mix->mrx", place, hot, preferred_element_type=F32).astype(BF16)

    grad_result = cotangent.astype(F32)
    grad_moe = (RESIDUAL_SCALE * grad_result).astype(BF16)
    beside = jnp.concatenate([grad_moe, named], 2).reshape(home_rows, width + LANES)
    beside = rings.gather_two(beside, "z", "x")
    gm_mask = jnp.concatenate([slot for column in beside for slot in column], 0)

    def to_z(w):
        w = w.reshape(own_experts, model_part, zn, hidden_part)
        return w.transpose(2, 0, 1, 3)

    gate_up = jnp.concatenate([to_z(w_gate), to_z(w_up)], 3)
    gate_up = lax.all_to_all(gate_up, "dp", 0, 0, axis_index_groups=rings.z_groups)
    gate_up = in_order(rings.gather(gate_up, "y"), rings.at["y"], yn)
    gate_up = jnp.stack(gate_up, 1).transpose(2, 0, 1, 3, 4)
    gate_up = gate_up.reshape(own_experts, width, 2 * hidden_part)
    down = in_order(rings.gather(w_down, "y"), rings.at["y"], yn)
    down = jnp.concatenate(down, 1)
    w_gu = jnp.concatenate(rings.gather(gate_up, "c"), 0)
    w_dn = jnp.concatenate(rings.gather(down, "c"), 0)
    ids = jnp.concatenate(
        [
            (rings.at["x"] * cn + rings.origin("c", s)) * own_experts
            + jnp.arange(own_experts, dtype=jnp.int32)
            for s in range(cn)
        ]
    )

    group_iota = jnp.arange(group_rows, dtype=jnp.int32)
    row_at = jnp.concatenate(
        [
            (rings.origin("x", s) * cn + rings.origin("c", t)) * rows
            + jnp.arange(rows, dtype=jnp.int32)
            for s in range(xn)
            for t in range(cn)
        ]
    )
    half = HEAD_DIM // 2
    lane = jnp.arange(LANES, dtype=jnp.int32)
    inverse = ROPE_BASE ** (-((lane % half).astype(F32) * 2.0) / HEAD_DIM)
    sign = jnp.where(lane % HEAD_DIM < half, -1.0, 1.0)
    cosine, sine, bias = [], [], []
    for m in range(micros):
        doc_lengths = lengths[m, 0]
        doc_ends = jnp.cumsum(doc_lengths)
        doc_starts = doc_ends - doc_lengths
        segment = jnp.sum((row_at[:, None] >= doc_ends[None, :]).astype(jnp.int32), 1)
        member_of = segment[:, None] == jnp.arange(doc_lengths.shape[0], dtype=jnp.int32)[None, :]
        position = row_at - jnp.sum(jnp.where(member_of, doc_starts[None, :], 0), 1)
        angles = position.astype(F32)[:, None] * inverse[None, :]
        cosine.append(jnp.cos(angles))
        sine.append(jnp.sin(angles) * sign)
        allowed = (segment[:, None] == segment[None, :]) & (row_at[None, :] <= row_at[:, None])
        bias.append(jnp.where(allowed, 0.0, NEGATIVE))
    cosine, sine, bias = jnp.stack(cosine), jnp.stack(sine), jnp.stack(bias)

    def over_members(value):
        both = jnp.concatenate(rings.gather(value, "c"), 1)
        return jnp.concatenate(rings.gather(both, "x"), 1)

    def sum_members(value):
        parts = value.reshape(micros, xn, cn, rows, width)
        parts = rings.reduce([parts[:, :, t] for t in range(cn)], "c")
        return rings.reduce([parts[:, s] for s in range(xn)], "x")

    inputs = tokens.astype(F32)
    inv_first = lax.rsqrt(jnp.mean(inputs * inputs, -1, keepdims=True) + EPSILON)
    unit_first = inputs * inv_first
    normed_first = over_members((unit_first * gain_first).astype(BF16))
    attn_part, qkv, merged, lse = attention_forward(
        normed_first, w_qkv, w_merge, cosine, sine, bias, heads, kv_heads
    )
    hidden = inputs + RESIDUAL_SCALE * sum_members(attn_part)
    inv_second = lax.rsqrt(jnp.mean(hidden * hidden, -1, keepdims=True) + EPSILON)
    unit_second = hidden * inv_second
    normed_second = (unit_second * gain_second).astype(BF16).reshape(home_rows, width)

    group_x = rings.gather_two(normed_second, "z", "x")
    group_x = jnp.concatenate([slot for column in group_x for slot in column], 0)
    mixed, dx, gates, grad_gates, act, dgu = run_experts(
        ids, group_x, gm_mask, router_cols, w_gu, w_dn, experts_all
    )

    def to_owner(value, wire):
        parts = value.reshape(xn, zn, home_rows, value.shape[1])
        return rings.reduce_two([[parts[s, t] for t in range(zn)] for s in range(xn)], "z", "x", wire)

    grad_gates = to_owner(grad_gates, F32)
    grad_dealt = to_owner(dx, BF16)
    own_gates = gates[:home_rows]
    grad_picked = own_gates * (grad_gates - jnp.sum(own_gates * grad_gates, -1, keepdims=True))
    grad_logits = grad_picked.astype(BF16)
    router_grad = dot(grad_logits, normed_second, ((0,), (0,)))[:experts_all]
    grad_dealt = (grad_dealt + dot(grad_logits, router_rows)).astype(BF16)
    grad_normed_second = grad_dealt.astype(F32).reshape(micros, rows, width)
    scaled_second = grad_normed_second * gain_second
    grad_hidden = grad_result + inv_second * (
        scaled_second - unit_second * jnp.mean(scaled_second * unit_second, -1, keepdims=True)
    )
    mlp_gain_grad = jnp.sum(grad_normed_second * unit_second, (0, 1))
    grad_attn = over_members((RESIDUAL_SCALE * grad_hidden).astype(BF16))

    moe_rows = to_owner(mixed, BF16).astype(BF16).reshape(micros, rows, width)
    output = (hidden + RESIDUAL_SCALE * moe_rows.astype(F32)).astype(BF16)

    first_part, dqkv = attention_backward(
        grad_attn, w_qkv, w_merge, cosine, sine, bias, qkv, lse, heads, kv_heads
    )
    grad_normed_first = sum_members(first_part)
    scaled_first = grad_normed_first * gain_first
    grad_tokens = grad_hidden + inv_first * (
        scaled_first - unit_first * jnp.mean(scaled_first * unit_first, -1, keepdims=True)
    )
    attn_gain_grad = jnp.sum(grad_normed_first * unit_first, (0, 1))

    small = jnp.concatenate([router_grad, mlp_gain_grad[None]], 0)
    small = small.reshape(experts_all + 1, devices, weight_rows).transpose(1, 0, 2)
    small = jnp.sum(lax.all_to_all(small, ALL, 0, 0), 0)
    grad_w_router, grad_mlp_gain = small[:experts_all].T, small[experts_all]
    grad_attn_gain = jnp.sum(
        lax.all_to_all(attn_gain_grad.reshape(devices, 1, weight_rows), ALL, 0, 0), (0, 1)
    )

    model_parts = zn * yn
    grad_gu = dot(group_x, dgu, ((0,), (0,))).astype(BF16)
    grad_gu = grad_gu.reshape(width, cn, own_experts * 2 * hidden_part)
    grad_gu = rings.reduce([grad_gu[:, s] for s in range(cn)], "c").astype(BF16)
    grad_gu = grad_gu.reshape(zn, yn, model_part, own_experts * 2 * hidden_part)
    grad_gu = rings.reduce(
        [lax.dynamic_index_in_dim(grad_gu, rings.origin("y", s), 1, False) for s in range(yn)], "y"
    ).astype(BF16)
    grad_gu = lax.all_to_all(grad_gu, "dp", 0, 0, axis_index_groups=rings.z_groups)
    grad_gu = grad_gu.reshape(zn, model_part, own_experts, 2, hidden_part).astype(F32)
    grad_gu = grad_gu.transpose(3, 2, 1, 0, 4).reshape(2, own_experts, model_part, hidden_all)
    grad_dn = dot(act, gm_mask[:, :width], ((0,), (0,))).astype(BF16)
    grad_dn = grad_dn.reshape(cn, own_experts, hidden_part, width)
    grad_dn = rings.reduce([grad_dn[s] for s in range(cn)], "c").astype(BF16)
    grad_dn = grad_dn.reshape(own_experts, yn, hidden_part // yn, width)
    grad_dn = rings.reduce(
        [lax.dynamic_index_in_dim(grad_dn, rings.origin("y", s), 1, False) for s in range(yn)], "y"
    )

    flat = micros * group_rows
    grad_qkv = dot(
        normed_first.reshape(flat, width), dqkv.reshape(flat, qkv_cols), ((0,), (0,))
    ).astype(BF16)
    grad_out = dot(
        merged.reshape(flat, heads * HEAD_DIM), grad_attn.reshape(flat, width), ((0,), (0,))
    ).astype(BF16)
    grad_out = grad_out.reshape(dp_count, weight_rows, members, merged_cols).transpose(0, 2, 1, 3)
    both = jnp.concatenate(
        [
            grad_qkv.reshape(dp_count, members * weight_rows, qkv_cols),
            grad_out.reshape(dp_count, members * weight_rows, merged_cols),
        ],
        2,
    )
    parts = [
        [
            lax.dynamic_index_in_dim(both, rings.origin("z", t) * yn + rings.origin("y", s), 0, False)
            for t in range(zn)
        ]
        for s in range(yn)
    ]
    both = rings.reduce_two(parts, "z", "y")
    grad_out = both[:, qkv_cols:].reshape(members, weight_rows, merged_cols).transpose(1, 0, 2)
    grad_out = lax.ppermute(grad_out.reshape(weight_rows, width), ALL, to_home)
    home = lax.all_to_all(both[:, :qkv_cols].reshape(members, weight_rows, qkv_cols), "expert", 0, 0)
    home = home.transpose(1, 0, 2)
    query_cols, key_cols = heads * HEAD_DIM, kv_heads * HEAD_DIM
    grad_query = home[:, :, :query_cols].reshape(weight_rows, -1)
    grad_key = home[:, :, query_cols : query_cols + key_cols].reshape(weight_rows, -1)
    grad_value = home[:, :, query_cols + key_cols :].reshape(weight_rows, -1)

    return (
        output,
        grad_tokens,
        grad_attn_gain,
        grad_mlp_gain,
        grad_query,
        grad_key,
        grad_value,
        grad_out,
        grad_w_router,
        grad_gu[0],
        grad_gu[1],
        grad_dn,
    )


def solution(mesh):
    rows = P(None, ALL, None)
    placed = (rows, rows, P(ALL), P(ALL)) + (P(ALL, None),) * 5
    placed += (P("expert", "dp", None),) * 3 + (rows, rows, P(None, "dp", None))
    results = (rows, rows, P(ALL), P(ALL)) + (P(ALL, None),) * 5
    results += (P("expert", "dp", None),) * 3
    return jax.shard_map(per_device, mesh=mesh, in_specs=placed, out_specs=results, check_vma=False)
```

```python
import functools

import jax
import jax.numpy as jnp
from jax import lax
from jax.experimental import pallas as pl
from jax.experimental.pallas import tpu as pltpu
from jax.sharding import PartitionSpec as P

HEADS = 24
KV_HEADS = 8
HEAD_DIM = 64

EPSILON = 1e-06
ROPE_BASE = 10000.0
RESIDUAL_SCALE = 0.22
SCORE_SCALE = 1.0 / 64.0
NEGATIVE = -1e30
LANES = 128

BF16 = jnp.bfloat16
F32 = jnp.float32
ALL = ("dp", "expert")


def dot(a, b, dims=((1,), (0,))):
    return lax.dot_general(a, b, (dims, ((), ())), preferred_element_type=F32)


class Rings:
    def __init__(self, dp_count, expert_count):
        y_count = 1
        while dp_count % (2 * y_count) == 0 and 8 * y_count * y_count <= dp_count:
            y_count *= 2
        self.y, self.z = y_count, dp_count // y_count
        self.core = 2 if expert_count % 2 == 0 else 1
        self.x = expert_count // self.core
        zs, ys, xs, cs = range(self.z), range(self.y), range(self.x), range(self.core)
        self.z_groups = [[z * self.y + y for z in zs] for y in ys]
        self.token_groups = [
            [(z * self.y + y) * expert_count + x * self.core + c for z in zs for x in xs]
            for y in ys
            for c in cs
        ]
        self.table = {
            "z": ("dp", self.z, [(z * self.y + y, (z + 1) % self.z * self.y + y) for z in zs for y in ys]),
            "y": ("dp", self.y, [(z * self.y + y, z * self.y + (y + 1) % self.y) for z in zs for y in ys]),
            "x": (
                "expert",
                self.x,
                [(x * self.core + c, (x + 1) % self.x * self.core + c) for x in xs for c in cs],
            ),
            "c": (
                "expert",
                self.core,
                [(x * self.core + c, x * self.core + (c + 1) % self.core) for x in xs for c in cs],
            ),
        }
        d, e = lax.axis_index("dp"), lax.axis_index("expert")
        self.at = {"z": d // self.y, "y": d % self.y, "x": e // self.core, "c": e % self.core}

    def count(self, ring):
        return self.table[ring][1]

    def step(self, value, ring):
        axis, _, pairs = self.table[ring]
        return lax.ppermute(value, axis, pairs)

    def origin(self, ring, slot):
        return lax.rem(self.at[ring] + (self.count(ring) - slot), self.count(ring))

    def gather(self, value, ring, meet=None):
        slots = [value]
        for s in range(1, self.count(ring)):
            arrived = self.step(slots[-1], ring)
            slots.append(arrived if meet is None else meet(s, arrived))
        return slots

    def reduce(self, parts, ring, wire=BF16, meet=None):
        running = None
        for slot in range(1, self.count(ring)):
            term = parts[slot]
            if running is not None:
                term = term.astype(F32) + running.astype(F32)
            running = self.step(term.astype(wire), ring)
            if meet is not None:
                running = meet(slot, running)
        own = parts[0].astype(F32)
        return own if running is None else own + running.astype(F32)

    def gather_two(self, value, first, second, meet=None):
        columns, slots = [], [value]
        for t in range(1, self.count(first)):
            arrived = self.step(slots[-1], first)
            column = self.gather(slots[-1], second)
            arrived, *rest = tie(arrived, *column[1:])
            columns.append([column[0]] + rest)
            slots.append(arrived if meet is None else meet(t, arrived))
        columns.append(self.gather(slots[-1], second))
        return [[column[s] for column in columns] for s in range(self.count(second))]

    def reduce_two(self, parts, first, second, wire=BF16, meet=None):
        count = self.count(first)
        arrived = {}
        for t in list(range(1, count)) + [0]:
            running = None
            for slot in range(1, self.count(second)):
                term = parts[slot][t]
                if running is not None:
                    term = term.astype(F32) + running.astype(F32)
                running = self.step(term.astype(wire), second)
            if running is not None and meet is not None:
                running = meet(second, t, running)
            arrived[t] = running

        def partial(t):
            own = parts[0][t].astype(F32)
            return own if arrived[t] is None else own + arrived[t].astype(F32)

        running = None
        for t in range(1, count):
            term = partial(t)
            if running is not None:
                term = term + running.astype(F32)
            running = self.step(term.astype(wire), first)
            ahead = (t + 2) % count
            if arrived[ahead] is not None and 0 < t < count - 1:
                running, arrived[ahead] = tie(running, arrived[ahead])
            if meet is not None:
                running = meet(first, t, running)
        own = partial(0)
        return own if running is None else own + running.astype(F32)


def tie(*values):
    return lax.optimization_barrier(values)


def in_order(slots, position_of, count):
    stacked = jnp.stack(slots)
    return [
        lax.dynamic_index_in_dim(stacked, lax.rem(position_of + (count - i), count), 0, False)
        for i in range(count)
    ]


def fetch(copies, semaphores):
    started = [pltpu.make_async_copy(a, b, semaphores.at[i]) for i, (a, b) in enumerate(copies)]
    for copy in started:
        copy.start()
    for copy in started:
        copy.wait()


def anywhere():
    return pl.BlockSpec(memory_space=pl.ANY)


def on_chip():
    return pl.BlockSpec(memory_space=pltpu.VMEM)


def rotate_pairs(values, cosine, sine, direction):
    lane = lax.broadcasted_iota(jnp.int32, (values.shape[0], LANES), 1)
    low = (lane & (HEAD_DIM - 1)) < HEAD_DIM // 2
    pieces = []
    for start in range(0, values.shape[1], LANES):
        piece = values[:, start : start + LANES]
        partner = jnp.where(
            low,
            pltpu.roll(piece, LANES - HEAD_DIM // 2, 1),
            pltpu.roll(piece, HEAD_DIM // 2, 1),
        )
        turned = partner * sine
        pieces.append(piece * cosine + turned if direction > 0 else piece * cosine - turned)
    return jnp.concatenate(pieces, 1)


def weight_copies(shape, spots_ref, packs, w_ref, wo_ref, small_ref=None):
    if shape["whole"]:
        copies = [(packs[0], w_ref), (packs[1], wo_ref)]
        return copies if small_ref is None else copies + [(packs[2], small_ref)]
    copies = []
    rows, part, columns = shape["pack_rows"], shape["weight_rows"], shape["qkv_columns"]
    wide = shape["merged_columns"]
    for slot, pack in enumerate(packs):
        spot = spots_ref[slot]
        at = pl.multiple_of(spot * rows, rows)
        copies.append((pack.at[:, pl.ds(0, columns)], w_ref.at[pl.ds(at, rows), :]))
        if small_ref is not None:
            copies.append((pack.at[:, pl.ds(columns, LANES)], small_ref.at[pl.ds(at, rows), :]))
        at = pl.multiple_of(spot * part, part)
        for i in range(rows // part):
            copies.append(
                (
                    pack.at[pl.ds(i * part, part), pl.ds(columns + LANES, wide)],
                    wo_ref.at[pl.ds(at, part), pl.ds(i * wide, wide)],
                )
            )
    return copies


def row_copies(slots, into_ref):
    micros, rows, _ = slots[0].shape
    return [
        (slot.at[m], into_ref.at[m, pl.ds(i * rows, rows), :])
        for i, slot in enumerate(slots)
        for m in range(micros)
    ]


def attention_forward_kernel(shape, spots_ref, *refs):
    packs, refs = refs[: shape["packs"]], refs[shape["packs"] :]
    slots, refs = refs[: shape["slots"]], refs[shape["slots"] :]
    cos_ref, sin_ref, bias_ref = refs[:3]
    out_refs, refs = refs[3 : 3 + shape["slots"]], refs[3 + shape["slots"] :]
    x_ref, n1_ref, small_ref, rows_ref, qkv_ref, merged_ref, lse_ref = refs[:7]
    w_ref, wo_ref, semaphores = refs[7:]
    heads, kv_heads = shape["heads"], shape["kv_heads"]
    share = heads // kv_heads
    rotated = (heads + kv_heads) * HEAD_DIM
    micro = pl.program_id(0)

    @pl.when(micro == 0)
    def _():
        copies = weight_copies(shape, spots_ref, packs, w_ref, wo_ref, small_ref)
        fetch(row_copies(slots, x_ref) + copies, semaphores)
        count = rows_ref.shape[0]
        row = lax.broadcasted_iota(jnp.int32, (count, LANES), 0)
        column = lax.broadcasted_iota(jnp.int32, (count, LANES), 1)
        same = jnp.where(row == column, 1.0, 0.0).astype(BF16)
        rows_ref[...] = dot(same, small_ref[...], ((1,), (1,)))

    x = x_ref[micro].astype(F32)
    inverse = lax.rsqrt(jnp.mean(x * x, -1, keepdims=True) + EPSILON)
    at = shape["gain_at"]
    n1_ref[micro] = (x * inverse * rows_ref[at : at + 1, :]).astype(BF16)
    pre = dot(n1_ref[micro], w_ref[...])
    turned = rotate_pairs(pre[:, :rotated], cos_ref[0], sin_ref[0], 1)
    qkv_ref[0, :, :rotated] = turned.astype(BF16)
    qkv_ref[0, :, rotated:] = pre[:, rotated:].astype(BF16)
    bias = bias_ref[0]
    lane = lax.broadcasted_iota(jnp.int32, (pre.shape[0], LANES), 1)
    sums = jnp.zeros((pre.shape[0], LANES), F32)
    for head in range(heads):
        group = head // share
        key_at = (heads + group) * HEAD_DIM
        value_at = rotated + group * HEAD_DIM
        query = qkv_ref[0, :, head * HEAD_DIM : (head + 1) * HEAD_DIM]
        key = qkv_ref[0, :, key_at : key_at + HEAD_DIM]
        value = qkv_ref[0, :, value_at : value_at + HEAD_DIM]
        scores = dot(query, key, ((1,), (1,))) * SCORE_SCALE + bias
        highest = jnp.max(scores, -1, keepdims=True)
        exponent = jnp.exp(scores - highest)
        total = jnp.sum(exponent, -1, keepdims=True)
        weights = (exponent / total).astype(BF16)
        merged_ref[0, :, head * HEAD_DIM : (head + 1) * HEAD_DIM] = dot(weights, value).astype(BF16)
        sums = jnp.where(lane == head, highest + jnp.log(total), sums)
    lse_ref[0] = sums
    rows = out_refs[0].shape[1]
    for i, out_ref in enumerate(out_refs):
        out_ref[0] = dot(merged_ref[0, i * rows : (i + 1) * rows, :], wo_ref[...]).astype(BF16)


def attention_backward_kernel(shape, spots_ref, *refs):
    packs, refs = refs[: shape["packs"]], refs[shape["packs"] :]
    slots, refs = refs[: shape["slots"]], refs[shape["slots"] :]
    cos_ref, sin_ref, bias_ref, qkv_ref, lse_ref, n1_ref, merged_ref = refs[:7]
    x_ref, n2_ref, logits_ref, mlp_ref = refs[7:11]
    refs = refs[11:]
    out_refs, refs = refs[: shape["slots"]], refs[shape["slots"] :]
    grads, refs = refs[: shape["packs"]], refs[shape["packs"] :]
    ga_ref, w_ref, wo_ref, dqkv_ref, turned_ref, gain_ref, dw_ref, dwo_ref, ds_ref, semaphores = refs
    heads, kv_heads = shape["heads"], shape["kv_heads"]
    share = heads // kv_heads
    rotated = (heads + kv_heads) * HEAD_DIM
    micro = pl.program_id(0)

    @pl.when(micro == 0)
    def _():
        copies = row_copies(slots, ga_ref) + weight_copies(shape, spots_ref, packs, w_ref, wo_ref)
        fetch(copies, semaphores)
        gain_ref[...] = jnp.zeros_like(gain_ref)
        gain_ref[1:2, :] = mlp_ref[...]

    grad_merged = dot(ga_ref[micro], wo_ref[...], ((1,), (1,))).astype(BF16)
    bias = bias_ref[0]
    for group in range(kv_heads):
        key_at = (heads + group) * HEAD_DIM
        value_at = rotated + group * HEAD_DIM
        key = qkv_ref[0, :, key_at : key_at + HEAD_DIM]
        value = qkv_ref[0, :, value_at : value_at + HEAD_DIM]
        grad_key, grad_value = None, None
        for head in range(group * share, (group + 1) * share):
            query = qkv_ref[0, :, head * HEAD_DIM : (head + 1) * HEAD_DIM]
            grad_rows = grad_merged[:, head * HEAD_DIM : (head + 1) * HEAD_DIM]
            scores = dot(query, key, ((1,), (1,))) * SCORE_SCALE + bias
            chance = jnp.exp(scores - lse_ref[0, :, head : head + 1])
            weights = chance.astype(BF16)
            grad_chance = dot(grad_rows, value, ((1,), (1,)))
            delta = jnp.sum(chance * grad_chance, -1, keepdims=True)
            grad_raw = (chance * (grad_chance - delta) * SCORE_SCALE).astype(BF16)
            turned_ref[:, head * HEAD_DIM : (head + 1) * HEAD_DIM] = dot(grad_raw, key)
            key_part = dot(grad_raw, query, ((0,), (0,)))
            value_part = dot(weights, grad_rows, ((0,), (0,)))
            grad_key = key_part if grad_key is None else grad_key + key_part
            grad_value = value_part if grad_value is None else grad_value + value_part
        turned_ref[:, key_at : key_at + HEAD_DIM] = grad_key
        dqkv_ref[micro, :, value_at : value_at + HEAD_DIM] = grad_value.astype(BF16)
    back = rotate_pairs(turned_ref[...], cos_ref[0], sin_ref[0], -1)
    dqkv_ref[micro, :, :rotated] = back.astype(BF16)
    rows = out_refs[0].shape[1]
    first = dot(dqkv_ref[micro], w_ref[...], ((1,), (1,)))
    for i, out_ref in enumerate(out_refs):
        out_ref[0] = first[i * rows : (i + 1) * rows, :].astype(BF16)
    x = x_ref[0].astype(F32)
    unit = x * lax.rsqrt(jnp.mean(x * x, -1, keepdims=True) + EPSILON)
    gain_ref[0:1, :] += jnp.sum(first * unit, 0, keepdims=True)

    @pl.when(micro == pl.num_programs(0) - 1)
    def _():
        def flat(ref):
            return ref[...].reshape(ref.shape[0] * ref.shape[1], ref.shape[2])

        dw = dot(flat(n1_ref), flat(dqkv_ref), ((0,), (0,))).astype(BF16)
        dwo = dot(flat(merged_ref), flat(ga_ref), ((0,), (0,))).astype(BF16)
        row = lax.broadcasted_iota(jnp.int32, (gain_ref.shape[0], LANES), 0)
        column = lax.broadcasted_iota(jnp.int32, (gain_ref.shape[0], LANES), 1)
        spread = jnp.where((row < 2) & (column == row + shape["gain_at"]), 1.0, 0.0)
        gains = lax.dot_general(
            gain_ref[...],
            spread,
            (((0,), (0,)), ((), ())),
            precision=lax.Precision.HIGHEST,
            preferred_element_type=F32,
        )
        ds = (gains + dot(n2_ref[...], logits_ref[...], ((0,), (0,)))).astype(BF16)
        if shape["whole"]:
            grads[0][...] = dw
            grads[1][...] = dwo
            grads[2][...] = ds
        else:
            dw_ref[...] = dw
            dwo_ref[...] = dwo
            ds_ref[...] = ds
            pack_rows, part, columns = shape["pack_rows"], shape["weight_rows"], shape["qkv_columns"]
            wide = shape["merged_columns"]
            for slot, grad_ref in enumerate(grads):
                spot = spots_ref[slot]
                at = pl.multiple_of(spot * pack_rows, pack_rows)
                grad_ref[:, :columns] = dw_ref[pl.ds(at, pack_rows), :]
                grad_ref[:, columns : columns + LANES] = ds_ref[pl.ds(at, pack_rows), :]
                at = pl.multiple_of(spot * part, part)
                for i in range(pack_rows // part):
                    grad_ref[i * part : (i + 1) * part, columns + LANES :] = dwo_ref[
                        pl.ds(at, part), i * wide : (i + 1) * wide
                    ]


def per_micro(shape):
    return pl.BlockSpec((1,) + tuple(shape[1:]), lambda m, s: (m,) + (0,) * (len(shape) - 1))


def fixed(shape):
    return pl.BlockSpec(tuple(shape), lambda m, s: (0,) * len(shape))


def attention_forward(shape, spots, packs, slots, cosine, sine, bias):
    micros, rows, width = slots[0].shape
    group = rows * len(slots)
    columns, merged = shape["qkv_columns"], shape["heads"] * HEAD_DIM
    outs = [jax.ShapeDtypeStruct((micros, rows, width), BF16) for _ in slots]
    specs = [per_micro(o.shape) for o in outs]
    more = [
        jax.ShapeDtypeStruct((micros, group, width), BF16),
        jax.ShapeDtypeStruct((micros, group, width), BF16),
        jax.ShapeDtypeStruct((width, LANES), BF16),
        jax.ShapeDtypeStruct((LANES // 2, width), F32),
        jax.ShapeDtypeStruct((micros, group, columns), BF16),
        jax.ShapeDtypeStruct((micros, group, merged), BF16),
        jax.ShapeDtypeStruct((micros, group, LANES), F32),
    ]
    specs += [fixed(o.shape) for o in more[:4]] + [per_micro(o.shape) for o in more[4:]]
    results = pl.pallas_call(
        functools.partial(attention_forward_kernel, shape),
        grid_spec=pltpu.PrefetchScalarGridSpec(
            num_scalar_prefetch=1,
            grid=(micros,),
            in_specs=[anywhere() for _ in packs + slots]
            + [per_micro(cosine.shape), per_micro(sine.shape), per_micro(bias.shape)],
            out_specs=specs,
            scratch_shapes=[
                pltpu.VMEM((width, columns), BF16),
                pltpu.VMEM((merged, width), BF16),
                pltpu.SemaphoreType.DMA((shape["copies"],)),
            ],
        ),
        out_shape=outs + more,
        name="attention_forward",
    )(spots, *packs, *slots, cosine, sine, bias)
    return (results[: len(slots)],) + tuple(results[len(slots) :])


def attention_backward(shape, spots, packs, slots, by_micro, at_once):
    micros, rows, width = slots[0].shape
    group = rows * len(slots)
    columns, merged_rows = shape["qkv_columns"], shape["heads"] * HEAD_DIM
    outs = [jax.ShapeDtypeStruct((micros, rows, width), BF16) for _ in slots]
    grads = [jax.ShapeDtypeStruct(pack.shape, BF16) for pack in packs]
    results = pl.pallas_call(
        functools.partial(attention_backward_kernel, shape),
        grid_spec=pltpu.PrefetchScalarGridSpec(
            num_scalar_prefetch=1,
            grid=(micros,),
            in_specs=[anywhere() for _ in packs + slots]
            + [per_micro(v.shape) for v in by_micro[:5]]
            + [fixed(v.shape) for v in at_once[:2]]
            + [per_micro(by_micro[5].shape)]
            + [fixed(v.shape) for v in at_once[2:]],
            out_specs=[per_micro(o.shape) for o in outs] + [fixed(g.shape) for g in grads],
            scratch_shapes=[
                pltpu.VMEM((micros, group, width), BF16),
                pltpu.VMEM((width, columns), BF16),
                pltpu.VMEM((merged_rows, width), BF16),
                pltpu.VMEM((micros, group, columns), BF16),
                pltpu.VMEM((group, (shape["heads"] + shape["kv_heads"]) * HEAD_DIM), F32),
                pltpu.VMEM((8, width), F32),
                pltpu.VMEM((width, columns), BF16),
                pltpu.VMEM((merged_rows, width), BF16),
                pltpu.VMEM((width, LANES), BF16),
                pltpu.SemaphoreType.DMA((shape["copies"],)),
            ],
        ),
        out_shape=outs + grads,
        name="attention_backward",
    )(spots, *packs, *slots, *by_micro[:5], *at_once[:2], by_micro[5], *at_once[2:])
    return list(results[: len(slots)]), list(results[len(slots) :])


def experts_kernel(shape, table_ref, *refs):
    slots, cores, ys, zs = shape["slots"], shape["cores"], shape["ys"], shape["zs"]
    own, hidden, half = shape["own"], shape["hidden"], LANES // 2
    x_slots, refs = refs[:slots], refs[slots:]
    beside, refs = refs[:slots], refs[slots:]
    gu_parts, refs = refs[: cores * ys], refs[cores * ys :]
    dn_parts, refs = refs[: cores * ys], refs[cores * ys :]
    wr_ref, mixed_ref, dx_ref, gate_ref, gg_ref, x_ref, gm_ref = refs[:7]
    act_refs, refs = refs[7 : 7 + cores], refs[7 + cores :]
    dgu_refs, refs = refs[:cores], refs[cores:]
    mask_ref, wgu_ref, wdn_ref, semaphores = refs
    rows, width = x_slots[0].shape
    part = width // (ys * zs)
    wide = 2 * hidden * own
    local = cores * own

    copies = []
    for i in range(slots):
        at = pl.ds(i * rows, rows)
        copies.append((x_slots[i], x_ref.at[at, :]))
        copies.append((beside[i].at[:, pl.ds(0, width)], gm_ref.at[at, :]))
        copies.append((beside[i].at[:, pl.ds(width, LANES)], mask_ref.at[at, :]))
    step = hidden // ys
    for c in range(cores):
        for s in range(ys):
            y = table_ref[local + s]
            for z in range(zs):
                at = pl.multiple_of((z * ys + y) * part, part)
                copies.append(
                    (
                        gu_parts[c * ys + s].at[z],
                        wgu_ref.at[pl.ds(at, part), pl.ds(c * wide, wide)],
                    )
                )
            for e in range(own):
                at = pl.multiple_of((c * own + e) * hidden + y * step, step)
                copies.append((dn_parts[c * ys + s].at[e], wdn_ref.at[pl.ds(at, step), :]))
    fetch(copies, semaphores)

    block = shape["block"]
    lane = lax.broadcasted_iota(jnp.int32, (block, LANES), 1)

    def body(b, carry):
        at = pl.ds(pl.multiple_of(b * block, block), block)
        x = x_ref[at, :]
        named = mask_ref[at, :].astype(F32) > 0.5
        logits = jnp.where(named, dot(x, wr_ref[...]), NEGATIVE)
        highest = jnp.max(logits, -1, keepdims=True)
        exponent = jnp.where(named, jnp.exp(logits - highest), 0.0)
        gates = exponent / jnp.sum(exponent, -1, keepdims=True)
        gate_ref[at, :] = gates
        picked = jnp.zeros((block, LANES), F32)
        pre_all = dot(x, wgu_ref[...])
        grad_act = dot(gm_ref[at, :], wdn_ref[...], ((1,), (1,)))
        for c in range(cores):
            for e in range(own):
                j = c * own + e
                mine = lane == table_ref[j]
                gate = jnp.sum(jnp.where(mine, gates, 0.0), -1, keepdims=True)
                gate_pre = pre_all[:, 2 * hidden * j : 2 * hidden * j + hidden]
                up_pre = pre_all[:, 2 * hidden * j + hidden : 2 * hidden * (j + 1)]
                grad_one = grad_act[:, j * hidden : (j + 1) * hidden]
                sig = jax.nn.sigmoid(gate_pre)
                silu = gate_pre * sig
                activated = (silu * up_pre).astype(BF16).astype(F32)
                found = jnp.sum(activated * grad_one, -1, keepdims=True)
                picked = jnp.where(mine, found, picked)
                act_refs[c][at, e * hidden : (e + 1) * hidden] = (activated * gate).astype(BF16)
                grad_one = grad_one * gate
                base = 2 * hidden * e
                dgu_refs[c][at, base : base + hidden] = (
                    grad_one * up_pre * sig * (1.0 + gate_pre * (1.0 - sig))
                ).astype(BF16)
                dgu_refs[c][at, base + hidden : base + 2 * hidden] = (grad_one * silu).astype(BF16)
        dgu = jnp.concatenate([ref[at, :] for ref in dgu_refs], 1)
        dx_ref[at, :] = dot(dgu, wgu_ref[...], ((1,), (1,))).astype(BF16)
        act = jnp.concatenate([ref[at, :] for ref in act_refs], 1)
        mixed_ref[at, :] = dot(act, wdn_ref[...]).astype(BF16)
        coarse = picked.astype(BF16).astype(F32)
        fine = pltpu.roll(picked - coarse, half, 1)
        packed = jnp.where(lane < half, coarse, fine).astype(BF16)
        for q in range(block // rows):
            place = table_ref[local + ys + b * (block // rows) + q]
            gg_ref[pl.ds(pl.multiple_of(place * rows, rows), rows), :] = packed[q * rows : (q + 1) * rows]
        return carry

    lax.fori_loop(0, slots * rows // block, body, 0)


def run_experts(shape, table, x_slots, beside, gu_parts, dn_parts, wr):
    rows, width = x_slots[0].shape
    total = rows * len(x_slots)
    cores, own, hidden = shape["cores"], shape["own"], shape["hidden"]
    outs = [
        jax.ShapeDtypeStruct((total, width), BF16),
        jax.ShapeDtypeStruct((total, width), BF16),
        jax.ShapeDtypeStruct((total, LANES), F32),
        jax.ShapeDtypeStruct((total, LANES), BF16),
        jax.ShapeDtypeStruct((total, width), BF16),
        jax.ShapeDtypeStruct((total, width), BF16),
    ]
    outs += [jax.ShapeDtypeStruct((total, own * hidden), BF16) for _ in range(cores)]
    outs += [jax.ShapeDtypeStruct((total, 2 * own * hidden), BF16) for _ in range(cores)]
    shape = dict(shape, slots=len(x_slots), block=2 * rows if len(x_slots) % 2 == 0 else rows)
    copies = 3 * len(x_slots) + cores * shape["ys"] * (shape["zs"] + own)
    operands = x_slots + beside + gu_parts + dn_parts
    return pl.pallas_call(
        functools.partial(experts_kernel, shape),
        in_specs=[pl.BlockSpec(memory_space=pltpu.SMEM)] + [anywhere() for _ in operands] + [on_chip()],
        out_specs=[on_chip() for _ in outs],
        out_shape=outs,
        scratch_shapes=[
            pltpu.VMEM((total, LANES), BF16),
            pltpu.VMEM((width, cores * own * 2 * hidden), BF16),
            pltpu.VMEM((cores * own * hidden, width), BF16),
            pltpu.SemaphoreType.DMA((copies,)),
        ],
        compiler_params=pltpu.CompilerParams(vmem_limit_bytes=60 << 20),
        name="experts",
    )(table, *operands, wr)


def pack_kernel(hidden, gate_ref, up_ref, out_ref):
    for z in range(out_ref.shape[0]):
        out_ref[z, :, :hidden] = gate_ref[0, :, z * hidden : (z + 1) * hidden]
        out_ref[z, :, hidden:] = up_ref[0, :, z * hidden : (z + 1) * hidden]


def pack_experts(w_gate, w_up, zs):
    own, part, hidden_all = w_gate.shape
    hidden = hidden_all // zs
    return pl.pallas_call(
        functools.partial(pack_kernel, hidden),
        grid=(own,),
        in_specs=[pl.BlockSpec((1, part, hidden_all), lambda e: (e, 0, 0))] * 2,
        out_specs=pl.BlockSpec((zs, part, 2 * hidden), lambda e: (0, 0, e)),
        out_shape=jax.ShapeDtypeStruct((zs, part, own * 2 * hidden), BF16),
        name="pack_experts",
    )(w_gate, w_up)


def unpack_kernel(hidden, in_ref, gate_ref, up_ref):
    for z in range(in_ref.shape[0]):
        gate_ref[0, :, z * hidden : (z + 1) * hidden] = in_ref[z, :, :hidden].astype(F32)
        up_ref[0, :, z * hidden : (z + 1) * hidden] = in_ref[z, :, hidden:].astype(F32)


def unpack_experts(packed, own):
    zs, part, wide = packed.shape
    hidden = wide // own // 2
    out = jax.ShapeDtypeStruct((own, part, zs * hidden), F32)
    return pl.pallas_call(
        functools.partial(unpack_kernel, hidden),
        grid=(own,),
        in_specs=[pl.BlockSpec((zs, part, 2 * hidden), lambda e: (0, 0, e))],
        out_specs=[pl.BlockSpec((1, part, zs * hidden), lambda e: (e, 0, 0))] * 2,
        out_shape=[out, out],
        name="unpack_experts",
    )(packed)


def per_device(
    tokens,
    cotangent,
    attn_gain,
    mlp_gain,
    w_query,
    w_key,
    w_value,
    w_out,
    w_router,
    w_gate,
    w_up,
    w_down,
    shuffle,
    routes,
    lengths,
):
    micros, rows, width = tokens.shape
    dp_count, members = lax.axis_size("dp"), lax.axis_size("expert")
    devices = dp_count * members
    rings = Rings(dp_count, members)
    zn, yn, xn, cn = rings.z, rings.y, rings.x, rings.core
    group_rows = rows * members
    experts_all = w_router.shape[1]
    own_experts, model_part, hidden_all = w_gate.shape
    hidden_part = hidden_all // zn
    heads, kv_heads = HEADS // members, KV_HEADS // members
    weight_rows = w_query.shape[0]
    home_rows = micros * rows
    half_lanes = LANES // 2

    def over_members(value):
        return [slot for column in rings.gather_two(value, "c", "x") for slot in column]

    def sum_members(parts):
        return rings.reduce_two([[parts[s * cn + t] for s in range(xn)] for t in range(cn)], "x", "c")

    def by_member(w):
        return w.reshape(weight_rows, members, w.shape[1] // members)

    small = jnp.concatenate([w_router, attn_gain[:, None], mlp_gain[:, None]], 1)
    small = jnp.pad(small, ((0, 0), (0, LANES - experts_all - 2)))
    small = jnp.broadcast_to(small[:, None, :], (weight_rows, members, LANES))
    mine = jnp.concatenate([by_member(w_query), by_member(w_key), by_member(w_value), small], 2)
    mine = lax.all_to_all(mine.transpose(1, 0, 2), "expert", 0, 0)
    gate_up = pack_experts(w_gate, w_up, zn)
    mine, gate_up = tie(mine, gate_up)
    small_at = mine.shape[2]
    qkv_columns = small_at - LANES
    pack_rows = members * weight_rows
    mine = mine.reshape(pack_rows, small_at)
    to_heads = [(s, (s % dp_count) * members + s // dp_count) for s in range(devices)]
    to_home = [(t, s) for s, t in to_heads]
    out_mine = lax.ppermute(w_out, ALL, to_heads)
    merged_columns = width // members
    pack = jnp.concatenate(
        [out_mine[:, i * merged_columns : (i + 1) * merged_columns] for i in range(members)], 0
    )
    pack = jnp.concatenate([mine, pack], 1)
    whole = weight_rows % 16 != 0
    attention_shape = {
        "heads": heads,
        "kv_heads": kv_heads,
        "whole": whole,
        "pack_rows": pack_rows,
        "weight_rows": weight_rows,
        "qkv_columns": qkv_columns,
        "merged_columns": merged_columns,
        "slots": members,
        "gain_at": experts_all,
        "packs": 3 if whole else dp_count,
        "copies": micros * members + (3 if whole else dp_count * (2 + members)),
    }
    inputs = tokens.astype(F32)
    inv_first = lax.rsqrt(jnp.mean(inputs * inputs, -1, keepdims=True) + EPSILON)
    unit_first = inputs * inv_first
    group_tokens = over_members(tokens)

    pack, routes = tie(pack, routes)
    dealt = lax.all_to_all(
        routes.reshape(micros, dp_count, rows // dp_count, routes.shape[2]), "dp", 1, 1
    ).reshape(micros, rows, routes.shape[2])
    lane_ids = jnp.arange(LANES, dtype=jnp.int32)
    hot = jnp.sum((dealt[:, :, :, None] == lane_ids).astype(F32), 2).astype(BF16)
    place = (shuffle[:, 0, :, None] == jnp.arange(rows, dtype=jnp.int32)).astype(BF16)
    named = jnp.einsum("mir,mix->mrx", place, hot, preferred_element_type=F32).astype(BF16)

    grad_result = cotangent.astype(F32)
    grad_moe = (RESIDUAL_SCALE * grad_result).astype(BF16)
    beside = jnp.concatenate([grad_moe, named], 2).reshape(home_rows, width + LANES)

    row_at = jnp.concatenate(
        [
            (rings.origin("x", s) * cn + rings.origin("c", t)) * rows
            + jnp.arange(rows, dtype=jnp.int32)
            for s in range(xn)
            for t in range(cn)
        ]
    )
    row_at, pack = tie(row_at, pack)
    half = HEAD_DIM // 2
    lane = jnp.arange(LANES, dtype=jnp.int32)
    inverse = ROPE_BASE ** (-((lane % half).astype(F32) * 2.0) / HEAD_DIM)
    sign = jnp.where(lane % HEAD_DIM < half, -1.0, 1.0)
    doc_lengths = lengths[:, 0]
    doc_ends = jnp.cumsum(doc_lengths, 1)
    doc_starts = doc_ends - doc_lengths
    segment = jnp.sum((row_at[None, :, None] >= doc_ends[:, None, :]).astype(jnp.int32), 2)
    docs = jnp.arange(doc_lengths.shape[1], dtype=jnp.int32)
    start = jnp.sum(jnp.where(segment[:, :, None] == docs, doc_starts[:, None, :], 0), 2)
    position = row_at[None, :] - start
    angles = position.astype(F32)[:, :, None] * inverse
    cosine, sine = jnp.cos(angles), jnp.sin(angles) * sign
    allowed = segment[:, :, None] == segment[:, None, :]
    bias = jnp.where(allowed & (row_at[None, :] <= row_at[:, None]), 0.0, NEGATIVE)

    waiting = {"beside": beside, "gate_up": gate_up, "down": w_down}
    tables = {"cosine": cosine, "sine": sine, "bias": bias}

    def weights_arrived(slot, value):
        if slot == 1:
            value, *tied = tie(value, *tables.values())
            tables.update(zip(list(tables), tied))
        if slot < zn - 1:
            return value
        names = list(waiting)
        tied = tie(value, *waiting.values())
        waiting.update(zip(names, tied[1:]))
        return tied[0]

    packs = rings.gather_two(pack, "z", "y", weights_arrived)
    spots = jnp.stack(
        [rings.origin("z", t) * yn + rings.origin("y", s) for s in range(yn) for t in range(zn)]
    )
    if whole:
        packs = [in_order(column, rings.at["z"], zn) for column in packs]
        packs = [in_order([packs[s][z] for s in range(yn)], rings.at["y"], yn) for z in range(zn)]
        packs = jnp.stack([packs[z][y] for z in range(zn) for y in range(yn)])
        w_merge = packs[:, :, small_at:].reshape(dp_count, members, weight_rows, merged_columns)
        w_merge = w_merge.transpose(0, 2, 1, 3).reshape(dp_count * weight_rows, width)
        w_small = packs[:, :, qkv_columns:small_at].reshape(width, LANES)
        packs = [packs[:, :, :qkv_columns].reshape(width, qkv_columns), w_merge, w_small]
    else:
        packs = [slot for column in packs for slot in column]

    beside = rings.gather_two(waiting["beside"], "z", "x")
    gate_up = lax.all_to_all(waiting["gate_up"], "dp", 0, 0, axis_index_groups=rings.z_groups)
    down = rings.gather(waiting["down"], "y")
    cosine, sine, bias = tables["cosine"], tables["sine"], tables["bias"]
    attn_parts, group_in, n1, router_columns, small_rows, qkv, merged, lse = attention_forward(
        attention_shape, spots, packs, group_tokens, cosine, sine, bias
    )
    gain_first = small_rows[experts_all]
    gain_second = small_rows[experts_all + 1]
    hidden = inputs + RESIDUAL_SCALE * sum_members(attn_parts)
    inv_second = lax.rsqrt(jnp.mean(hidden * hidden, -1, keepdims=True) + EPSILON)
    unit_second = hidden * inv_second
    normed_second = (unit_second * gain_second).astype(BF16).reshape(home_rows, width)
    def meeting(store, *names):
        def meet(value):
            value, *values = tie(value, *[store[name] for name in names])
            store.update(zip(names, values))
            return value

        return meet

    waiting = {"gate_up": gate_up, "down": down[-1]}

    def rows_arrived(slot, value):
        if slot == 1:
            value = meeting(waiting, "gate_up", "down")(value)
            waiting["parts"] = rings.gather(waiting["gate_up"], "y")[1:]
        if slot == zn - 1:
            value, *waiting["parts"] = tie(value, *waiting["parts"])
        return value

    group_x = rings.gather_two(normed_second, "z", "x", rows_arrived)

    gate_up = [rings.gather(part, "c") for part in [waiting["gate_up"]] + waiting["parts"]]
    down = [rings.gather(part, "c") for part in down[:-1] + [waiting["down"]]]
    gu_parts = [gate_up[s][c] for c in range(cn) for s in range(yn)]
    dn_parts = [down[s][c] for c in range(cn) for s in range(yn)]

    slots = [(s, t) for s in range(xn) for t in range(zn)]
    x_slots = [group_x[s][t] for s, t in slots]
    beside = [beside[s][t] for s, t in slots]
    chunk = min(len(slots), 8)
    chunks = len(slots) // chunk
    table = [
        (rings.at["x"] * cn + rings.origin("c", s)) * own_experts
        + jnp.arange(own_experts, dtype=jnp.int32)
        for s in range(cn)
    ]
    table.append(jnp.stack([rings.origin("y", s) for s in range(yn)]))
    goals = jnp.stack([rings.origin("z", t) * xn + rings.origin("x", s) for s, t in slots])
    table.append(goals if chunks == 1 else jnp.arange(chunk, dtype=jnp.int32))
    table = jnp.concatenate(table)
    experts_shape = {"cores": cn, "ys": yn, "zs": zn, "own": own_experts, "hidden": hidden_part}
    results = [
        run_experts(
            experts_shape,
            table,
            x_slots[i * chunk : (i + 1) * chunk],
            beside[i * chunk : (i + 1) * chunk],
            gu_parts,
            dn_parts,
            router_columns,
        )
        for i in range(chunks)
    ]
    if chunks == 1:
        results = list(results[0])
    else:
        results = [jnp.concatenate(pieces, 0) for pieces in zip(*results)]
    mixed, dx, gates, grad_gates, x_all, gm_all = results[:6]
    acts, dgus = results[6 : 6 + cn], results[6 + cn :]

    def to_owner(value, meet=None):
        parts = value.reshape(xn, zn, home_rows, width)
        parts = [[parts[s, t] for t in range(zn)] for s in range(xn)]
        return rings.reduce_two(parts, "z", "x", meet=meet)

    grad_gates = grad_gates.reshape(len(slots), home_rows, LANES)
    if chunks > 1:
        grad_gates = jnp.zeros_like(grad_gates).at[goals].set(grad_gates)
    grad_gates = lax.all_to_all(grad_gates, ALL, 0, 0, axis_index_groups=rings.token_groups)
    grad_gates = jnp.sum(grad_gates.astype(F32), 0)
    grad_gates = grad_gates[:, :half_lanes] + grad_gates[:, half_lanes:]
    def sum_cores(terms):
        running = None
        for slot in range(1, cn):
            term = terms(slot)
            running = rings.step((term if running is None else term + running).astype(BF16), "c")
            running = running.astype(F32)
        own = terms(0)
        return (own if running is None else own + running).astype(BF16)

    grad_gu = sum_cores(lambda s: dot(x_all, dgus[s], ((0,), (0,))))
    grad_dn = sum_cores(lambda s: dot(acts[s], gm_all, ((0,), (0,))))
    wide = own_experts * 2 * hidden_part
    grad_gu = grad_gu.reshape(zn, yn, model_part, wide)
    grad_gu = [lax.dynamic_index_in_dim(grad_gu, rings.origin("y", s), 1, False) for s in range(yn)]
    grad_dn = grad_dn.reshape(own_experts, yn, hidden_part // yn, width)
    grad_dn = [lax.dynamic_index_in_dim(grad_dn, rings.origin("y", s), 1, False) for s in range(yn)]
    waiting = {"mixed": mixed, "weights": grad_gu + grad_dn}

    def rows_sent(ring, slot, value):
        if ring == "x" and slot == 0:
            value = meeting(waiting, "mixed")(value)
        if ring == "z" and slot == min(2, zn - 1):
            value, *waiting["weights"] = tie(value, *waiting["weights"])
        return value

    grad_dealt = to_owner(dx, rows_sent)
    grad_gu, grad_dn = waiting["weights"][:yn], waiting["weights"][yn:]
    own_gates = gates[:home_rows, :half_lanes]
    grad_picked = own_gates * (grad_gates - jnp.sum(own_gates * grad_gates, -1, keepdims=True))
    grad_logits = grad_picked.astype(BF16)
    grad_dealt = (grad_dealt + dot(grad_logits, small_rows.astype(BF16))).astype(BF16)
    grad_normed_second = grad_dealt.astype(F32).reshape(micros, rows, width)
    scaled_second = grad_normed_second * gain_second
    grad_hidden = grad_result + inv_second * (
        scaled_second - unit_second * jnp.mean(scaled_second * unit_second, -1, keepdims=True)
    )
    mlp_gain_grad = jnp.sum(grad_normed_second * unit_second, (0, 1))[None]
    grad_attn = (RESIDUAL_SCALE * grad_hidden).astype(BF16)

    grad_attn = over_members(grad_attn)
    moe_rows = to_owner(waiting["mixed"]).astype(BF16).reshape(micros, rows, width)
    grad_attn[-1], moe_rows = tie(grad_attn[-1], moe_rows)
    output = (hidden + RESIDUAL_SCALE * moe_rows.astype(F32)).astype(BF16)

    first_parts, weight_grads = attention_backward(
        attention_shape,
        spots,
        packs,
        grad_attn,
        [cosine, sine, bias, qkv, lse, group_in],
        [n1, merged, normed_second, jnp.pad(grad_logits, ((0, 0), (0, half_lanes))), mlp_gain_grad],
    )
    grad_normed_first = sum_members(first_parts)
    scaled_first = grad_normed_first * gain_first
    grad_tokens = grad_hidden + inv_first * (
        scaled_first - unit_first * jnp.mean(scaled_first * unit_first, -1, keepdims=True)
    )

    waiting = {"weights": weight_grads}

    def experts_sent(slot, value):
        value, *waiting["weights"] = tie(value, *waiting["weights"])
        return value

    grad_gu = rings.reduce(grad_gu, "y", meet=experts_sent).astype(BF16)
    grad_dn = rings.reduce(grad_dn, "y", meet=experts_sent)
    grad_gu = lax.all_to_all(grad_gu, "dp", 0, 0, axis_index_groups=rings.z_groups)
    weight_grads = waiting["weights"]

    if whole:
        grad_qkv, grad_out, grad_small = weight_grads
        grad_out = grad_out.reshape(dp_count, weight_rows, members, merged_columns).transpose(0, 2, 1, 3)
        both = jnp.concatenate(
            [
                grad_qkv.reshape(dp_count, pack_rows, qkv_columns),
                grad_small.reshape(dp_count, pack_rows, LANES),
                grad_out.reshape(dp_count, pack_rows, merged_columns),
            ],
            2,
        )
        weight_grads = [
            lax.dynamic_index_in_dim(both, spots[i], 0, False) for i in range(dp_count)
        ]
    both = rings.reduce_two(
        [[weight_grads[s * zn + t] for t in range(zn)] for s in range(yn)], "z", "y"
    )
    both, grad_gu = tie(both, grad_gu)
    grad_gate, grad_up = unpack_experts(grad_gu, own_experts)
    grad_out = [
        both[i * weight_rows : (i + 1) * weight_rows, small_at:] for i in range(members)
    ]
    grad_out = lax.ppermute(jnp.concatenate(grad_out, 1), ALL, to_home)
    home = both[:, :small_at].reshape(members, weight_rows, small_at)
    home = lax.all_to_all(home, "expert", 0, 0)

    def columns(start, count):
        return jnp.concatenate([home[i, :, start : start + count] for i in range(members)], 1)

    query_columns, key_columns = heads * HEAD_DIM, kv_heads * HEAD_DIM
    grad_query = columns(0, query_columns)
    grad_key = columns(query_columns, key_columns)
    grad_value = columns(query_columns + key_columns, key_columns)

    small = jnp.sum(home[:, :, qkv_columns:], 0)
    grad_w_router = small[:, :experts_all]
    grad_attn_gain, grad_mlp_gain = small[:, experts_all], small[:, experts_all + 1]

    return (
        output,
        grad_tokens,
        grad_attn_gain,
        grad_mlp_gain,
        grad_query,
        grad_key,
        grad_value,
        grad_out,
        grad_w_router,
        grad_gate,
        grad_up,
        grad_dn,
    )


def solution(mesh):
    rows = P(None, ALL, None)
    placed = (rows, rows, P(ALL), P(ALL)) + (P(ALL, None),) * 5
    placed += (P("expert", "dp", None),) * 3 + (rows, rows, P(None, "dp", None))
    results = (rows, rows, P(ALL), P(ALL)) + (P(ALL, None),) * 5
    results += (P("expert", "dp", None),) * 3
    return jax.shard_map(per_device, mesh=mesh, in_specs=placed, out_specs=results, check_vma=False)
```

```python
import functools

import jax
import jax.numpy as jnp
from jax import lax
from jax.experimental import pallas as pl
from jax.experimental.pallas import tpu as pltpu
from jax.sharding import PartitionSpec as P

HEADS = 24
KV_HEADS = 8
HEAD_DIM = 64

EPSILON = 1e-06
ROPE_BASE = 10000.0
RESIDUAL_SCALE = 0.22
SCORE_SCALE = 1.0 / 64.0
NEGATIVE = -1e30
LANES = 128

BF16 = jnp.bfloat16
F32 = jnp.float32
ALL = ("dp", "expert")


def dot(a, b, dims=((1,), (0,))):
    return lax.dot_general(a, b, (dims, ((), ())), preferred_element_type=F32)


class Rings:
    def __init__(self, dp_count, expert_count):
        y_count = 1
        while dp_count % (2 * y_count) == 0 and 8 * y_count * y_count <= dp_count:
            y_count *= 2
        self.y, self.z = y_count, dp_count // y_count
        self.core = 2 if expert_count % 2 == 0 else 1
        self.x = expert_count // self.core
        zs, ys, xs, cs = range(self.z), range(self.y), range(self.x), range(self.core)
        self.z_groups = [[z * self.y + y for z in zs] for y in ys]
        self.token_groups = [
            [(z * self.y + y) * expert_count + x * self.core + c for z in zs for x in xs]
            for y in ys
            for c in cs
        ]
        self.table = {
            "z": ("dp", self.z, [(z * self.y + y, (z + 1) % self.z * self.y + y) for z in zs for y in ys]),
            "y": ("dp", self.y, [(z * self.y + y, z * self.y + (y + 1) % self.y) for z in zs for y in ys]),
            "x": (
                "expert",
                self.x,
                [(x * self.core + c, (x + 1) % self.x * self.core + c) for x in xs for c in cs],
            ),
            "c": (
                "expert",
                self.core,
                [(x * self.core + c, x * self.core + (c + 1) % self.core) for x in xs for c in cs],
            ),
        }
        d, e = lax.axis_index("dp"), lax.axis_index("expert")
        self.at = {"z": d // self.y, "y": d % self.y, "x": e // self.core, "c": e % self.core}

    def count(self, ring):
        return self.table[ring][1]

    def step(self, value, ring):
        axis, _, pairs = self.table[ring]
        return lax.ppermute(value, axis, pairs)

    def origin(self, ring, slot):
        return lax.rem(self.at[ring] + (self.count(ring) - slot), self.count(ring))

    def gather(self, value, ring):
        slots = [value]
        for _ in range(1, self.count(ring)):
            slots.append(self.step(slots[-1], ring))
        return slots

    def send(self, terms, ring, wire=None):
        running = None
        for term in terms[1:]:
            if running is None:
                term = term.astype(BF16)
            else:
                term = term.astype(F32) + running.astype(F32)
                term = term.astype(BF16) if wire is None else wire(term)
            running = self.step(term, ring)
        return running


    def gather_two(self, value, first, second, count=None):
        columns, slot = [], value
        count = self.count(first) if count is None else count
        for t in range(count):
            column = self.gather(slot, second)
            ahead = [self.step(slot, first)] if t + 1 < count else []
            tied = yield ahead + column[1:]
            columns.append([column[0]] + tied[len(ahead) :])
            slot = tied[0]
        return [[column[s] for column in columns] for s in range(self.count(second))]

    def reduce(self, parts, ring):
        running = self.send(parts, ring)
        own = parts[0]
        if running is not None:
            own, running = yield [own, running]
        return own.astype(F32) if running is None else own.astype(F32) + running.astype(F32)

    def reduce_two(self, parts, first, second, wire=None):
        count = self.count(first)
        parts = [list(row) for row in parts]
        arrived, running = {}, None
        order = list(range(1, count)) + [0]
        for phase in range(count + (count > 1)):
            made = []
            if phase > 0:
                t = order[phase - 1]
                term = self.partial(parts, arrived, t)
                if running is not None:
                    term = term + running.astype(F32)
                made.append(self.step(term.astype(BF16) if wire is None else wire(term), first))
            if phase < count:
                passing = self.send([row[order[phase]] for row in parts], second, wire)
                if passing is not None:
                    made.append(passing)
            after = [row[order[phase + 1]] for row in parts] if phase + 1 < count else []
            tied = yield made + after
            if after:
                for row, value in zip(parts, tied[len(made) :]):
                    row[order[phase + 1]] = value
            if phase < count and passing is not None:
                arrived[order[phase]] = tied[len(made) - 1]
            if phase > 0:
                running = tied[0]
            if phase == count - 1 and count > 1:
                break
        own = self.partial(parts, arrived, 0)
        return own if running is None else own + running.astype(F32)

    def partial(self, parts, arrived, t):
        own = parts[0][t].astype(F32)
        return own if t not in arrived else own + arrived[t].astype(F32)


def two_part(term):
    width = term.shape[1] - 2 * LANES
    value = term[:, width : width + LANES] + term[:, width + LANES :]
    coarse = value.astype(BF16)
    fine = (value - coarse.astype(F32)).astype(BF16)
    return jnp.concatenate([term[:, :width].astype(BF16), coarse, fine], 1)


class Task:
    def __init__(self, steps):
        self.steps, self.made, self.result, self.done = steps, [], None, False
        self.advance(None)

    def advance(self, values):
        try:
            self.made = list(self.steps.send(values))
        except StopIteration as stop:
            self.result, self.done, self.made = stop.value, True, []


class Phases:
    def __init__(self):
        self.tasks = []

    def start(self, steps):
        task = Task(steps)
        self.tasks.append(task)
        return task

    def phase(self):
        self.tasks = [task for task in self.tasks if not task.done]
        made = [value for task in self.tasks for value in task.made]
        tied = list(tie(*made)) if made else []
        for task in self.tasks:
            count = len(task.made)
            values, tied = tied[:count], tied[count:]
            task.advance(values)

    def finish(self, *tasks):
        while not all(task.done for task in tasks):
            self.phase()
        return [task.result for task in tasks]


def resumed(steps, made):
    while True:
        made = yield made
        try:
            made = steps.send(made)
        except StopIteration as stop:
            return stop.value


def paced(steps, ready):
    made = next(steps)
    while True:
        tied = yield made
        while not ready:
            tied = yield tied
        try:
            made = steps.send(tied)
        except StopIteration as stop:
            return stop.value


def make(function, *arguments):
    flat, tree = jax.tree.flatten(function(*arguments))
    flat = yield flat
    return jax.tree.unflatten(tree, flat)


def tie(*values):
    return lax.optimization_barrier(values)


def in_order(slots, position_of, count):
    stacked = jnp.stack(slots)
    return [
        lax.dynamic_index_in_dim(stacked, lax.rem(position_of + (count - i), count), 0, False)
        for i in range(count)
    ]


def fetch(copies, semaphores):
    started = [pltpu.make_async_copy(a, b, semaphores.at[i]) for i, (a, b) in enumerate(copies)]
    for copy in started:
        copy.start()
    for copy in started:
        copy.wait()


def anywhere():
    return pl.BlockSpec(memory_space=pl.ANY)


def on_chip():
    return pl.BlockSpec(memory_space=pltpu.VMEM)


def rotate_pairs(values, cosine, sine, direction):
    lane = lax.broadcasted_iota(jnp.int32, (values.shape[0], LANES), 1)
    low = (lane & (HEAD_DIM - 1)) < HEAD_DIM // 2
    pieces = []
    for start in range(0, values.shape[1], LANES):
        piece = values[:, start : start + LANES]
        partner = jnp.where(
            low,
            pltpu.roll(piece, LANES - HEAD_DIM // 2, 1),
            pltpu.roll(piece, HEAD_DIM // 2, 1),
        )
        turned = partner * sine
        pieces.append(piece * cosine + turned if direction > 0 else piece * cosine - turned)
    return jnp.concatenate(pieces, 1)


def weight_copies(shape, spots_ref, packs, w_ref, wo_ref, small_ref=None):
    if shape["whole"]:
        copies = [(packs[0], w_ref), (packs[1], wo_ref)]
        return copies if small_ref is None else copies + [(packs[2], small_ref)]
    copies = []
    rows, part, columns = shape["pack_rows"], shape["weight_rows"], shape["qkv_columns"]
    wide = shape["merged_columns"]
    for slot, pack in enumerate(packs):
        spot = spots_ref[slot]
        at = pl.multiple_of(spot * rows, rows)
        copies.append((pack.at[:, pl.ds(0, columns)], w_ref.at[pl.ds(at, rows), :]))
        if small_ref is not None:
            copies.append((pack.at[:, pl.ds(columns, LANES)], small_ref.at[pl.ds(at, rows), :]))
        at = pl.multiple_of(spot * part, part)
        for i in range(rows // part):
            copies.append(
                (
                    pack.at[pl.ds(i * part, part), pl.ds(columns + LANES, wide)],
                    wo_ref.at[pl.ds(at, part), pl.ds(i * wide, wide)],
                )
            )
    return copies


def row_copies(slots, into_ref):
    micros, rows, _ = slots[0].shape
    return [
        (slot.at[m], into_ref.at[m, pl.ds(i * rows, rows), :])
        for i, slot in enumerate(slots)
        for m in range(micros)
    ]


def attention_forward_kernel(shape, spots_ref, *refs):
    packs, refs = refs[: shape["packs"]], refs[shape["packs"] :]
    slots, refs = refs[: shape["slots"]], refs[shape["slots"] :]
    cos_ref, sin_ref, bias_ref = refs[:3]
    out_refs, refs = refs[3 : 3 + shape["slots"]], refs[3 + shape["slots"] :]
    x_ref, n1_ref, small_ref, rows_ref, qkv_ref, merged_ref, lse_ref = refs[:7]
    w_ref, wo_ref, semaphores = refs[7:]
    heads, kv_heads = shape["heads"], shape["kv_heads"]
    share = heads // kv_heads
    rotated = (heads + kv_heads) * HEAD_DIM
    micro = pl.program_id(0)

    @pl.when(micro == 0)
    def _():
        copies = weight_copies(shape, spots_ref, packs, w_ref, wo_ref, small_ref)
        fetch(row_copies(slots, x_ref) + copies, semaphores)
        count = rows_ref.shape[0]
        row = lax.broadcasted_iota(jnp.int32, (count, LANES), 0)
        column = lax.broadcasted_iota(jnp.int32, (count, LANES), 1)
        same = jnp.where(row == column, 1.0, 0.0).astype(BF16)
        rows_ref[...] = dot(same, small_ref[...], ((1,), (1,)))

    x = x_ref[micro].astype(F32)
    inverse = lax.rsqrt(jnp.mean(x * x, -1, keepdims=True) + EPSILON)
    at = shape["gain_at"]
    n1_ref[micro] = (x * inverse * rows_ref[at : at + 1, :]).astype(BF16)
    pre = dot(n1_ref[micro], w_ref[...])
    turned = rotate_pairs(pre[:, :rotated], cos_ref[0], sin_ref[0], 1)
    qkv_ref[0, :, :rotated] = turned.astype(BF16)
    qkv_ref[0, :, rotated:] = pre[:, rotated:].astype(BF16)
    bias = bias_ref[0]
    lane = lax.broadcasted_iota(jnp.int32, (pre.shape[0], LANES), 1)
    sums = jnp.zeros((pre.shape[0], LANES), F32)
    for head in range(heads):
        group = head // share
        key_at = (heads + group) * HEAD_DIM
        value_at = rotated + group * HEAD_DIM
        query = qkv_ref[0, :, head * HEAD_DIM : (head + 1) * HEAD_DIM]
        key = qkv_ref[0, :, key_at : key_at + HEAD_DIM]
        value = qkv_ref[0, :, value_at : value_at + HEAD_DIM]
        scores = dot(query, key, ((1,), (1,))) * SCORE_SCALE + bias
        highest = jnp.max(scores, -1, keepdims=True)
        exponent = jnp.exp(scores - highest)
        total = jnp.sum(exponent, -1, keepdims=True)
        weights = (exponent / total).astype(BF16)
        merged_ref[0, :, head * HEAD_DIM : (head + 1) * HEAD_DIM] = dot(weights, value).astype(BF16)
        sums = jnp.where(lane == head, highest + jnp.log(total), sums)
    lse_ref[0] = sums
    rows = out_refs[0].shape[1]
    for i, out_ref in enumerate(out_refs):
        out_ref[0] = dot(merged_ref[0, i * rows : (i + 1) * rows, :], wo_ref[...]).astype(BF16)


def attention_backward_kernel(shape, spots_ref, *refs):
    packs, refs = refs[: shape["packs"]], refs[shape["packs"] :]
    slots, refs = refs[: shape["slots"]], refs[shape["slots"] :]
    cos_ref, sin_ref, bias_ref, qkv_ref, lse_ref, n1_ref, merged_ref = refs[:7]
    x_ref, n2_ref, logits_ref, mlp_ref = refs[7:11]
    refs = refs[11:]
    out_refs, refs = refs[: shape["slots"]], refs[shape["slots"] :]
    grads, refs = refs[: shape["packs"]], refs[shape["packs"] :]
    ga_ref, w_ref, wo_ref, dqkv_ref, turned_ref, gain_ref, dw_ref, dwo_ref, ds_ref, semaphores = refs
    heads, kv_heads = shape["heads"], shape["kv_heads"]
    share = heads // kv_heads
    rotated = (heads + kv_heads) * HEAD_DIM
    micro = pl.program_id(0)

    @pl.when(micro == 0)
    def _():
        copies = row_copies(slots, ga_ref) + weight_copies(shape, spots_ref, packs, w_ref, wo_ref)
        fetch(copies, semaphores)
        gain_ref[...] = jnp.zeros_like(gain_ref)
        gain_ref[1:2, :] = mlp_ref[...]

    grad_merged = dot(ga_ref[micro], wo_ref[...], ((1,), (1,))).astype(BF16)
    bias = bias_ref[0]
    for group in range(kv_heads):
        key_at = (heads + group) * HEAD_DIM
        value_at = rotated + group * HEAD_DIM
        key = qkv_ref[0, :, key_at : key_at + HEAD_DIM]
        value = qkv_ref[0, :, value_at : value_at + HEAD_DIM]
        grad_key, grad_value = None, None
        for head in range(group * share, (group + 1) * share):
            query = qkv_ref[0, :, head * HEAD_DIM : (head + 1) * HEAD_DIM]
            grad_rows = grad_merged[:, head * HEAD_DIM : (head + 1) * HEAD_DIM]
            scores = dot(query, key, ((1,), (1,))) * SCORE_SCALE + bias
            chance = jnp.exp(scores - lse_ref[0, :, head : head + 1])
            weights = chance.astype(BF16)
            grad_chance = dot(grad_rows, value, ((1,), (1,)))
            delta = jnp.sum(chance * grad_chance, -1, keepdims=True)
            grad_raw = (chance * (grad_chance - delta) * SCORE_SCALE).astype(BF16)
            turned_ref[:, head * HEAD_DIM : (head + 1) * HEAD_DIM] = dot(grad_raw, key)
            key_part = dot(grad_raw, query, ((0,), (0,)))
            value_part = dot(weights, grad_rows, ((0,), (0,)))
            grad_key = key_part if grad_key is None else grad_key + key_part
            grad_value = value_part if grad_value is None else grad_value + value_part
        turned_ref[:, key_at : key_at + HEAD_DIM] = grad_key
        dqkv_ref[micro, :, value_at : value_at + HEAD_DIM] = grad_value.astype(BF16)
    back = rotate_pairs(turned_ref[...], cos_ref[0], sin_ref[0], -1)
    dqkv_ref[micro, :, :rotated] = back.astype(BF16)
    rows = out_refs[0].shape[1]
    first = dot(dqkv_ref[micro], w_ref[...], ((1,), (1,)))
    for i, out_ref in enumerate(out_refs):
        out_ref[0] = first[i * rows : (i + 1) * rows, :].astype(BF16)
    x = x_ref[0].astype(F32)
    unit = x * lax.rsqrt(jnp.mean(x * x, -1, keepdims=True) + EPSILON)
    gain_ref[0:1, :] += jnp.sum(first * unit, 0, keepdims=True)

    @pl.when(micro == pl.num_programs(0) - 1)
    def _():
        def flat(ref):
            return ref[...].reshape(ref.shape[0] * ref.shape[1], ref.shape[2])

        dw = dot(flat(n1_ref), flat(dqkv_ref), ((0,), (0,))).astype(BF16)
        dwo = dot(flat(merged_ref), flat(ga_ref), ((0,), (0,))).astype(BF16)
        row = lax.broadcasted_iota(jnp.int32, (gain_ref.shape[0], LANES), 0)
        column = lax.broadcasted_iota(jnp.int32, (gain_ref.shape[0], LANES), 1)
        spread = jnp.where((row < 2) & (column == row + shape["gain_at"]), 1.0, 0.0)
        gains = lax.dot_general(
            gain_ref[...],
            spread,
            (((0,), (0,)), ((), ())),
            precision=lax.Precision.HIGHEST,
            preferred_element_type=F32,
        )
        ds = (gains + dot(n2_ref[...], logits_ref[...], ((0,), (0,)))).astype(BF16)
        if shape["whole"]:
            grads[0][...] = dw
            grads[1][...] = dwo
            grads[2][...] = ds
        else:
            dw_ref[...] = dw
            dwo_ref[...] = dwo
            ds_ref[...] = ds
            pack_rows, part, columns = shape["pack_rows"], shape["weight_rows"], shape["qkv_columns"]
            wide = shape["merged_columns"]
            for slot, grad_ref in enumerate(grads):
                spot = spots_ref[slot]
                at = pl.multiple_of(spot * pack_rows, pack_rows)
                grad_ref[:, :columns] = dw_ref[pl.ds(at, pack_rows), :]
                grad_ref[:, columns : columns + LANES] = ds_ref[pl.ds(at, pack_rows), :]
                at = pl.multiple_of(spot * part, part)
                for i in range(pack_rows // part):
                    grad_ref[i * part : (i + 1) * part, columns + LANES :] = dwo_ref[
                        pl.ds(at, part), i * wide : (i + 1) * wide
                    ]


def per_micro(shape):
    return pl.BlockSpec((1,) + tuple(shape[1:]), lambda m, s: (m,) + (0,) * (len(shape) - 1))


def fixed(shape):
    return pl.BlockSpec(tuple(shape), lambda m, s: (0,) * len(shape))


def attention_forward(shape, spots, packs, slots, cosine, sine, bias):
    micros, rows, width = slots[0].shape
    group = rows * len(slots)
    columns, merged = shape["qkv_columns"], shape["heads"] * HEAD_DIM
    outs = [jax.ShapeDtypeStruct((micros, rows, width), BF16) for _ in slots]
    specs = [per_micro(o.shape) for o in outs]
    more = [
        jax.ShapeDtypeStruct((micros, group, width), BF16),
        jax.ShapeDtypeStruct((micros, group, width), BF16),
        jax.ShapeDtypeStruct((width, LANES), BF16),
        jax.ShapeDtypeStruct((LANES // 2, width), F32),
        jax.ShapeDtypeStruct((micros, group, columns), BF16),
        jax.ShapeDtypeStruct((micros, group, merged), BF16),
        jax.ShapeDtypeStruct((micros, group, LANES), F32),
    ]
    specs += [fixed(o.shape) for o in more[:4]] + [per_micro(o.shape) for o in more[4:]]
    results = pl.pallas_call(
        functools.partial(attention_forward_kernel, shape),
        grid_spec=pltpu.PrefetchScalarGridSpec(
            num_scalar_prefetch=1,
            grid=(micros,),
            in_specs=[anywhere() for _ in packs + slots]
            + [per_micro(cosine.shape), per_micro(sine.shape), per_micro(bias.shape)],
            out_specs=specs,
            scratch_shapes=[
                pltpu.VMEM((width, columns), BF16),
                pltpu.VMEM((merged, width), BF16),
                pltpu.SemaphoreType.DMA((shape["copies"],)),
            ],
        ),
        out_shape=outs + more,
        name="attention_forward",
    )(spots, *packs, *slots, cosine, sine, bias)
    return (results[: len(slots)],) + tuple(results[len(slots) :])


def attention_backward(shape, spots, packs, slots, by_micro, at_once):
    micros, rows, width = slots[0].shape
    group = rows * len(slots)
    columns, merged_rows = shape["qkv_columns"], shape["heads"] * HEAD_DIM
    outs = [jax.ShapeDtypeStruct((micros, rows, width), BF16) for _ in slots]
    grads = [jax.ShapeDtypeStruct(pack.shape, BF16) for pack in packs]
    results = pl.pallas_call(
        functools.partial(attention_backward_kernel, shape),
        grid_spec=pltpu.PrefetchScalarGridSpec(
            num_scalar_prefetch=1,
            grid=(micros,),
            in_specs=[anywhere() for _ in packs + slots]
            + [per_micro(v.shape) for v in by_micro[:5]]
            + [fixed(v.shape) for v in at_once[:2]]
            + [per_micro(by_micro[5].shape)]
            + [fixed(v.shape) for v in at_once[2:]],
            out_specs=[per_micro(o.shape) for o in outs] + [fixed(g.shape) for g in grads],
            scratch_shapes=[
                pltpu.VMEM((micros, group, width), BF16),
                pltpu.VMEM((width, columns), BF16),
                pltpu.VMEM((merged_rows, width), BF16),
                pltpu.VMEM((micros, group, columns), BF16),
                pltpu.VMEM((group, (shape["heads"] + shape["kv_heads"]) * HEAD_DIM), F32),
                pltpu.VMEM((8, width), F32),
                pltpu.VMEM((width, columns), BF16),
                pltpu.VMEM((merged_rows, width), BF16),
                pltpu.VMEM((width, LANES), BF16),
                pltpu.SemaphoreType.DMA((shape["copies"],)),
            ],
        ),
        out_shape=outs + grads,
        name="attention_backward",
    )(spots, *packs, *slots, *by_micro[:5], *at_once[:2], by_micro[5], *at_once[2:])
    return list(results[: len(slots)]), list(results[len(slots) :])


def experts_kernel(shape, table_ref, *refs):
    slots, cores, ys, zs = shape["slots"], shape["cores"], shape["ys"], shape["zs"]
    own, hidden = shape["own"], shape["hidden"]
    x_slots, refs = refs[:slots], refs[slots:]
    beside, refs = refs[:slots], refs[slots:]
    gu_parts, refs = refs[: cores * ys], refs[cores * ys :]
    dn_parts, refs = refs[: cores * ys], refs[cores * ys :]
    wr_ref, gate_ref, x_out, gm_out = refs[:4]
    back_outs, refs = refs[4 : 4 + slots], refs[4 + slots :]
    act_outs, refs = refs[:cores], refs[cores:]
    dgu_outs, refs = refs[:cores], refs[cores:]
    x_ref, gm_ref, mask_ref, wgu_ref, wdn_ref, act_ref, dgu_ref, back_ref, in_sems, out_sems = refs
    rows, width = x_slots[0].shape[0], x_ref.shape[1]
    part = width // (ys * zs)
    wide, tall = 2 * hidden * own, hidden * own
    local = cores * own

    fetched = [[] for _ in range(cores + 2)]
    for i in range(slots):
        at = pl.ds(i * rows, rows)
        first = width if shape["joined"][i] else 0
        fetched[0].append((x_slots[i].at[:, pl.ds(0, width)], x_ref.at[at, :]))
        fetched[cores].append((beside[i].at[:, pl.ds(first + width, LANES)], mask_ref.at[at, :]))
        fetched[cores + 1].append((beside[i].at[:, pl.ds(first, width)], gm_ref.at[at, :]))
    step = hidden // ys
    for c in range(cores):
        for s in range(ys):
            y = table_ref[local + s]
            for z in range(zs):
                at = pl.multiple_of((z * ys + y) * part, part)
                goal = wgu_ref.at[pl.ds(at, part), pl.ds(c * wide, wide)]
                fetched[c].append((gu_parts[c * ys + s].at[z], goal))
            for e in range(own):
                at = pl.multiple_of((c * own + e) * hidden + y * step, step)
                goal = wdn_ref.at[pl.ds(at, step), :]
                fetched[cores + 1].append((dn_parts[c * ys + s].at[e], goal))
    used = 0
    for group in fetched:
        for i, (source, goal) in enumerate(group):
            group[i] = pltpu.make_async_copy(source, goal, in_sems.at[used])
            group[i].start()
            used += 1

    def arrive(group):
        for copy in fetched[group]:
            copy.wait()

    leaving = []

    def leave(source, goal):
        leaving.append(pltpu.make_async_copy(source, goal, out_sems.at[len(leaving)]))
        leaving[-1].start()

    pre = []
    for c in range(cores):
        arrive(c)
        if c == 0:
            leave(x_ref, x_out)
        pre.append(dot(x_ref[...], wgu_ref[:, c * wide : (c + 1) * wide]))
    arrive(cores)
    total = slots * rows
    lane = lax.broadcasted_iota(jnp.int32, (total, LANES), 1)
    named = mask_ref[...].astype(F32) > 0.5
    logits = jnp.where(named, dot(x_ref[...], wr_ref[...]), NEGATIVE)
    highest = jnp.max(logits, -1, keepdims=True)
    exponent = jnp.where(named, jnp.exp(logits - highest), 0.0)
    gates = exponent / jnp.sum(exponent, -1, keepdims=True)
    gate_ref[...] = gates
    arrive(cores + 1)
    leave(gm_ref, gm_out)
    grad_act = dot(gm_ref[...], wdn_ref[...], ((1,), (1,)))
    picked = jnp.zeros((total, LANES), F32)
    for c in range(cores):
        for e in range(own):
            j = c * own + e
            mine = lane == table_ref[j]
            gate = jnp.sum(jnp.where(mine, gates, 0.0), -1, keepdims=True)
            base = 2 * hidden * e
            gate_pre = pre[c][:, base : base + hidden]
            up_pre = pre[c][:, base + hidden : base + 2 * hidden]
            grad_one = grad_act[:, j * hidden : (j + 1) * hidden]
            sig = jax.nn.sigmoid(gate_pre)
            silu = gate_pre * sig
            activated = (silu * up_pre).astype(BF16).astype(F32)
            found = jnp.sum(activated * grad_one, -1, keepdims=True)
            picked = jnp.where(mine, found, picked)
            act_ref[c, :, e * hidden : (e + 1) * hidden] = (activated * gate).astype(BF16)
            grad_one = grad_one * gate
            base = 2 * hidden * j
            dgu_ref[:, base : base + hidden] = (
                grad_one * up_pre * sig * (1.0 + gate_pre * (1.0 - sig))
            ).astype(BF16)
            dgu_ref[:, base + hidden : base + 2 * hidden] = (grad_one * silu).astype(BF16)
        leave(dgu_ref.at[:, pl.ds(c * wide, wide)], dgu_outs[c])
        leave(act_ref.at[c], act_outs[c])

    coarse = picked.astype(BF16)
    back_ref[:, 2 * width : 2 * width + LANES] = coarse
    back_ref[:, 2 * width + LANES :] = (picked - coarse.astype(F32)).astype(BF16)
    back_ref[:, :width] = dot(dgu_ref[...], wgu_ref[...], ((1,), (1,))).astype(BF16)

    def leave_back(low, count):
        for i in range(slots):
            source = back_ref.at[pl.ds(i * rows, rows), pl.ds(low, count)]
            leave(source, back_outs[i].at[:, pl.ds(low, count)])

    leave_back(0, width)
    leave_back(2 * width, 2 * LANES)
    if tall % LANES == 0:
        acts = jnp.concatenate([act_ref[c] for c in range(cores)], 1)
        mixed = dot(acts, wdn_ref[...])
    else:
        mixed = sum(dot(act_ref[c], wdn_ref[c * tall : (c + 1) * tall, :]) for c in range(cores))
    back_ref[:, width : 2 * width] = mixed.astype(BF16)
    leave_back(width, width)
    for copy in leaving:
        copy.wait()


def run_experts(shape, table, x_slots, beside, gu_parts, dn_parts, wr):
    rows, width = x_slots[0].shape[0], wr.shape[0]
    total = rows * len(x_slots)
    cores, own, hidden = shape["cores"], shape["own"], shape["hidden"]
    outs = [
        jax.ShapeDtypeStruct((total, LANES), F32),
        jax.ShapeDtypeStruct((total, width), BF16),
        jax.ShapeDtypeStruct((total, width), BF16),
    ]
    outs += [jax.ShapeDtypeStruct((rows, 2 * width + 2 * LANES), BF16) for _ in x_slots]
    outs += [jax.ShapeDtypeStruct((total, own * hidden), BF16) for _ in range(cores)]
    outs += [jax.ShapeDtypeStruct((total, 2 * own * hidden), BF16) for _ in range(cores)]
    joined = [slot.shape[1] > width for slot in x_slots]
    shape = dict(shape, slots=len(x_slots), joined=joined)
    copies = 3 * len(x_slots) + cores * shape["ys"] * (shape["zs"] + own)
    operands = x_slots + beside + gu_parts + dn_parts
    return pl.pallas_call(
        functools.partial(experts_kernel, shape),
        in_specs=[pl.BlockSpec(memory_space=pltpu.SMEM)] + [anywhere() for _ in operands] + [on_chip()],
        out_specs=[on_chip()] + [anywhere() for _ in outs[1:]],
        out_shape=outs,
        scratch_shapes=[
            pltpu.VMEM((total, width), BF16),
            pltpu.VMEM((total, width), BF16),
            pltpu.VMEM((total, LANES), BF16),
            pltpu.VMEM((width, cores * own * 2 * hidden), BF16),
            pltpu.VMEM((cores * own * hidden, width), BF16),
            pltpu.VMEM((cores, total, own * hidden), BF16),
            pltpu.VMEM((total, cores * own * 2 * hidden), BF16),
            pltpu.VMEM((total, 2 * width + 2 * LANES), BF16),
            pltpu.SemaphoreType.DMA((copies,)),
            pltpu.SemaphoreType.DMA((2 + 2 * cores + 3 * len(x_slots),)),
        ],
        compiler_params=pltpu.CompilerParams(vmem_limit_bytes=60 << 20),
        name="experts",
    )(table, *operands, wr)


def pack_kernel(hidden, gate_ref, up_ref, out_ref):
    for z in range(out_ref.shape[0]):
        out_ref[z, :, :hidden] = gate_ref[0, :, z * hidden : (z + 1) * hidden]
        out_ref[z, :, hidden:] = up_ref[0, :, z * hidden : (z + 1) * hidden]


def pack_experts(w_gate, w_up, zs):
    own, part, hidden_all = w_gate.shape
    hidden = hidden_all // zs
    return pl.pallas_call(
        functools.partial(pack_kernel, hidden),
        grid=(own,),
        in_specs=[pl.BlockSpec((1, part, hidden_all), lambda e: (e, 0, 0))] * 2,
        out_specs=pl.BlockSpec((zs, part, 2 * hidden), lambda e: (0, 0, e)),
        out_shape=jax.ShapeDtypeStruct((zs, part, own * 2 * hidden), BF16),
        name="pack_experts",
    )(w_gate, w_up)


def unpack_kernel(hidden, in_ref, gate_ref, up_ref):
    for z in range(in_ref.shape[0]):
        gate_ref[0, :, z * hidden : (z + 1) * hidden] = in_ref[z, :, :hidden].astype(F32)
        up_ref[0, :, z * hidden : (z + 1) * hidden] = in_ref[z, :, hidden:].astype(F32)


def unpack_experts(packed, own):
    zs, part, wide = packed.shape
    hidden = wide // own // 2
    out = jax.ShapeDtypeStruct((own, part, zs * hidden), F32)
    return pl.pallas_call(
        functools.partial(unpack_kernel, hidden),
        grid=(own,),
        in_specs=[pl.BlockSpec((zs, part, 2 * hidden), lambda e: (0, 0, e))],
        out_specs=[pl.BlockSpec((1, part, zs * hidden), lambda e: (e, 0, 0))] * 2,
        out_shape=[out, out],
        name="unpack_experts",
    )(packed)


def per_device(
    tokens,
    cotangent,
    attn_gain,
    mlp_gain,
    w_query,
    w_key,
    w_value,
    w_out,
    w_router,
    w_gate,
    w_up,
    w_down,
    shuffle,
    routes,
    lengths,
):
    micros, rows, width = tokens.shape
    dp_count, members = lax.axis_size("dp"), lax.axis_size("expert")
    devices = dp_count * members
    rings = Rings(dp_count, members)
    zn, yn, xn, cn = rings.z, rings.y, rings.x, rings.core
    group_rows = rows * members
    experts_all = w_router.shape[1]
    own_experts, model_part, hidden_all = w_gate.shape
    hidden_part = hidden_all // zn
    heads, kv_heads = HEADS // members, KV_HEADS // members
    weight_rows = w_query.shape[0]
    home_rows = micros * rows

    phases = Phases()

    def over_members(value):
        return phases.start(rings.gather_two(value, "c", "x"))

    def sum_members(parts):
        parts = [[parts[s * cn + t] for s in range(xn)] for t in range(cn)]
        return phases.start(rings.reduce_two(parts, "x", "c"))

    def line(columns):
        return [slot for column in columns for slot in column]

    def by_member(w):
        return w.reshape(weight_rows, members, w.shape[1] // members)

    small = jnp.concatenate([w_router, attn_gain[:, None], mlp_gain[:, None]], 1)
    small = jnp.pad(small, ((0, 0), (0, LANES - experts_all - 2)))
    small = jnp.broadcast_to(small[:, None, :], (weight_rows, members, LANES))
    mine = jnp.concatenate([by_member(w_query), by_member(w_key), by_member(w_value), small], 2)
    mine = lax.all_to_all(mine.transpose(1, 0, 2), "expert", 0, 0)
    small_at = mine.shape[2]
    qkv_columns = small_at - LANES
    pack_rows = members * weight_rows
    mine = mine.reshape(pack_rows, small_at)
    to_heads = [(s, (s % dp_count) * members + s // dp_count) for s in range(devices)]
    to_home = [(t, s) for s, t in to_heads]
    out_mine = lax.ppermute(w_out, ALL, to_heads)
    weights_started = []
    group_tokens = phases.start(paced(rings.gather_two(tokens, "c", "x"), weights_started))
    gate_up = pack_experts(w_gate, w_up, zn)
    begun = phases.start(make(lambda: (mine, gate_up, out_mine, routes)))
    phases.phase()
    (mine, gate_up, out_mine, routes) = begun.result
    merged_columns = width // members
    pack = jnp.concatenate(
        [out_mine[:, i * merged_columns : (i + 1) * merged_columns] for i in range(members)], 0
    )
    pack = jnp.concatenate([mine, pack], 1)
    whole = weight_rows % 16 != 0
    attention_shape = {
        "heads": heads,
        "kv_heads": kv_heads,
        "whole": whole,
        "pack_rows": pack_rows,
        "weight_rows": weight_rows,
        "qkv_columns": qkv_columns,
        "merged_columns": merged_columns,
        "slots": members,
        "gain_at": experts_all,
        "packs": 3 if whole else dp_count,
        "copies": micros * members + (3 if whole else dp_count * (2 + members)),
    }
    def beside_started(value):
        column = rings.gather(value, "x")
        ahead = [rings.step(value, "z")] if zn > 1 else []
        tied = yield ahead + column[1:]
        return [column[0]] + tied[len(ahead) :], tied[0]

    inputs = tokens.astype(F32)
    inv_first = lax.rsqrt(jnp.mean(inputs * inputs, -1, keepdims=True) + EPSILON)
    unit_first = inputs * inv_first

    pack, routes, w_down = tie(pack, routes, w_down)
    packs = phases.start(rings.gather_two(pack, "z", "y"))
    weights_started.append(True)
    phases.phase()
    dealt = lax.all_to_all(
        routes.reshape(micros, dp_count, rows // dp_count, routes.shape[2]), "dp", 1, 1
    ).reshape(micros, rows, routes.shape[2])
    held = phases.start(make(lambda: dealt))
    phases.phase()
    dealt = held.result
    lane_ids = jnp.arange(LANES, dtype=jnp.int32)
    hot = jnp.sum((dealt[:, :, :, None] == lane_ids).astype(F32), 2).astype(BF16)
    place = (shuffle[:, 0, :, None] == jnp.arange(rows, dtype=jnp.int32)).astype(BF16)
    named = jnp.einsum("mir,mix->mrx", place, hot, preferred_element_type=F32).astype(BF16)

    grad_result = cotangent.astype(F32)
    grad_moe = (RESIDUAL_SCALE * grad_result).astype(BF16)
    beside = jnp.concatenate([grad_moe, named], 2).reshape(home_rows, width + LANES)

    row_at = jnp.concatenate(
        [
            (rings.origin("x", s) * cn + rings.origin("c", t)) * rows
            + jnp.arange(rows, dtype=jnp.int32)
            for s in range(xn)
            for t in range(cn)
        ]
    )
    row_at, dealt = tie(row_at, dealt)
    half = HEAD_DIM // 2
    lane = jnp.arange(LANES, dtype=jnp.int32)
    inverse = ROPE_BASE ** (-((lane % half).astype(F32) * 2.0) / HEAD_DIM)
    sign = jnp.where(lane % HEAD_DIM < half, -1.0, 1.0)
    doc_lengths = lengths[:, 0]
    doc_ends = jnp.cumsum(doc_lengths, 1)
    doc_starts = doc_ends - doc_lengths
    segment = jnp.sum((row_at[None, :, None] >= doc_ends[:, None, :]).astype(jnp.int32), 2)
    docs = jnp.arange(doc_lengths.shape[1], dtype=jnp.int32)
    start = jnp.sum(jnp.where(segment[:, :, None] == docs, doc_starts[:, None, :], 0), 2)
    position = row_at[None, :] - start
    angles = position.astype(F32)[:, :, None] * inverse
    cosine, sine = jnp.cos(angles), jnp.sin(angles) * sign
    allowed = segment[:, :, None] == segment[:, None, :]
    bias = jnp.where(allowed & (row_at[None, :] <= row_at[:, None]), 0.0, NEGATIVE)

    tables = phases.start(make(lambda: (cosine, sine, bias, beside, gate_up, w_down)))
    phases.phase()
    cosine, sine, bias, beside, gate_up, w_down = tables.result
    beside = phases.start(beside_started(beside))
    gate_up = lax.all_to_all(gate_up, "dp", 0, 0, axis_index_groups=rings.z_groups)
    held = phases.start(make(lambda: w_down))
    packs, group_tokens = phases.finish(packs, group_tokens)
    w_down = held.result
    spots = jnp.stack(
        [rings.origin("z", t) * yn + rings.origin("y", s) for s in range(yn) for t in range(zn)]
    )
    if whole:
        packs = [in_order(column, rings.at["z"], zn) for column in packs]
        packs = [in_order([packs[s][z] for s in range(yn)], rings.at["y"], yn) for z in range(zn)]
        packs = jnp.stack([packs[z][y] for z in range(zn) for y in range(yn)])
        w_merge = packs[:, :, small_at:].reshape(dp_count, members, weight_rows, merged_columns)
        w_merge = w_merge.transpose(0, 2, 1, 3).reshape(dp_count * weight_rows, width)
        w_small = packs[:, :, qkv_columns:small_at].reshape(width, LANES)
        packs = [packs[:, :, :qkv_columns].reshape(width, qkv_columns), w_merge, w_small]
    else:
        packs = line(packs)

    down = rings.gather(w_down, "y")
    attention = phases.start(
        make(
            attention_forward,
            attention_shape,
            spots,
            packs,
            line(group_tokens),
            cosine,
            sine,
            bias,
        )
    )
    down_task = phases.start(make(lambda: down))
    phases.finish(attention)
    down = phases.start(make(lambda: [rings.gather(part, "c") for part in down_task.result]))
    attn_parts, group_in, n1, router_columns, small_rows, qkv, merged, lse = attention.result
    gain_first = small_rows[experts_all]
    gain_second = small_rows[experts_all + 1]
    attended = sum_members(attn_parts)
    for _ in range(xn - 1):
        phases.phase()
    gate_up = phases.start(make(lambda: gate_up))
    attended, down, gate_up = phases.finish(attended, down, gate_up)
    hidden = inputs + RESIDUAL_SCALE * attended
    inv_second = lax.rsqrt(jnp.mean(hidden * hidden, -1, keepdims=True) + EPSILON)
    unit_second = hidden * inv_second
    normed_second = (unit_second * gain_second).astype(BF16).reshape(home_rows, width)

    if zn > 1:
        first = phases.start(make(lambda: [rings.step(normed_second, "z")] + rings.gather(normed_second, "x")))
        phases.finish(first)
        passed, *column = first.result
        together = jnp.concatenate([passed, beside.result[1]], 1)
        group = phases.start(rings.gather_two(together, "z", "x", zn - 1))
    else:
        first = phases.start(make(lambda: rings.gather(normed_second, "x")))
        phases.finish(first)
        column, group = first.result, None
    gate_up = rings.gather(gate_up, "y")
    if group is not None:
        phases.phase()
        phases.phase()
    mine_too = phases.start(make(lambda: rings.gather(gate_up[0], "c")))
    gate_up = phases.start(make(lambda: gate_up[1:]))
    phases.finish(mine_too, gate_up, *([] if group is None else [group]))
    gate_up = [mine_too.result] + [rings.gather(part, "c") for part in gate_up.result]
    later = [[] for _ in range(xn)] if group is None else group.result
    group_x = [[column[i]] + later[i] for i in range(xn)]
    beside = [[beside.result[0][i]] + later[i] for i in range(xn)]
    gu_parts = [gate_up[s][c] for c in range(cn) for s in range(yn)]
    dn_parts = [down[s][c] for c in range(cn) for s in range(yn)]

    slots = [(s, t) for s in range(xn) for t in range(zn)]
    x_slots = [group_x[s][t] for s, t in slots]
    beside = [beside[s][t] for s, t in slots]
    chunk = min(len(slots), 8)
    chunks = len(slots) // chunk
    table = [
        (rings.at["x"] * cn + rings.origin("c", s)) * own_experts
        + jnp.arange(own_experts, dtype=jnp.int32)
        for s in range(cn)
    ]
    table.append(jnp.stack([rings.origin("y", s) for s in range(yn)]))
    table = jnp.concatenate(table)
    experts_shape = {"cores": cn, "ys": yn, "zs": zn, "own": own_experts, "hidden": hidden_part}
    results = [
        run_experts(
            experts_shape,
            table,
            x_slots[i * chunk : (i + 1) * chunk],
            beside[i * chunk : (i + 1) * chunk],
            gu_parts,
            dn_parts,
            router_columns,
        )
        for i in range(chunks)
    ]
    back = [part for pieces in results for part in pieces[3 : 3 + chunk]]
    results = [pieces[:3] + pieces[3 + chunk :] for pieces in results]
    results = [pieces[0] if chunks == 1 else jnp.concatenate(pieces, 0) for pieces in zip(*results)]
    gates, x_all, gm_all = results[:3]
    acts, dgus = results[3 : 3 + cn], results[3 + cn :]
    back = [back[i * zn : (i + 1) * zn] for i in range(xn)]

    def by_y(value, axis):
        return [lax.dynamic_index_in_dim(value, rings.origin("y", s), axis, False) for s in range(yn)]

    def product(core, kind, x, gm, coming):
        if kind == 0:
            term = dot(x, dgus[core], ((0,), (0,)))
        else:
            term = dot(acts[core], gm, ((0,), (0,)))
        return (term if coming is None else term + coming.astype(F32)).astype(BF16)

    def own_gu(x, coming):
        return by_y(product(0, 0, x, None, coming).reshape(zn, yn, model_part, -1), 1)

    def own_dn(gm, coming):
        value = product(0, 1, None, gm, coming)
        return by_y(value.reshape(own_experts, yn, hidden_part // yn, width), 1)

    rows_back = phases.start(rings.reduce_two(back, "z", "x", two_part))
    if cn > 1:
        work = phases.start(make(lambda: (product(1, 0, x_all, None, None), x_all, gm_all)))
        phases.phase()
        other, x, gm = work.result
        coming = rings.step(other, "c")
    else:
        x, gm, coming = x_all, gm_all, None
    work = phases.start(make(lambda: (own_gu(x, coming), gm)))
    phases.phase()
    made, gm = work.result
    groups = [(0, 2), (2, 4), (4, own_experts)] if own_experts > 4 else [(0, own_experts)]
    wide = 2 * hidden_part
    made = [[part[:, :, low * wide : high * wide] for part in made] for low, high in groups]
    grad_gu = []

    def next_group():
        if len(grad_gu) < len(groups):
            grad_gu.append(phases.start(rings.reduce(made[len(grad_gu)], "y")))

    next_group()
    if cn > 1:
        work = phases.start(make(lambda: (product(1, 1, None, gm, None), gm)))
        phases.phase()
        other, gm = work.result
        coming = rings.step(other, "c")
    next_group()
    work = phases.start(make(lambda: own_dn(gm, coming)))
    phases.finish(rows_back, work)
    grad_dn = work.result
    grad_dealt, moe_rows = rows_back.result[:, :width], rows_back.result[:, width : 2 * width]
    grad_gates = rows_back.result[:, 2 * width :]
    grad_gates = grad_gates[:, :LANES] + grad_gates[:, LANES:]
    own_gates = gates[:home_rows]
    grad_picked = own_gates * (grad_gates - jnp.sum(own_gates * grad_gates, -1, keepdims=True))
    grad_logits = grad_picked.astype(BF16)
    router_rows = small_rows.astype(BF16)
    grad_dealt = (grad_dealt + dot(grad_logits[:, : LANES // 2], router_rows)).astype(BF16)
    grad_normed_second = grad_dealt.astype(F32).reshape(micros, rows, width)
    scaled_second = grad_normed_second * gain_second
    grad_hidden = grad_result + inv_second * (
        scaled_second - unit_second * jnp.mean(scaled_second * unit_second, -1, keepdims=True)
    )
    mlp_gain_grad = jnp.sum(grad_normed_second * unit_second, (0, 1))[None]
    grad_attn = (RESIDUAL_SCALE * grad_hidden).astype(BF16)

    grad_attn = over_members(grad_attn)
    grad_dn = rings.reduce(grad_dn, "y")
    made_dn = next(grad_dn)
    while len(grad_gu) < len(groups):
        next_group()
    phases.phase()
    grad_gu = jnp.concatenate([part.astype(BF16) for part in phases.finish(*grad_gu)], 2)
    grad_gu = lax.all_to_all(grad_gu, "dp", 0, 0, axis_index_groups=rings.z_groups)
    phases.finish(grad_attn)
    grad_dn = phases.start(resumed(grad_dn, made_dn))

    attention = phases.start(
        make(
            attention_backward,
            attention_shape,
            spots,
            packs,
            line(grad_attn.result),
            [cosine, sine, bias, qkv, lse, group_in],
            [n1, merged, normed_second, grad_logits, mlp_gain_grad],
        )
    )
    phases.finish(attention)
    first_parts, weight_grads = attention.result

    if whole:
        grad_qkv, grad_out, grad_small = weight_grads
        grad_out = grad_out.reshape(dp_count, weight_rows, members, merged_columns).transpose(0, 2, 1, 3)
        both = jnp.concatenate(
            [
                grad_qkv.reshape(dp_count, pack_rows, qkv_columns),
                grad_small.reshape(dp_count, pack_rows, LANES),
                grad_out.reshape(dp_count, pack_rows, merged_columns),
            ],
            2,
        )
        weight_grads = [
            lax.dynamic_index_in_dim(both, spots[i], 0, False) for i in range(dp_count)
        ]
    both = phases.start(
        rings.reduce_two([[weight_grads[s * zn + t] for t in range(zn)] for s in range(yn)], "z", "y")
    )
    grad_gu = phases.start(make(lambda: grad_gu))
    phases.phase()
    grad_normed_first = sum_members(first_parts)
    both, grad_gu, grad_dn, grad_normed_first = phases.finish(
        both, grad_gu, grad_dn, grad_normed_first
    )
    grad_gate, grad_up = unpack_experts(grad_gu, own_experts)
    moe_rows = moe_rows.astype(BF16).reshape(micros, rows, width)
    output = (hidden + RESIDUAL_SCALE * moe_rows.astype(F32)).astype(BF16)
    scaled_first = grad_normed_first * gain_first
    grad_tokens = grad_hidden + inv_first * (
        scaled_first - unit_first * jnp.mean(scaled_first * unit_first, -1, keepdims=True)
    )
    grad_out = [
        both[i * weight_rows : (i + 1) * weight_rows, small_at:] for i in range(members)
    ]
    grad_out = lax.ppermute(jnp.concatenate(grad_out, 1), ALL, to_home)
    home = both[:, :small_at].reshape(members, weight_rows, small_at)
    home = lax.all_to_all(home, "expert", 0, 0)

    def columns(start, count):
        return jnp.concatenate([home[i, :, start : start + count] for i in range(members)], 1)

    query_columns, key_columns = heads * HEAD_DIM, kv_heads * HEAD_DIM
    grad_query = columns(0, query_columns)
    grad_key = columns(query_columns, key_columns)
    grad_value = columns(query_columns + key_columns, key_columns)

    small = jnp.sum(home[:, :, qkv_columns:], 0)
    grad_w_router = small[:, :experts_all]
    grad_attn_gain, grad_mlp_gain = small[:, experts_all], small[:, experts_all + 1]

    return (
        output,
        grad_tokens,
        grad_attn_gain,
        grad_mlp_gain,
        grad_query,
        grad_key,
        grad_value,
        grad_out,
        grad_w_router,
        grad_gate,
        grad_up,
        grad_dn,
    )


def solution(mesh):
    rows = P(None, ALL, None)
    placed = (rows, rows, P(ALL), P(ALL)) + (P(ALL, None),) * 5
    placed += (P("expert", "dp", None),) * 3 + (rows, rows, P(None, "dp", None))
    results = (rows, rows, P(ALL), P(ALL)) + (P(ALL, None),) * 5
    results += (P("expert", "dp", None),) * 3
    return jax.shard_map(per_device, mesh=mesh, in_specs=placed, out_specs=results, check_vma=False)
```

```python
import functools

import jax
import jax.numpy as jnp
from jax import lax
from jax.experimental import pallas as pl
from jax.experimental.pallas import tpu as pltpu
from jax.sharding import PartitionSpec as P

HEADS = 24
KV_HEADS = 8
HEAD_DIM = 64

EPSILON = 1e-06
ROPE_BASE = 10000.0
RESIDUAL_SCALE = 0.22
SCORE_SCALE = 1.0 / 64.0
NEGATIVE = -1e30
LANES = 128

BF16 = jnp.bfloat16
F32 = jnp.float32
ALL = ("dp", "expert")


def dot(a, b, dims=((1,), (0,))):
    return lax.dot_general(a, b, (dims, ((), ())), preferred_element_type=F32)


class Rings:
    def __init__(self, dp_count, expert_count):
        y_count = 1
        while dp_count % (2 * y_count) == 0 and 8 * y_count * y_count <= dp_count:
            y_count *= 2
        self.y, self.z = y_count, dp_count // y_count
        self.core = 2 if expert_count % 2 == 0 else 1
        self.x = expert_count // self.core
        zs, ys, xs, cs = range(self.z), range(self.y), range(self.x), range(self.core)
        self.z_groups = [[z * self.y + y for z in zs] for y in ys]
        self.token_groups = [
            [(z * self.y + y) * expert_count + x * self.core + c for z in zs for x in xs]
            for y in ys
            for c in cs
        ]
        self.table = {
            "z": ("dp", self.z, [(z * self.y + y, (z + 1) % self.z * self.y + y) for z in zs for y in ys]),
            "y": ("dp", self.y, [(z * self.y + y, z * self.y + (y + 1) % self.y) for z in zs for y in ys]),
            "x": (
                "expert",
                self.x,
                [(x * self.core + c, (x + 1) % self.x * self.core + c) for x in xs for c in cs],
            ),
            "c": (
                "expert",
                self.core,
                [(x * self.core + c, x * self.core + (c + 1) % self.core) for x in xs for c in cs],
            ),
        }
        d, e = lax.axis_index("dp"), lax.axis_index("expert")
        self.at = {"z": d // self.y, "y": d % self.y, "x": e // self.core, "c": e % self.core}

    def count(self, ring):
        return self.table[ring][1]

    def step(self, value, ring):
        axis, _, pairs = self.table[ring]
        return lax.ppermute(value, axis, pairs)

    def origin(self, ring, slot):
        return lax.rem(self.at[ring] + (self.count(ring) - slot), self.count(ring))

    def gather(self, value, ring):
        slots = [value]
        for _ in range(1, self.count(ring)):
            slots.append(self.step(slots[-1], ring))
        return slots

    def send(self, terms, ring, wire=None):
        running = None
        for term in terms[1:]:
            if running is None:
                term = term.astype(BF16)
            else:
                term = term.astype(F32) + running.astype(F32)
                term = term.astype(BF16) if wire is None else wire(term)
            running = self.step(term, ring)
        return running


    def gather_two(self, value, first, second, count=None):
        columns, slot = [], value
        count = self.count(first) if count is None else count
        for t in range(count):
            column = self.gather(slot, second)
            ahead = [self.step(slot, first)] if t + 1 < count else []
            tied = yield ahead + column[1:]
            columns.append([column[0]] + tied[len(ahead) :])
            slot = tied[0]
        return [[column[s] for column in columns] for s in range(self.count(second))]

    def reduce(self, parts, ring):
        running = self.send(parts, ring)
        own = parts[0]
        if running is not None:
            own, running = yield [own, running]
        return own.astype(F32) if running is None else own.astype(F32) + running.astype(F32)

    def reduce_two(self, parts, first, second, wire=None):
        count = self.count(first)
        parts = [list(row) for row in parts]
        arrived, running = {}, None
        order = list(range(1, count)) + [0]
        for phase in range(count + (count > 1)):
            made = []
            if phase > 0:
                t = order[phase - 1]
                term = self.partial(parts, arrived, t)
                if running is not None:
                    term = term + running.astype(F32)
                made.append(self.step(term.astype(BF16) if wire is None else wire(term), first))
            if phase < count:
                passing = self.send([row[order[phase]] for row in parts], second, wire)
                if passing is not None:
                    made.append(passing)
            after = [row[order[phase + 1]] for row in parts] if phase + 1 < count else []
            tied = yield made + after
            if after:
                for row, value in zip(parts, tied[len(made) :]):
                    row[order[phase + 1]] = value
            if phase < count and passing is not None:
                arrived[order[phase]] = tied[len(made) - 1]
            if phase > 0:
                running = tied[0]
            if phase == count - 1 and count > 1:
                break
        own = self.partial(parts, arrived, 0)
        return own if running is None else own + running.astype(F32)

    def partial(self, parts, arrived, t):
        own = parts[0][t].astype(F32)
        return own if t not in arrived else own + arrived[t].astype(F32)


def two_part(term):
    width = term.shape[1] - 2 * LANES
    value = term[:, width : width + LANES] + term[:, width + LANES :]
    coarse = value.astype(BF16)
    fine = (value - coarse.astype(F32)).astype(BF16)
    return jnp.concatenate([term[:, :width].astype(BF16), coarse, fine], 1)


class Task:
    def __init__(self, steps):
        self.steps, self.made, self.result, self.done = steps, [], None, False
        self.advance(None)

    def advance(self, values):
        try:
            self.made = list(self.steps.send(values))
        except StopIteration as stop:
            self.result, self.done, self.made = stop.value, True, []


class Phases:
    def __init__(self):
        self.tasks = []

    def start(self, steps):
        task = Task(steps)
        self.tasks.append(task)
        return task

    def phase(self):
        self.tasks = [task for task in self.tasks if not task.done]
        made = [value for task in self.tasks for value in task.made]
        tied = list(tie(*made)) if made else []
        for task in self.tasks:
            count = len(task.made)
            values, tied = tied[:count], tied[count:]
            task.advance(values)

    def finish(self, *tasks):
        while not all(task.done for task in tasks):
            self.phase()
        return [task.result for task in tasks]


def resumed(steps, made):
    while True:
        made = yield made
        try:
            made = steps.send(made)
        except StopIteration as stop:
            return stop.value


def paced(steps, ready):
    made = next(steps)
    while True:
        tied = yield made
        while not ready:
            tied = yield tied
        try:
            made = steps.send(tied)
        except StopIteration as stop:
            return stop.value


def make(function, *arguments):
    flat, tree = jax.tree.flatten(function(*arguments))
    flat = yield flat
    return jax.tree.unflatten(tree, flat)


def tie(*values):
    return lax.optimization_barrier(values)


def in_order(slots, position_of, count):
    stacked = jnp.stack(slots)
    return [
        lax.dynamic_index_in_dim(stacked, lax.rem(position_of + (count - i), count), 0, False)
        for i in range(count)
    ]


def fetch(copies, semaphores):
    started = [pltpu.make_async_copy(a, b, semaphores.at[i]) for i, (a, b) in enumerate(copies)]
    for copy in started:
        copy.start()
    for copy in started:
        copy.wait()


def anywhere():
    return pl.BlockSpec(memory_space=pl.ANY)


def on_chip():
    return pl.BlockSpec(memory_space=pltpu.VMEM)


def rotate_pairs(values, cosine, sine, direction):
    lane = lax.broadcasted_iota(jnp.int32, (values.shape[0], LANES), 1)
    low = (lane & (HEAD_DIM - 1)) < HEAD_DIM // 2
    pieces = []
    for start in range(0, values.shape[1], LANES):
        piece = values[:, start : start + LANES]
        partner = jnp.where(
            low,
            pltpu.roll(piece, LANES - HEAD_DIM // 2, 1),
            pltpu.roll(piece, HEAD_DIM // 2, 1),
        )
        turned = partner * sine
        pieces.append(piece * cosine + turned if direction > 0 else piece * cosine - turned)
    return jnp.concatenate(pieces, 1)


def weight_copies(shape, spots_ref, packs, w_ref, wo_ref, small_ref=None):
    if shape["whole"]:
        copies = [(packs[0], w_ref), (packs[1], wo_ref)]
        return copies if small_ref is None else copies + [(packs[2], small_ref)]
    copies = []
    rows, part, columns = shape["pack_rows"], shape["weight_rows"], shape["qkv_columns"]
    wide = shape["merged_columns"]
    for slot, pack in enumerate(packs):
        spot = spots_ref[slot]
        at = pl.multiple_of(spot * rows, rows)
        copies.append((pack.at[:, pl.ds(0, columns)], w_ref.at[pl.ds(at, rows), :]))
        if small_ref is not None:
            copies.append((pack.at[:, pl.ds(columns, LANES)], small_ref.at[pl.ds(at, rows), :]))
        at = pl.multiple_of(spot * part, part)
        for i in range(rows // part):
            copies.append(
                (
                    pack.at[pl.ds(i * part, part), pl.ds(columns + LANES, wide)],
                    wo_ref.at[pl.ds(at, part), pl.ds(i * wide, wide)],
                )
            )
    return copies


def row_copies(slots, into_ref):
    micros, rows, _ = slots[0].shape
    return [
        (slot.at[m], into_ref.at[m, pl.ds(i * rows, rows), :])
        for i, slot in enumerate(slots)
        for m in range(micros)
    ]


def attention_forward_kernel(shape, spots_ref, *refs):
    packs, refs = refs[: shape["packs"]], refs[shape["packs"] :]
    slots, refs = refs[: shape["slots"]], refs[shape["slots"] :]
    cos_ref, sin_ref, bias_ref = refs[:3]
    out_refs, refs = refs[3 : 3 + shape["slots"]], refs[3 + shape["slots"] :]
    x_ref, n1_ref, small_ref, rows_ref, qkv_ref, merged_ref, lse_ref = refs[:7]
    w_ref, wo_ref, semaphores = refs[7:]
    heads, kv_heads = shape["heads"], shape["kv_heads"]
    share = heads // kv_heads
    rotated = (heads + kv_heads) * HEAD_DIM
    micro = pl.program_id(0)

    @pl.when(micro == 0)
    def _():
        copies = weight_copies(shape, spots_ref, packs, w_ref, wo_ref, small_ref)
        fetch(row_copies(slots, x_ref) + copies, semaphores)
        count = rows_ref.shape[0]
        row = lax.broadcasted_iota(jnp.int32, (count, LANES), 0)
        column = lax.broadcasted_iota(jnp.int32, (count, LANES), 1)
        same = jnp.where(row == column, 1.0, 0.0).astype(BF16)
        rows_ref[...] = dot(same, small_ref[...], ((1,), (1,)))

    x = x_ref[micro].astype(F32)
    inverse = lax.rsqrt(jnp.mean(x * x, -1, keepdims=True) + EPSILON)
    at = shape["gain_at"]
    n1_ref[micro] = (x * inverse * rows_ref[at : at + 1, :]).astype(BF16)
    pre = dot(n1_ref[micro], w_ref[...])
    turned = rotate_pairs(pre[:, :rotated], cos_ref[0], sin_ref[0], 1)
    qkv_ref[0, :, :rotated] = turned.astype(BF16)
    qkv_ref[0, :, rotated:] = pre[:, rotated:].astype(BF16)
    bias = bias_ref[0]
    lane = lax.broadcasted_iota(jnp.int32, (pre.shape[0], LANES), 1)
    sums = jnp.zeros((pre.shape[0], LANES), F32)
    for head in range(heads):
        group = head // share
        key_at = (heads + group) * HEAD_DIM
        value_at = rotated + group * HEAD_DIM
        query = qkv_ref[0, :, head * HEAD_DIM : (head + 1) * HEAD_DIM]
        key = qkv_ref[0, :, key_at : key_at + HEAD_DIM]
        value = qkv_ref[0, :, value_at : value_at + HEAD_DIM]
        scores = dot(query * SCORE_SCALE, key, ((1,), (1,))) + bias
        highest = jnp.max(scores, -1, keepdims=True)
        exponent = jnp.exp(scores - highest)
        total = jnp.sum(exponent, -1, keepdims=True)
        weights = (exponent * (1.0 / total)).astype(BF16)
        merged_ref[0, :, head * HEAD_DIM : (head + 1) * HEAD_DIM] = dot(weights, value).astype(BF16)
        sums = jnp.where(lane == head, highest + jnp.log(total), sums)
    lse_ref[0] = sums
    rows = out_refs[0].shape[1]
    for i, out_ref in enumerate(out_refs):
        out_ref[0] = dot(merged_ref[0, i * rows : (i + 1) * rows, :], wo_ref[...]).astype(BF16)


def attention_backward_kernel(shape, spots_ref, *refs):
    packs, refs = refs[: shape["packs"]], refs[shape["packs"] :]
    slots, refs = refs[: shape["slots"]], refs[shape["slots"] :]
    cos_ref, sin_ref, bias_ref, qkv_ref, lse_ref, n1_ref, merged_ref = refs[:7]
    x_ref, n2_ref, logits_ref, mlp_ref = refs[7:11]
    refs = refs[11:]
    out_refs, refs = refs[: shape["slots"]], refs[shape["slots"] :]
    grads, refs = refs[: shape["packs"]], refs[shape["packs"] :]
    ga_ref, w_ref, wo_ref, dqkv_ref, turned_ref, gain_ref, dw_ref, dwo_ref, ds_ref, semaphores = refs
    heads, kv_heads = shape["heads"], shape["kv_heads"]
    share = heads // kv_heads
    rotated = (heads + kv_heads) * HEAD_DIM
    micro = pl.program_id(0)

    @pl.when(micro == 0)
    def _():
        copies = row_copies(slots, ga_ref) + weight_copies(shape, spots_ref, packs, w_ref, wo_ref)
        fetch(copies, semaphores)
        gain_ref[...] = jnp.zeros_like(gain_ref)
        gain_ref[1:2, :] = mlp_ref[...]

    grad_merged = dot(ga_ref[micro], wo_ref[...], ((1,), (1,))).astype(BF16)
    bias = bias_ref[0]
    for group in range(kv_heads):
        key_at = (heads + group) * HEAD_DIM
        value_at = rotated + group * HEAD_DIM
        key = qkv_ref[0, :, key_at : key_at + HEAD_DIM] * SCORE_SCALE
        value = qkv_ref[0, :, value_at : value_at + HEAD_DIM]
        grad_key, grad_value = None, None
        for head in range(group * share, (group + 1) * share):
            query = qkv_ref[0, :, head * HEAD_DIM : (head + 1) * HEAD_DIM]
            grad_rows = grad_merged[:, head * HEAD_DIM : (head + 1) * HEAD_DIM]
            scores = dot(query, key, ((1,), (1,))) + bias
            chance = jnp.exp(scores - lse_ref[0, :, head : head + 1])
            weights = chance.astype(BF16)
            grad_chance = dot(grad_rows, value, ((1,), (1,)))
            delta = jnp.sum(chance * grad_chance, -1, keepdims=True)
            grad_raw = (chance * (grad_chance - delta)).astype(BF16)
            turned_ref[:, head * HEAD_DIM : (head + 1) * HEAD_DIM] = dot(grad_raw, key)
            key_part = dot(grad_raw, query, ((0,), (0,)))
            value_part = dot(weights, grad_rows, ((0,), (0,)))
            grad_key = key_part if grad_key is None else grad_key + key_part
            grad_value = value_part if grad_value is None else grad_value + value_part
        turned_ref[:, key_at : key_at + HEAD_DIM] = grad_key * SCORE_SCALE
        dqkv_ref[micro, :, value_at : value_at + HEAD_DIM] = grad_value.astype(BF16)
    back = rotate_pairs(turned_ref[...], cos_ref[0], sin_ref[0], -1)
    dqkv_ref[micro, :, :rotated] = back.astype(BF16)
    rows = out_refs[0].shape[1]
    first = dot(dqkv_ref[micro], w_ref[...], ((1,), (1,)))
    for i, out_ref in enumerate(out_refs):
        out_ref[0] = first[i * rows : (i + 1) * rows, :].astype(BF16)
    x = x_ref[0].astype(F32)
    unit = x * lax.rsqrt(jnp.mean(x * x, -1, keepdims=True) + EPSILON)
    gain_ref[0:1, :] += jnp.sum(first * unit, 0, keepdims=True)

    @pl.when(micro == pl.num_programs(0) - 1)
    def _():
        def flat(ref):
            return ref[...].reshape(ref.shape[0] * ref.shape[1], ref.shape[2])

        dw = dot(flat(n1_ref), flat(dqkv_ref), ((0,), (0,))).astype(BF16)
        dwo = dot(flat(merged_ref), flat(ga_ref), ((0,), (0,))).astype(BF16)
        row = lax.broadcasted_iota(jnp.int32, (gain_ref.shape[0], LANES), 0)
        column = lax.broadcasted_iota(jnp.int32, (gain_ref.shape[0], LANES), 1)
        spread = jnp.where((row < 2) & (column == row + shape["gain_at"]), 1.0, 0.0)
        gains = lax.dot_general(
            gain_ref[...],
            spread,
            (((0,), (0,)), ((), ())),
            precision=lax.Precision.HIGHEST,
            preferred_element_type=F32,
        )
        ds = (gains + dot(n2_ref[...], logits_ref[...], ((0,), (0,)))).astype(BF16)
        if shape["whole"]:
            grads[0][...] = dw
            grads[1][...] = dwo
            grads[2][...] = ds
        else:
            dw_ref[...] = dw
            dwo_ref[...] = dwo
            ds_ref[...] = ds
            pack_rows, part, columns = shape["pack_rows"], shape["weight_rows"], shape["qkv_columns"]
            wide = shape["merged_columns"]
            for slot, grad_ref in enumerate(grads):
                spot = spots_ref[slot]
                at = pl.multiple_of(spot * pack_rows, pack_rows)
                grad_ref[:, :columns] = dw_ref[pl.ds(at, pack_rows), :]
                grad_ref[:, columns : columns + LANES] = ds_ref[pl.ds(at, pack_rows), :]
                at = pl.multiple_of(spot * part, part)
                for i in range(pack_rows // part):
                    grad_ref[i * part : (i + 1) * part, columns + LANES :] = dwo_ref[
                        pl.ds(at, part), i * wide : (i + 1) * wide
                    ]


def per_micro(shape):
    return pl.BlockSpec((1,) + tuple(shape[1:]), lambda m, s: (m,) + (0,) * (len(shape) - 1))


def fixed(shape):
    return pl.BlockSpec(tuple(shape), lambda m, s: (0,) * len(shape))


def attention_forward(shape, spots, packs, slots, cosine, sine, bias):
    micros, rows, width = slots[0].shape
    group = rows * len(slots)
    columns, merged = shape["qkv_columns"], shape["heads"] * HEAD_DIM
    outs = [jax.ShapeDtypeStruct((micros, rows, width), BF16) for _ in slots]
    specs = [per_micro(o.shape) for o in outs]
    more = [
        jax.ShapeDtypeStruct((micros, group, width), BF16),
        jax.ShapeDtypeStruct((micros, group, width), BF16),
        jax.ShapeDtypeStruct((width, LANES), BF16),
        jax.ShapeDtypeStruct((LANES // 2, width), F32),
        jax.ShapeDtypeStruct((micros, group, columns), BF16),
        jax.ShapeDtypeStruct((micros, group, merged), BF16),
        jax.ShapeDtypeStruct((micros, group, LANES), F32),
    ]
    specs += [fixed(o.shape) for o in more[:4]] + [per_micro(o.shape) for o in more[4:]]
    results = pl.pallas_call(
        functools.partial(attention_forward_kernel, shape),
        grid_spec=pltpu.PrefetchScalarGridSpec(
            num_scalar_prefetch=1,
            grid=(micros,),
            in_specs=[anywhere() for _ in packs + slots]
            + [per_micro(cosine.shape), per_micro(sine.shape), per_micro(bias.shape)],
            out_specs=specs,
            scratch_shapes=[
                pltpu.VMEM((width, columns), BF16),
                pltpu.VMEM((merged, width), BF16),
                pltpu.SemaphoreType.DMA((shape["copies"],)),
            ],
        ),
        out_shape=outs + more,
        name="attention_forward",
    )(spots, *packs, *slots, cosine, sine, bias)
    return (results[: len(slots)],) + tuple(results[len(slots) :])


def attention_backward(shape, spots, packs, slots, by_micro, at_once):
    micros, rows, width = slots[0].shape
    group = rows * len(slots)
    columns, merged_rows = shape["qkv_columns"], shape["heads"] * HEAD_DIM
    outs = [jax.ShapeDtypeStruct((micros, rows, width), BF16) for _ in slots]
    grads = [jax.ShapeDtypeStruct(pack.shape, BF16) for pack in packs]
    results = pl.pallas_call(
        functools.partial(attention_backward_kernel, shape),
        grid_spec=pltpu.PrefetchScalarGridSpec(
            num_scalar_prefetch=1,
            grid=(micros,),
            in_specs=[anywhere() for _ in packs + slots]
            + [per_micro(v.shape) for v in by_micro[:5]]
            + [fixed(v.shape) for v in at_once[:2]]
            + [per_micro(by_micro[5].shape)]
            + [fixed(v.shape) for v in at_once[2:]],
            out_specs=[per_micro(o.shape) for o in outs] + [fixed(g.shape) for g in grads],
            scratch_shapes=[
                pltpu.VMEM((micros, group, width), BF16),
                pltpu.VMEM((width, columns), BF16),
                pltpu.VMEM((merged_rows, width), BF16),
                pltpu.VMEM((micros, group, columns), BF16),
                pltpu.VMEM((group, (shape["heads"] + shape["kv_heads"]) * HEAD_DIM), F32),
                pltpu.VMEM((8, width), F32),
                pltpu.VMEM((width, columns), BF16),
                pltpu.VMEM((merged_rows, width), BF16),
                pltpu.VMEM((width, LANES), BF16),
                pltpu.SemaphoreType.DMA((shape["copies"],)),
            ],
        ),
        out_shape=outs + grads,
        name="attention_backward",
    )(spots, *packs, *slots, *by_micro[:5], *at_once[:2], by_micro[5], *at_once[2:])
    return list(results[: len(slots)]), list(results[len(slots) :])


def experts_kernel(shape, table_ref, *refs):
    slots, cores, ys, zs = shape["slots"], shape["cores"], shape["ys"], shape["zs"]
    own, hidden = shape["own"], shape["hidden"]
    x_slots, refs = refs[:slots], refs[slots:]
    beside, refs = refs[:slots], refs[slots:]
    gu_parts, refs = refs[: cores * ys], refs[cores * ys :]
    dn_parts, refs = refs[: cores * ys], refs[cores * ys :]
    wr_ref, gate_ref, x_out, gm_out = refs[:4]
    back_outs, refs = refs[4 : 4 + slots], refs[4 + slots :]
    mixed_outs, refs = refs[:slots], refs[slots:]
    act_outs, refs = refs[:cores], refs[cores:]
    dgu_outs, refs = refs[:cores], refs[cores:]
    x_ref, gm_ref, mask_ref, wgu_ref, wdn_ref, act_ref, dgu_ref, back_ref, mixed_ref = refs[:9]
    in_sems, out_sems = refs[9:]
    rows, width = x_slots[0].shape[0], x_ref.shape[1]
    part = width // (ys * zs)
    wide, tall = 2 * hidden * own, hidden * own
    local = cores * own

    fetched = [[] for _ in range(cores + 2)]
    for i in range(slots):
        at = pl.ds(i * rows, rows)
        first = width if shape["joined"][i] else 0
        fetched[0].append((x_slots[i].at[:, pl.ds(0, width)], x_ref.at[at, :]))
        fetched[cores].append((beside[i].at[:, pl.ds(first + width, LANES)], mask_ref.at[at, :]))
        fetched[cores + 1].append((beside[i].at[:, pl.ds(first, width)], gm_ref.at[at, :]))
    step = hidden // ys
    for c in range(cores):
        for s in range(ys):
            y = table_ref[local + s]
            for z in range(zs):
                at = pl.multiple_of((z * ys + y) * part, part)
                goal = wgu_ref.at[pl.ds(at, part), pl.ds(c * wide, wide)]
                fetched[c].append((gu_parts[c * ys + s].at[z], goal))
            for e in range(own):
                at = pl.multiple_of((c * own + e) * hidden + y * step, step)
                goal = wdn_ref.at[pl.ds(at, step), :]
                fetched[cores + 1].append((dn_parts[c * ys + s].at[e], goal))
    used = 0
    for group in fetched:
        for i, (source, goal) in enumerate(group):
            group[i] = pltpu.make_async_copy(source, goal, in_sems.at[used])
            group[i].start()
            used += 1

    def arrive(group):
        for copy in fetched[group]:
            copy.wait()

    leaving = []

    def leave(source, goal):
        leaving.append(pltpu.make_async_copy(source, goal, out_sems.at[len(leaving)]))
        leaving[-1].start()

    pre = []
    for c in range(cores):
        arrive(c)
        if c == 0:
            leave(x_ref, x_out)
        pre.append(dot(x_ref[...], wgu_ref[:, c * wide : (c + 1) * wide]))
    arrive(cores)
    total = slots * rows
    lane = lax.broadcasted_iota(jnp.int32, (total, LANES), 1)
    named = mask_ref[...].astype(F32) > 0.5
    logits = jnp.where(named, dot(x_ref[...], wr_ref[...]), NEGATIVE)
    highest = jnp.max(logits, -1, keepdims=True)
    exponent = jnp.where(named, jnp.exp(logits - highest), 0.0)
    gates = exponent / jnp.sum(exponent, -1, keepdims=True)
    gate_ref[...] = gates
    arrive(cores + 1)
    leave(gm_ref, gm_out)
    grad_act = dot(gm_ref[...], wdn_ref[...], ((1,), (1,)))
    picked = jnp.zeros((total, LANES), F32)
    for c in range(cores):
        for e in range(own):
            j = c * own + e
            mine = lane == table_ref[j]
            gate = jnp.sum(jnp.where(mine, gates, 0.0), -1, keepdims=True)
            base = 2 * hidden * e
            gate_pre = pre[c][:, base : base + hidden]
            up_pre = pre[c][:, base + hidden : base + 2 * hidden]
            grad_one = grad_act[:, j * hidden : (j + 1) * hidden]
            sig = jax.nn.sigmoid(gate_pre)
            silu = gate_pre * sig
            activated = (silu * up_pre).astype(BF16).astype(F32)
            found = jnp.sum(activated * grad_one, -1, keepdims=True)
            picked = jnp.where(mine, found, picked)
            act_ref[c, :, e * hidden : (e + 1) * hidden] = (activated * gate).astype(BF16)
            grad_one = grad_one * gate
            base = 2 * hidden * j
            dgu_ref[:, base : base + hidden] = (
                grad_one * up_pre * sig * (1.0 + gate_pre * (1.0 - sig))
            ).astype(BF16)
            dgu_ref[:, base + hidden : base + 2 * hidden] = (grad_one * silu).astype(BF16)
        leave(dgu_ref.at[:, pl.ds(c * wide, wide)], dgu_outs[c])
        leave(act_ref.at[c], act_outs[c])

    coarse = picked.astype(BF16)
    back_ref[:, width : width + LANES] = coarse
    back_ref[:, width + LANES :] = (picked - coarse.astype(F32)).astype(BF16)
    back_ref[:, :width] = dot(dgu_ref[...], wgu_ref[...], ((1,), (1,))).astype(BF16)

    def leave_slots(source, goals):
        for i in range(slots):
            leave(source.at[pl.ds(i * rows, rows), :], goals[i])

    leave_slots(back_ref, back_outs)
    if tall % LANES == 0:
        acts = jnp.concatenate([act_ref[c] for c in range(cores)], 1)
        mixed = dot(acts, wdn_ref[...])
    else:
        mixed = sum(dot(act_ref[c], wdn_ref[c * tall : (c + 1) * tall, :]) for c in range(cores))
    mixed_ref[...] = mixed.astype(BF16)
    leave_slots(mixed_ref, mixed_outs)
    for copy in leaving:
        copy.wait()


def run_experts(shape, table, x_slots, beside, gu_parts, dn_parts, wr):
    rows, width = x_slots[0].shape[0], wr.shape[0]
    total = rows * len(x_slots)
    cores, own, hidden = shape["cores"], shape["own"], shape["hidden"]
    outs = [
        jax.ShapeDtypeStruct((total, LANES), F32),
        jax.ShapeDtypeStruct((total, width), BF16),
        jax.ShapeDtypeStruct((total, width), BF16),
    ]
    outs += [jax.ShapeDtypeStruct((rows, width + 2 * LANES), BF16) for _ in x_slots]
    outs += [jax.ShapeDtypeStruct((rows, width), BF16) for _ in x_slots]
    outs += [jax.ShapeDtypeStruct((total, own * hidden), BF16) for _ in range(cores)]
    outs += [jax.ShapeDtypeStruct((total, 2 * own * hidden), BF16) for _ in range(cores)]
    joined = [slot.shape[1] > width for slot in x_slots]
    shape = dict(shape, slots=len(x_slots), joined=joined)
    copies = 3 * len(x_slots) + cores * shape["ys"] * (shape["zs"] + own)
    operands = x_slots + beside + gu_parts + dn_parts
    return pl.pallas_call(
        functools.partial(experts_kernel, shape),
        in_specs=[pl.BlockSpec(memory_space=pltpu.SMEM)] + [anywhere() for _ in operands] + [on_chip()],
        out_specs=[on_chip()] + [anywhere() for _ in outs[1:]],
        out_shape=outs,
        scratch_shapes=[
            pltpu.VMEM((total, width), BF16),
            pltpu.VMEM((total, width), BF16),
            pltpu.VMEM((total, LANES), BF16),
            pltpu.VMEM((width, cores * own * 2 * hidden), BF16),
            pltpu.VMEM((cores * own * hidden, width), BF16),
            pltpu.VMEM((cores, total, own * hidden), BF16),
            pltpu.VMEM((total, cores * own * 2 * hidden), BF16),
            pltpu.VMEM((total, width + 2 * LANES), BF16),
            pltpu.VMEM((total, width), BF16),
            pltpu.SemaphoreType.DMA((copies,)),
            pltpu.SemaphoreType.DMA((2 + 2 * cores + 2 * len(x_slots),)),
        ],
        compiler_params=pltpu.CompilerParams(vmem_limit_bytes=60 << 20),
        name="experts",
    )(table, *operands, wr)


def pack_kernel(hidden, gate_ref, up_ref, out_ref):
    for z in range(out_ref.shape[0]):
        out_ref[z, :, :hidden] = gate_ref[0, :, z * hidden : (z + 1) * hidden]
        out_ref[z, :, hidden:] = up_ref[0, :, z * hidden : (z + 1) * hidden]


def pack_experts(w_gate, w_up, zs):
    own, part, hidden_all = w_gate.shape
    hidden = hidden_all // zs
    return pl.pallas_call(
        functools.partial(pack_kernel, hidden),
        grid=(own,),
        in_specs=[pl.BlockSpec((1, part, hidden_all), lambda e: (e, 0, 0))] * 2,
        out_specs=pl.BlockSpec((zs, part, 2 * hidden), lambda e: (0, 0, e)),
        out_shape=jax.ShapeDtypeStruct((zs, part, own * 2 * hidden), BF16),
        name="pack_experts",
    )(w_gate, w_up)


def unpack_kernel(hidden, in_ref, gate_ref, up_ref):
    for z in range(in_ref.shape[0]):
        gate_ref[0, :, z * hidden : (z + 1) * hidden] = in_ref[z, :, :hidden].astype(F32)
        up_ref[0, :, z * hidden : (z + 1) * hidden] = in_ref[z, :, hidden:].astype(F32)


def unpack_experts(packed, own):
    zs, part, wide = packed.shape
    hidden = wide // own // 2
    out = jax.ShapeDtypeStruct((own, part, zs * hidden), F32)
    return pl.pallas_call(
        functools.partial(unpack_kernel, hidden),
        grid=(own,),
        in_specs=[pl.BlockSpec((zs, part, 2 * hidden), lambda e: (0, 0, e))],
        out_specs=[pl.BlockSpec((1, part, zs * hidden), lambda e: (e, 0, 0))] * 2,
        out_shape=[out, out],
        name="unpack_experts",
    )(packed)


def per_device(
    tokens,
    cotangent,
    attn_gain,
    mlp_gain,
    w_query,
    w_key,
    w_value,
    w_out,
    w_router,
    w_gate,
    w_up,
    w_down,
    shuffle,
    routes,
    lengths,
):
    micros, rows, width = tokens.shape
    dp_count, members = lax.axis_size("dp"), lax.axis_size("expert")
    devices = dp_count * members
    rings = Rings(dp_count, members)
    zn, yn, xn, cn = rings.z, rings.y, rings.x, rings.core
    group_rows = rows * members
    experts_all = w_router.shape[1]
    own_experts, model_part, hidden_all = w_gate.shape
    hidden_part = hidden_all // zn
    heads, kv_heads = HEADS // members, KV_HEADS // members
    weight_rows = w_query.shape[0]
    home_rows = micros * rows

    phases = Phases()

    def over_members(value):
        return phases.start(rings.gather_two(value, "c", "x"))

    def sum_members(parts):
        parts = [[parts[s * cn + t] for s in range(xn)] for t in range(cn)]
        return phases.start(rings.reduce_two(parts, "x", "c"))

    def line(columns):
        return [slot for column in columns for slot in column]

    def by_member(w):
        return w.reshape(weight_rows, members, w.shape[1] // members)

    small = jnp.concatenate([w_router, attn_gain[:, None], mlp_gain[:, None]], 1)
    small = jnp.pad(small, ((0, 0), (0, LANES - experts_all - 2)))
    small = jnp.broadcast_to(small[:, None, :], (weight_rows, members, LANES))
    mine = jnp.concatenate([by_member(w_query), by_member(w_key), by_member(w_value), small], 2)
    mine = lax.all_to_all(mine.transpose(1, 0, 2), "expert", 0, 0)
    small_at = mine.shape[2]
    qkv_columns = small_at - LANES
    pack_rows = members * weight_rows
    mine = mine.reshape(pack_rows, small_at)
    to_heads = [(s, (s % dp_count) * members + s // dp_count) for s in range(devices)]
    to_home = [(t, s) for s, t in to_heads]
    out_mine = lax.ppermute(w_out, ALL, to_heads)
    weights_started = []
    group_tokens = phases.start(paced(rings.gather_two(tokens, "c", "x"), weights_started))
    gate_up = pack_experts(w_gate, w_up, zn)
    begun = phases.start(make(lambda: (mine, gate_up, out_mine, routes)))
    phases.phase()
    (mine, gate_up, out_mine, routes) = begun.result
    merged_columns = width // members
    pack = jnp.concatenate(
        [out_mine[:, i * merged_columns : (i + 1) * merged_columns] for i in range(members)], 0
    )
    pack = jnp.concatenate([mine, pack], 1)
    whole = weight_rows % 16 != 0
    attention_shape = {
        "heads": heads,
        "kv_heads": kv_heads,
        "whole": whole,
        "pack_rows": pack_rows,
        "weight_rows": weight_rows,
        "qkv_columns": qkv_columns,
        "merged_columns": merged_columns,
        "slots": members,
        "gain_at": experts_all,
        "packs": 3 if whole else dp_count,
        "copies": micros * members + (3 if whole else dp_count * (2 + members)),
    }
    def beside_started(value):
        column = rings.gather(value, "x")
        ahead = [rings.step(value, "z")] if zn > 1 else []
        tied = yield ahead + column[1:]
        return [column[0]] + tied[len(ahead) :], tied[0]

    inputs = tokens.astype(F32)
    inv_first = lax.rsqrt(jnp.mean(inputs * inputs, -1, keepdims=True) + EPSILON)
    unit_first = inputs * inv_first

    pack, routes, w_down = tie(pack, routes, w_down)
    packs = phases.start(rings.gather_two(pack, "z", "y"))
    weights_started.append(True)
    phases.phase()
    dealt = lax.all_to_all(
        routes.reshape(micros, dp_count, rows // dp_count, routes.shape[2]), "dp", 1, 1
    ).reshape(micros, rows, routes.shape[2])
    held = phases.start(make(lambda: dealt))
    phases.phase()
    dealt = held.result
    lane_ids = jnp.arange(LANES, dtype=jnp.int32)
    hot = jnp.sum((dealt[:, :, :, None] == lane_ids).astype(F32), 2).astype(BF16)
    place = (shuffle[:, 0, :, None] == jnp.arange(rows, dtype=jnp.int32)).astype(BF16)
    named = jnp.einsum("mir,mix->mrx", place, hot, preferred_element_type=F32).astype(BF16)

    grad_result = cotangent.astype(F32)
    grad_moe = (RESIDUAL_SCALE * grad_result).astype(BF16)
    beside = jnp.concatenate([grad_moe, named], 2).reshape(home_rows, width + LANES)

    row_at = jnp.concatenate(
        [
            (rings.origin("x", s) * cn + rings.origin("c", t)) * rows
            + jnp.arange(rows, dtype=jnp.int32)
            for s in range(xn)
            for t in range(cn)
        ]
    )
    row_at, dealt = tie(row_at, dealt)
    half = HEAD_DIM // 2
    lane = jnp.arange(LANES, dtype=jnp.int32)
    inverse = ROPE_BASE ** (-((lane % half).astype(F32) * 2.0) / HEAD_DIM)
    sign = jnp.where(lane % HEAD_DIM < half, -1.0, 1.0)
    doc_lengths = lengths[:, 0]
    doc_ends = jnp.cumsum(doc_lengths, 1)
    doc_starts = doc_ends - doc_lengths
    segment = jnp.sum((row_at[None, :, None] >= doc_ends[:, None, :]).astype(jnp.int32), 2)
    docs = jnp.arange(doc_lengths.shape[1], dtype=jnp.int32)
    start = jnp.sum(jnp.where(segment[:, :, None] == docs, doc_starts[:, None, :], 0), 2)
    position = row_at[None, :] - start
    angles = position.astype(F32)[:, :, None] * inverse
    cosine, sine = jnp.cos(angles), jnp.sin(angles) * sign
    allowed = segment[:, :, None] == segment[:, None, :]
    bias = jnp.where(allowed & (row_at[None, :] <= row_at[:, None]), 0.0, NEGATIVE)

    tables = phases.start(make(lambda: (cosine, sine, bias, beside, gate_up, w_down)))
    phases.phase()
    cosine, sine, bias, beside, gate_up, w_down = tables.result
    beside = phases.start(beside_started(beside))
    gate_up = lax.all_to_all(gate_up, "dp", 0, 0, axis_index_groups=rings.z_groups)
    held = phases.start(make(lambda: w_down))
    packs, group_tokens = phases.finish(packs, group_tokens)
    w_down = held.result
    spots = jnp.stack(
        [rings.origin("z", t) * yn + rings.origin("y", s) for s in range(yn) for t in range(zn)]
    )
    if whole:
        packs = [in_order(column, rings.at["z"], zn) for column in packs]
        packs = [in_order([packs[s][z] for s in range(yn)], rings.at["y"], yn) for z in range(zn)]
        packs = jnp.stack([packs[z][y] for z in range(zn) for y in range(yn)])
        w_merge = packs[:, :, small_at:].reshape(dp_count, members, weight_rows, merged_columns)
        w_merge = w_merge.transpose(0, 2, 1, 3).reshape(dp_count * weight_rows, width)
        w_small = packs[:, :, qkv_columns:small_at].reshape(width, LANES)
        packs = [packs[:, :, :qkv_columns].reshape(width, qkv_columns), w_merge, w_small]
    else:
        packs = line(packs)

    down = rings.gather(w_down, "y")
    attention = phases.start(
        make(
            attention_forward,
            attention_shape,
            spots,
            packs,
            line(group_tokens),
            cosine,
            sine,
            bias,
        )
    )
    down_task = phases.start(make(lambda: down))
    phases.finish(attention)
    down = phases.start(make(lambda: [rings.gather(part, "c") for part in down_task.result]))
    attn_parts, group_in, n1, router_columns, small_rows, qkv, merged, lse = attention.result
    gain_first = small_rows[experts_all]
    gain_second = small_rows[experts_all + 1]
    attended = sum_members(attn_parts)
    for _ in range(xn - 1):
        phases.phase()
    gate_up = phases.start(make(lambda: gate_up))
    attended, down, gate_up = phases.finish(attended, down, gate_up)
    hidden = inputs + RESIDUAL_SCALE * attended
    inv_second = lax.rsqrt(jnp.mean(hidden * hidden, -1, keepdims=True) + EPSILON)
    unit_second = hidden * inv_second
    normed_second = (unit_second * gain_second).astype(BF16).reshape(home_rows, width)

    if zn > 1:
        first = phases.start(make(lambda: [rings.step(normed_second, "z")] + rings.gather(normed_second, "x")))
        phases.finish(first)
        passed, *column = first.result
        together = jnp.concatenate([passed, beside.result[1]], 1)
        group = phases.start(rings.gather_two(together, "z", "x", zn - 1))
    else:
        first = phases.start(make(lambda: rings.gather(normed_second, "x")))
        phases.finish(first)
        column, group = first.result, None
    gate_up = rings.gather(gate_up, "y")
    if group is not None:
        phases.phase()
        phases.phase()
    mine_too = phases.start(make(lambda: rings.gather(gate_up[0], "c")))
    gate_up = phases.start(make(lambda: gate_up[1:]))
    phases.finish(mine_too, gate_up, *([] if group is None else [group]))
    gate_up = [mine_too.result] + [rings.gather(part, "c") for part in gate_up.result]
    later = [[] for _ in range(xn)] if group is None else group.result
    group_x = [[column[i]] + later[i] for i in range(xn)]
    beside = [[beside.result[0][i]] + later[i] for i in range(xn)]
    gu_parts = [gate_up[s][c] for c in range(cn) for s in range(yn)]
    dn_parts = [down[s][c] for c in range(cn) for s in range(yn)]

    slots = [(s, t) for s in range(xn) for t in range(zn)]
    x_slots = [group_x[s][t] for s, t in slots]
    beside = [beside[s][t] for s, t in slots]
    chunk = min(len(slots), 8)
    chunks = len(slots) // chunk
    table = [
        (rings.at["x"] * cn + rings.origin("c", s)) * own_experts
        + jnp.arange(own_experts, dtype=jnp.int32)
        for s in range(cn)
    ]
    table.append(jnp.stack([rings.origin("y", s) for s in range(yn)]))
    table = jnp.concatenate(table)
    experts_shape = {"cores": cn, "ys": yn, "zs": zn, "own": own_experts, "hidden": hidden_part}
    results = [
        run_experts(
            experts_shape,
            table,
            x_slots[i * chunk : (i + 1) * chunk],
            beside[i * chunk : (i + 1) * chunk],
            gu_parts,
            dn_parts,
            router_columns,
        )
        for i in range(chunks)
    ]
    back = [part for pieces in results for part in pieces[3 : 3 + chunk]]
    mixed = [part for pieces in results for part in pieces[3 + chunk : 3 + 2 * chunk]]
    results = [pieces[:3] + pieces[3 + 2 * chunk :] for pieces in results]
    results = [pieces[0] if chunks == 1 else jnp.concatenate(pieces, 0) for pieces in zip(*results)]
    gates, x_all, gm_all = results[:3]
    acts, dgus = results[3 : 3 + cn], results[3 + cn :]
    back = [back[i * zn : (i + 1) * zn] for i in range(xn)]
    mixed = [mixed[i * zn : (i + 1) * zn] for i in range(xn)]

    def by_y(value, axis):
        return [lax.dynamic_index_in_dim(value, rings.origin("y", s), axis, False) for s in range(yn)]

    def product(core, kind, x, gm, coming):
        if kind == 0:
            term = dot(x, dgus[core], ((0,), (0,)))
        else:
            term = dot(acts[core], gm, ((0,), (0,)))
        return (term if coming is None else term + coming.astype(F32)).astype(BF16)

    def own_gu(x, coming):
        return by_y(product(0, 0, x, None, coming).reshape(zn, yn, model_part, -1), 1)

    def own_dn(gm, coming):
        value = product(0, 1, None, gm, coming)
        return by_y(value.reshape(own_experts, yn, hidden_part // yn, width), 1)

    def held(*values):
        return phases.start(make(lambda: values))

    rows_back = phases.start(rings.reduce_two(back, "z", "x", two_part))
    x, gm, coming = x_all, gm_all, [None, None]
    if cn > 1:
        work = held(product(1, 0, x, None, None), x, gm)
        phases.phase()
        other, x, gm = work.result
        coming[0] = rings.step(other, "c")
    first = min(1, zn - 1)
    other = [product(1, 1, None, gm, None)] if cn > 1 else []
    work = held(own_gu(x, coming[0]), other, gm, [row[first] for row in mixed])
    phases.phase()
    made, other, gm, mixed_first = work.result
    if cn > 1:
        coming[1] = rings.step(other[0], "c")
    groups = [(0, 2), (2, 4), (4, 5)] if own_experts == 5 else [(0, own_experts)]
    wide = 2 * hidden_part
    waiting = [[part[:, :, low * wide : high * wide] for part in made] for low, high in groups]
    grad_gu = []

    def next_group(*keep):
        nonlocal waiting
        if waiting:
            grad_gu.append(phases.start(rings.reduce(waiting[0], "y")))
            waiting = waiting[1:]
        work = held(waiting, *keep)
        phases.phase()
        waiting, *keep = work.result
        return keep

    for row, value in zip(mixed, mixed_first):
        row[first] = value
    moe_rows = phases.start(rings.reduce_two(mixed, "z", "x"))
    (gm, *coming) = next_group(gm, *([coming[1]] if cn > 1 else []))
    (grad_dn,) = next_group(own_dn(gm, coming[0] if coming else None))
    phases.finish(rows_back)
    grad_dealt = rows_back.result[:, :width]
    grad_gates = rows_back.result[:, width:]
    grad_gates = grad_gates[:, :LANES] + grad_gates[:, LANES:]
    own_gates = gates[:home_rows]
    grad_picked = own_gates * (grad_gates - jnp.sum(own_gates * grad_gates, -1, keepdims=True))
    grad_logits = grad_picked.astype(BF16)
    router_rows = small_rows.astype(BF16)
    grad_dealt = (grad_dealt + dot(grad_logits[:, : LANES // 2], router_rows)).astype(BF16)
    grad_normed_second = grad_dealt.astype(F32).reshape(micros, rows, width)
    scaled_second = grad_normed_second * gain_second
    grad_hidden = grad_result + inv_second * (
        scaled_second - unit_second * jnp.mean(scaled_second * unit_second, -1, keepdims=True)
    )
    mlp_gain_grad = jnp.sum(grad_normed_second * unit_second, (0, 1))[None]
    grad_attn = (RESIDUAL_SCALE * grad_hidden).astype(BF16)

    grad_attn = over_members(grad_attn)
    while waiting:
        next_group()
    grad_gu = jnp.concatenate([part.astype(BF16) for part in phases.finish(*grad_gu)], 2)
    work = held(grad_gu, grad_dn)
    phases.finish(grad_attn, moe_rows, work)
    grad_gu, grad_dn = work.result
    grad_gu = lax.all_to_all(grad_gu, "dp", 0, 0, axis_index_groups=rings.z_groups)
    grad_dn = phases.start(rings.reduce(grad_dn, "y"))

    attention = phases.start(
        make(
            attention_backward,
            attention_shape,
            spots,
            packs,
            line(grad_attn.result),
            [cosine, sine, bias, qkv, lse, group_in],
            [n1, merged, normed_second, grad_logits, mlp_gain_grad],
        )
    )
    phases.finish(attention)
    first_parts, weight_grads = attention.result

    if whole:
        grad_qkv, grad_out, grad_small = weight_grads
        grad_out = grad_out.reshape(dp_count, weight_rows, members, merged_columns).transpose(0, 2, 1, 3)
        both = jnp.concatenate(
            [
                grad_qkv.reshape(dp_count, pack_rows, qkv_columns),
                grad_small.reshape(dp_count, pack_rows, LANES),
                grad_out.reshape(dp_count, pack_rows, merged_columns),
            ],
            2,
        )
        weight_grads = [
            lax.dynamic_index_in_dim(both, spots[i], 0, False) for i in range(dp_count)
        ]
    both = phases.start(
        rings.reduce_two([[weight_grads[s * zn + t] for t in range(zn)] for s in range(yn)], "z", "y")
    )
    phases.phase()
    grad_gu = held(grad_gu)
    grad_normed_first = sum_members(first_parts)
    both, grad_gu, grad_dn, grad_normed_first, moe_rows = phases.finish(
        both, grad_gu, grad_dn, grad_normed_first, moe_rows
    )
    grad_gate, grad_up = unpack_experts(grad_gu[0], own_experts)
    moe_rows = moe_rows.astype(BF16).reshape(micros, rows, width)
    output = (hidden + RESIDUAL_SCALE * moe_rows.astype(F32)).astype(BF16)
    scaled_first = grad_normed_first * gain_first
    grad_tokens = grad_hidden + inv_first * (
        scaled_first - unit_first * jnp.mean(scaled_first * unit_first, -1, keepdims=True)
    )
    grad_out = [
        both[i * weight_rows : (i + 1) * weight_rows, small_at:] for i in range(members)
    ]
    grad_out = lax.ppermute(jnp.concatenate(grad_out, 1).astype(BF16), ALL, to_home).astype(F32)
    home = both[:, :small_at].reshape(members, weight_rows, small_at)
    home = lax.all_to_all(home.astype(BF16), "expert", 0, 0).astype(F32)

    def columns(start, count):
        return jnp.concatenate([home[i, :, start : start + count] for i in range(members)], 1)

    query_columns, key_columns = heads * HEAD_DIM, kv_heads * HEAD_DIM
    grad_query = columns(0, query_columns)
    grad_key = columns(query_columns, key_columns)
    grad_value = columns(query_columns + key_columns, key_columns)

    small = jnp.sum(home[:, :, qkv_columns:], 0)
    grad_w_router = small[:, :experts_all]
    grad_attn_gain, grad_mlp_gain = small[:, experts_all], small[:, experts_all + 1]

    return (
        output,
        grad_tokens,
        grad_attn_gain,
        grad_mlp_gain,
        grad_query,
        grad_key,
        grad_value,
        grad_out,
        grad_w_router,
        grad_gate,
        grad_up,
        grad_dn,
    )


def solution(mesh):
    rows = P(None, ALL, None)
    placed = (rows, rows, P(ALL), P(ALL)) + (P(ALL, None),) * 5
    placed += (P("expert", "dp", None),) * 3 + (rows, rows, P(None, "dp", None))
    results = (rows, rows, P(ALL), P(ALL)) + (P(ALL, None),) * 5
    results += (P("expert", "dp", None),) * 3
    return jax.shard_map(per_device, mesh=mesh, in_specs=placed, out_specs=results, check_vma=False)
```

```python
import functools

import jax
import jax.numpy as jnp
from jax import lax
from jax.experimental import pallas as pl
from jax.experimental.pallas import tpu as pltpu
from jax.sharding import PartitionSpec as P

HEADS = 24
KV_HEADS = 8
HEAD_DIM = 64

EPSILON = 1e-06
ROPE_BASE = 10000.0
RESIDUAL_SCALE = 0.22
SCORE_SCALE = 1.0 / 64.0
NEGATIVE = -1e30
LANES = 128

BF16 = jnp.bfloat16
F32 = jnp.float32
ALL = ("dp", "expert")


def dot(a, b, dims=((1,), (0,))):
    return lax.dot_general(a, b, (dims, ((), ())), preferred_element_type=F32)


class Rings:
    def __init__(self, dp_count, expert_count):
        y_count = 1
        while dp_count % (2 * y_count) == 0 and 8 * y_count * y_count <= dp_count:
            y_count *= 2
        self.y, self.z = y_count, dp_count // y_count
        self.core = 2 if expert_count % 2 == 0 else 1
        self.x = expert_count // self.core
        zs, ys, xs, cs = range(self.z), range(self.y), range(self.x), range(self.core)
        self.z_groups = [[z * self.y + y for z in zs] for y in ys]
        self.token_groups = [
            [(z * self.y + y) * expert_count + x * self.core + c for z in zs for x in xs]
            for y in ys
            for c in cs
        ]
        self.table = {
            "z": ("dp", self.z, [(z * self.y + y, (z + 1) % self.z * self.y + y) for z in zs for y in ys]),
            "y": ("dp", self.y, [(z * self.y + y, z * self.y + (y + 1) % self.y) for z in zs for y in ys]),
            "x": (
                "expert",
                self.x,
                [(x * self.core + c, (x + 1) % self.x * self.core + c) for x in xs for c in cs],
            ),
            "c": (
                "expert",
                self.core,
                [(x * self.core + c, x * self.core + (c + 1) % self.core) for x in xs for c in cs],
            ),
        }
        d, e = lax.axis_index("dp"), lax.axis_index("expert")
        self.at = {"z": d // self.y, "y": d % self.y, "x": e // self.core, "c": e % self.core}

    def count(self, ring):
        return self.table[ring][1]

    def step(self, value, ring):
        axis, _, pairs = self.table[ring]
        return lax.ppermute(value, axis, pairs)

    def origin(self, ring, slot):
        return lax.rem(self.at[ring] + (self.count(ring) - slot), self.count(ring))

    def gather(self, value, ring):
        slots = [value]
        for _ in range(1, self.count(ring)):
            slots.append(self.step(slots[-1], ring))
        return slots

    def send(self, terms, ring, wire=None):
        running = None
        for term in terms[1:]:
            if running is None:
                term = term.astype(BF16)
            else:
                term = term.astype(F32) + running.astype(F32)
                term = term.astype(BF16) if wire is None else wire(term)
            running = self.step(term, ring)
        return running


    def gather_two(self, value, first, second, count=None):
        columns, slot = [], value
        count = self.count(first) if count is None else count
        for t in range(count):
            column = self.gather(slot, second)
            ahead = [self.step(slot, first)] if t + 1 < count else []
            tied = yield ahead + column[1:]
            columns.append([column[0]] + tied[len(ahead) :])
            slot = tied[0]
        return [[column[s] for column in columns] for s in range(self.count(second))]

    def reduce(self, parts, ring):
        running = self.send(parts, ring)
        own = parts[0]
        if running is not None:
            own, running = yield [own, running]
        return own.astype(F32) if running is None else own.astype(F32) + running.astype(F32)

    def reduce_two(self, parts, first, second, wire=None):
        count = self.count(first)
        parts = [list(row) for row in parts]
        arrived, running = {}, None
        order = list(range(1, count)) + [0]
        for phase in range(count + (count > 1)):
            made = []
            if phase > 0:
                t = order[phase - 1]
                term = self.partial(parts, arrived, t)
                if running is not None:
                    term = term + running.astype(F32)
                made.append(self.step(term.astype(BF16) if wire is None else wire(term), first))
            if phase < count:
                passing = self.send([row[order[phase]] for row in parts], second, wire)
                if passing is not None:
                    made.append(passing)
            after = [row[order[phase + 1]] for row in parts] if phase + 1 < count else []
            tied = yield made + after
            if after:
                for row, value in zip(parts, tied[len(made) :]):
                    row[order[phase + 1]] = value
            if phase < count and passing is not None:
                arrived[order[phase]] = tied[len(made) - 1]
            if phase > 0:
                running = tied[0]
            if phase == count - 1 and count > 1:
                break
        own = self.partial(parts, arrived, 0)
        return own if running is None else own + running.astype(F32)

    def partial(self, parts, arrived, t):
        own = parts[0][t].astype(F32)
        return own if t not in arrived else own + arrived[t].astype(F32)


def two_part(term):
    width = term.shape[1] - 2 * LANES
    value = term[:, width : width + LANES] + term[:, width + LANES :]
    coarse = value.astype(BF16)
    fine = (value - coarse.astype(F32)).astype(BF16)
    return jnp.concatenate([term[:, :width].astype(BF16), coarse, fine], 1)


class Task:
    def __init__(self, steps):
        self.steps, self.made, self.result, self.done = steps, [], None, False
        self.advance(None)

    def advance(self, values):
        try:
            self.made = list(self.steps.send(values))
        except StopIteration as stop:
            self.result, self.done, self.made = stop.value, True, []


class Phases:
    def __init__(self):
        self.tasks = []

    def start(self, steps):
        task = Task(steps)
        self.tasks.append(task)
        return task

    def phase(self):
        self.tasks = [task for task in self.tasks if not task.done]
        made = [value for task in self.tasks for value in task.made]
        tied = list(tie(*made)) if made else []
        for task in self.tasks:
            count = len(task.made)
            values, tied = tied[:count], tied[count:]
            task.advance(values)

    def finish(self, *tasks):
        while not all(task.done for task in tasks):
            self.phase()
        return [task.result for task in tasks]


def resumed(steps, made):
    while True:
        made = yield made
        try:
            made = steps.send(made)
        except StopIteration as stop:
            return stop.value


def paced(steps, ready):
    made = next(steps)
    while True:
        tied = yield made
        while not ready:
            tied = yield tied
        try:
            made = steps.send(tied)
        except StopIteration as stop:
            return stop.value


def make(function, *arguments):
    flat, tree = jax.tree.flatten(function(*arguments))
    flat = yield flat
    return jax.tree.unflatten(tree, flat)


def tie(*values):
    return lax.optimization_barrier(values)


def in_order(slots, position_of, count):
    stacked = jnp.stack(slots)
    return [
        lax.dynamic_index_in_dim(stacked, lax.rem(position_of + (count - i), count), 0, False)
        for i in range(count)
    ]


def fetch(copies, semaphores):
    started = [pltpu.make_async_copy(a, b, semaphores.at[i]) for i, (a, b) in enumerate(copies)]
    for copy in started:
        copy.start()
    for copy in started:
        copy.wait()


def anywhere():
    return pl.BlockSpec(memory_space=pl.ANY)


def on_chip():
    return pl.BlockSpec(memory_space=pltpu.VMEM)


def rotate_pairs(values, cosine, sine, direction):
    lane = lax.broadcasted_iota(jnp.int32, (values.shape[0], LANES), 1)
    low = (lane & (HEAD_DIM - 1)) < HEAD_DIM // 2
    pieces = []
    for start in range(0, values.shape[1], LANES):
        piece = values[:, start : start + LANES]
        partner = jnp.where(
            low,
            pltpu.roll(piece, LANES - HEAD_DIM // 2, 1),
            pltpu.roll(piece, HEAD_DIM // 2, 1),
        )
        turned = partner * sine
        pieces.append(piece * cosine + turned if direction > 0 else piece * cosine - turned)
    return jnp.concatenate(pieces, 1)


def weight_copies(shape, spots_ref, packs, w_ref, wo_ref, small_ref=None):
    if shape["whole"]:
        copies = [(packs[0], w_ref), (packs[1], wo_ref)]
        return copies if small_ref is None else copies + [(packs[2], small_ref)]
    copies = []
    rows, part, columns = shape["pack_rows"], shape["weight_rows"], shape["qkv_columns"]
    wide = shape["merged_columns"]
    for slot, pack in enumerate(packs):
        spot = spots_ref[slot]
        at = pl.multiple_of(spot * rows, rows)
        copies.append((pack.at[:, pl.ds(0, columns)], w_ref.at[pl.ds(at, rows), :]))
        if small_ref is not None:
            copies.append((pack.at[:, pl.ds(columns, LANES)], small_ref.at[pl.ds(at, rows), :]))
        at = pl.multiple_of(spot * part, part)
        for i in range(rows // part):
            copies.append(
                (
                    pack.at[pl.ds(i * part, part), pl.ds(columns + LANES, wide)],
                    wo_ref.at[pl.ds(at, part), pl.ds(i * wide, wide)],
                )
            )
    return copies


def row_copies(slots, into_ref):
    micros, rows, _ = slots[0].shape
    return [
        (slot.at[m], into_ref.at[m, pl.ds(i * rows, rows), :])
        for i, slot in enumerate(slots)
        for m in range(micros)
    ]


def attention_forward_kernel(shape, spots_ref, *refs):
    packs, refs = refs[: shape["packs"]], refs[shape["packs"] :]
    slots, refs = refs[: shape["slots"]], refs[shape["slots"] :]
    cos_ref, sin_ref, bias_ref = refs[:3]
    out_refs, refs = refs[3 : 3 + shape["slots"]], refs[3 + shape["slots"] :]
    x_ref, n1_ref, small_ref, rows_ref, qkv_ref, merged_ref, lse_ref = refs[:7]
    w_ref, wo_ref, semaphores = refs[7:]
    heads, kv_heads = shape["heads"], shape["kv_heads"]
    share = heads // kv_heads
    rotated = (heads + kv_heads) * HEAD_DIM
    micro = pl.program_id(0)

    @pl.when(micro == 0)
    def _():
        copies = weight_copies(shape, spots_ref, packs, w_ref, wo_ref, small_ref)
        fetch(row_copies(slots, x_ref) + copies, semaphores)
        count = rows_ref.shape[0]
        row = lax.broadcasted_iota(jnp.int32, (count, LANES), 0)
        column = lax.broadcasted_iota(jnp.int32, (count, LANES), 1)
        same = jnp.where(row == column, 1.0, 0.0).astype(BF16)
        rows_ref[...] = dot(same, small_ref[...], ((1,), (1,)))

    x = x_ref[micro].astype(F32)
    inverse = lax.rsqrt(jnp.mean(x * x, -1, keepdims=True) + EPSILON)
    at = shape["gain_at"]
    n1_ref[micro] = (x * inverse * rows_ref[at : at + 1, :]).astype(BF16)
    pre = dot(n1_ref[micro], w_ref[...])
    turned = rotate_pairs(pre[:, :rotated], cos_ref[0], sin_ref[0], 1)
    qkv_ref[0, :, :rotated] = turned.astype(BF16)
    qkv_ref[0, :, rotated:] = pre[:, rotated:].astype(BF16)
    bias = bias_ref[0]
    lane = lax.broadcasted_iota(jnp.int32, (pre.shape[0], LANES), 1)
    sums = jnp.zeros((pre.shape[0], LANES), F32)
    for head in range(heads):
        group = head // share
        key_at = (heads + group) * HEAD_DIM
        value_at = rotated + group * HEAD_DIM
        query = qkv_ref[0, :, head * HEAD_DIM : (head + 1) * HEAD_DIM]
        key = qkv_ref[0, :, key_at : key_at + HEAD_DIM]
        value = qkv_ref[0, :, value_at : value_at + HEAD_DIM]
        scores = dot(query * SCORE_SCALE, key, ((1,), (1,))) + bias
        highest = jnp.max(scores, -1, keepdims=True)
        exponent = jnp.exp(scores - highest)
        total = jnp.sum(exponent, -1, keepdims=True)
        weights = (exponent * (1.0 / total)).astype(BF16)
        merged_ref[0, :, head * HEAD_DIM : (head + 1) * HEAD_DIM] = dot(weights, value).astype(BF16)
        sums = jnp.where(lane == head, highest + jnp.log(total), sums)
    lse_ref[0] = sums
    rows = out_refs[0].shape[1]
    for i, out_ref in enumerate(out_refs):
        out_ref[0] = dot(merged_ref[0, i * rows : (i + 1) * rows, :], wo_ref[...]).astype(BF16)


def attention_backward_kernel(shape, spots_ref, *refs):
    packs, refs = refs[: shape["packs"]], refs[shape["packs"] :]
    slots, refs = refs[: shape["slots"]], refs[shape["slots"] :]
    cos_ref, sin_ref, bias_ref, qkv_ref, lse_ref, n1_ref, merged_ref = refs[:7]
    x_ref, n2_ref, logits_ref, mlp_ref = refs[7:11]
    refs = refs[11:]
    out_refs, refs = refs[: shape["slots"]], refs[shape["slots"] :]
    grads, refs = refs[: shape["packs"]], refs[shape["packs"] :]
    ga_ref, w_ref, wo_ref, dqkv_ref, turned_ref, gain_ref, dw_ref, dwo_ref, ds_ref, semaphores = refs
    heads, kv_heads = shape["heads"], shape["kv_heads"]
    share = heads // kv_heads
    rotated = (heads + kv_heads) * HEAD_DIM
    micro = pl.program_id(0)

    @pl.when(micro == 0)
    def _():
        copies = row_copies(slots, ga_ref) + weight_copies(shape, spots_ref, packs, w_ref, wo_ref)
        fetch(copies, semaphores)
        gain_ref[...] = jnp.zeros_like(gain_ref)
        gain_ref[1:2, :] = mlp_ref[...]

    grad_merged = dot(ga_ref[micro], wo_ref[...], ((1,), (1,))).astype(BF16)
    bias = bias_ref[0]
    for group in range(kv_heads):
        key_at = (heads + group) * HEAD_DIM
        value_at = rotated + group * HEAD_DIM
        key = qkv_ref[0, :, key_at : key_at + HEAD_DIM] * SCORE_SCALE
        value = qkv_ref[0, :, value_at : value_at + HEAD_DIM]
        grad_key, grad_value = None, None
        for head in range(group * share, (group + 1) * share):
            query = qkv_ref[0, :, head * HEAD_DIM : (head + 1) * HEAD_DIM]
            grad_rows = grad_merged[:, head * HEAD_DIM : (head + 1) * HEAD_DIM]
            scores = dot(query, key, ((1,), (1,))) + bias
            chance = jnp.exp(scores - lse_ref[0, :, head : head + 1])
            weights = chance.astype(BF16)
            grad_chance = dot(grad_rows, value, ((1,), (1,)))
            delta = jnp.sum(chance * grad_chance, -1, keepdims=True)
            grad_raw = (chance * (grad_chance - delta)).astype(BF16)
            turned_ref[:, head * HEAD_DIM : (head + 1) * HEAD_DIM] = dot(grad_raw, key)
            key_part = dot(grad_raw, query, ((0,), (0,)))
            value_part = dot(weights, grad_rows, ((0,), (0,)))
            grad_key = key_part if grad_key is None else grad_key + key_part
            grad_value = value_part if grad_value is None else grad_value + value_part
        turned_ref[:, key_at : key_at + HEAD_DIM] = grad_key * SCORE_SCALE
        dqkv_ref[micro, :, value_at : value_at + HEAD_DIM] = grad_value.astype(BF16)
    back = rotate_pairs(turned_ref[...], cos_ref[0], sin_ref[0], -1)
    dqkv_ref[micro, :, :rotated] = back.astype(BF16)
    rows = out_refs[0].shape[1]
    first = dot(dqkv_ref[micro], w_ref[...], ((1,), (1,)))
    for i, out_ref in enumerate(out_refs):
        out_ref[0] = first[i * rows : (i + 1) * rows, :].astype(BF16)
    x = x_ref[0].astype(F32)
    unit = x * lax.rsqrt(jnp.mean(x * x, -1, keepdims=True) + EPSILON)
    gain_ref[0:1, :] += jnp.sum(first * unit, 0, keepdims=True)

    @pl.when(micro == pl.num_programs(0) - 1)
    def _():
        def flat(ref):
            return ref[...].reshape(ref.shape[0] * ref.shape[1], ref.shape[2])

        dw = dot(flat(n1_ref), flat(dqkv_ref), ((0,), (0,))).astype(BF16)
        dwo = dot(flat(merged_ref), flat(ga_ref), ((0,), (0,))).astype(BF16)
        row = lax.broadcasted_iota(jnp.int32, (gain_ref.shape[0], LANES), 0)
        column = lax.broadcasted_iota(jnp.int32, (gain_ref.shape[0], LANES), 1)
        spread = jnp.where((row < 2) & (column == row + shape["gain_at"]), 1.0, 0.0)
        gains = lax.dot_general(
            gain_ref[...],
            spread,
            (((0,), (0,)), ((), ())),
            precision=lax.Precision.HIGHEST,
            preferred_element_type=F32,
        )
        ds = (gains + dot(n2_ref[...], logits_ref[...], ((0,), (0,)))).astype(BF16)
        if shape["whole"]:
            grads[0][...] = dw
            grads[1][...] = dwo
            grads[2][...] = ds
        else:
            dw_ref[...] = dw
            dwo_ref[...] = dwo
            ds_ref[...] = ds
            pack_rows, part, columns = shape["pack_rows"], shape["weight_rows"], shape["qkv_columns"]
            wide = shape["merged_columns"]
            for slot, grad_ref in enumerate(grads):
                spot = spots_ref[slot]
                at = pl.multiple_of(spot * pack_rows, pack_rows)
                grad_ref[:, :columns] = dw_ref[pl.ds(at, pack_rows), :]
                grad_ref[:, columns : columns + LANES] = ds_ref[pl.ds(at, pack_rows), :]
                at = pl.multiple_of(spot * part, part)
                for i in range(pack_rows // part):
                    grad_ref[i * part : (i + 1) * part, columns + LANES :] = dwo_ref[
                        pl.ds(at, part), i * wide : (i + 1) * wide
                    ]


def per_micro(shape):
    return pl.BlockSpec((1,) + tuple(shape[1:]), lambda m, s: (m,) + (0,) * (len(shape) - 1))


def fixed(shape):
    return pl.BlockSpec(tuple(shape), lambda m, s: (0,) * len(shape))


def attention_forward(shape, spots, packs, slots, cosine, sine, bias):
    micros, rows, width = slots[0].shape
    group = rows * len(slots)
    columns, merged = shape["qkv_columns"], shape["heads"] * HEAD_DIM
    outs = [jax.ShapeDtypeStruct((micros, rows, width), BF16) for _ in slots]
    specs = [per_micro(o.shape) for o in outs]
    more = [
        jax.ShapeDtypeStruct((micros, group, width), BF16),
        jax.ShapeDtypeStruct((micros, group, width), BF16),
        jax.ShapeDtypeStruct((width, LANES), BF16),
        jax.ShapeDtypeStruct((LANES // 2, width), F32),
        jax.ShapeDtypeStruct((micros, group, columns), BF16),
        jax.ShapeDtypeStruct((micros, group, merged), BF16),
        jax.ShapeDtypeStruct((micros, group, LANES), F32),
    ]
    specs += [fixed(o.shape) for o in more[:4]] + [per_micro(o.shape) for o in more[4:]]
    results = pl.pallas_call(
        functools.partial(attention_forward_kernel, shape),
        grid_spec=pltpu.PrefetchScalarGridSpec(
            num_scalar_prefetch=1,
            grid=(micros,),
            in_specs=[anywhere() for _ in packs + slots]
            + [per_micro(cosine.shape), per_micro(sine.shape), per_micro(bias.shape)],
            out_specs=specs,
            scratch_shapes=[
                pltpu.VMEM((width, columns), BF16),
                pltpu.VMEM((merged, width), BF16),
                pltpu.SemaphoreType.DMA((shape["copies"],)),
            ],
        ),
        out_shape=outs + more,
        name="attention_forward",
    )(spots, *packs, *slots, cosine, sine, bias)
    return (results[: len(slots)],) + tuple(results[len(slots) :])


def attention_backward(shape, spots, packs, slots, by_micro, at_once):
    micros, rows, width = slots[0].shape
    group = rows * len(slots)
    columns, merged_rows = shape["qkv_columns"], shape["heads"] * HEAD_DIM
    outs = [jax.ShapeDtypeStruct((micros, rows, width), BF16) for _ in slots]
    grads = [jax.ShapeDtypeStruct(pack.shape, BF16) for pack in packs]
    results = pl.pallas_call(
        functools.partial(attention_backward_kernel, shape),
        grid_spec=pltpu.PrefetchScalarGridSpec(
            num_scalar_prefetch=1,
            grid=(micros,),
            in_specs=[anywhere() for _ in packs + slots]
            + [per_micro(v.shape) for v in by_micro[:5]]
            + [fixed(v.shape) for v in at_once[:2]]
            + [per_micro(by_micro[5].shape)]
            + [fixed(v.shape) for v in at_once[2:]],
            out_specs=[per_micro(o.shape) for o in outs] + [fixed(g.shape) for g in grads],
            scratch_shapes=[
                pltpu.VMEM((micros, group, width), BF16),
                pltpu.VMEM((width, columns), BF16),
                pltpu.VMEM((merged_rows, width), BF16),
                pltpu.VMEM((micros, group, columns), BF16),
                pltpu.VMEM((group, (shape["heads"] + shape["kv_heads"]) * HEAD_DIM), F32),
                pltpu.VMEM((8, width), F32),
                pltpu.VMEM((width, columns), BF16),
                pltpu.VMEM((merged_rows, width), BF16),
                pltpu.VMEM((width, LANES), BF16),
                pltpu.SemaphoreType.DMA((shape["copies"],)),
            ],
        ),
        out_shape=outs + grads,
        name="attention_backward",
    )(spots, *packs, *slots, *by_micro[:5], *at_once[:2], by_micro[5], *at_once[2:])
    return list(results[: len(slots)]), list(results[len(slots) :])


def experts_kernel(shape, table_ref, *refs):
    slots, cores, ys, zs = shape["slots"], shape["cores"], shape["ys"], shape["zs"]
    own, hidden = shape["own"], shape["hidden"]
    x_slots, refs = refs[:slots], refs[slots:]
    beside, refs = refs[:slots], refs[slots:]
    gu_parts, refs = refs[: cores * ys], refs[cores * ys :]
    dn_parts, refs = refs[: cores * ys], refs[cores * ys :]
    wr_ref, gate_ref, x_out, gm_out = refs[:4]
    back_outs, refs = refs[4 : 4 + slots], refs[4 + slots :]
    mixed_outs, refs = refs[:slots], refs[slots:]
    act_outs, refs = refs[:cores], refs[cores:]
    dgu_outs, refs = refs[:cores], refs[cores:]
    x_ref, gm_ref, mask_ref, wgu_ref, wdn_ref, act_ref, dgu_ref, back_ref, mixed_ref = refs[:9]
    in_sems, out_sems = refs[9:]
    rows, width = x_slots[0].shape[0], x_ref.shape[1]
    part = width // (ys * zs)
    wide, tall = 2 * hidden * own, hidden * own
    local = cores * own

    fetched = [[] for _ in range(cores + 2)]
    for i in range(slots):
        at = pl.ds(i * rows, rows)
        fetched[0].append((x_slots[i].at[:, pl.ds(0, width)], x_ref.at[at, :]))
        fetched[cores].append((x_slots[i].at[:, pl.ds(width, LANES)], mask_ref.at[at, :]))
        fetched[cores + 1].append((beside[i], gm_ref.at[at, :]))
    step = hidden // ys
    for c in range(cores):
        for s in range(ys):
            y = table_ref[local + s]
            for z in range(zs):
                at = pl.multiple_of((z * ys + y) * part, part)
                goal = wgu_ref.at[pl.ds(at, part), pl.ds(c * wide, wide)]
                fetched[c].append((gu_parts[c * ys + s].at[z], goal))
            for e in range(own):
                at = pl.multiple_of((c * own + e) * hidden + y * step, step)
                goal = wdn_ref.at[pl.ds(at, step), :]
                fetched[cores + 1].append((dn_parts[c * ys + s].at[e], goal))
    used = 0
    for group in fetched:
        for i, (source, goal) in enumerate(group):
            group[i] = pltpu.make_async_copy(source, goal, in_sems.at[used])
            group[i].start()
            used += 1

    def arrive(group):
        for copy in fetched[group]:
            copy.wait()

    leaving = []

    def leave(source, goal):
        leaving.append(pltpu.make_async_copy(source, goal, out_sems.at[len(leaving)]))
        leaving[-1].start()

    pre = []
    for c in range(cores):
        arrive(c)
        if c == 0:
            leave(x_ref, x_out)
        pre.append(dot(x_ref[...], wgu_ref[:, c * wide : (c + 1) * wide]))
    arrive(cores)
    total = slots * rows
    lane = lax.broadcasted_iota(jnp.int32, (total, LANES), 1)
    named = mask_ref[...].astype(F32) > 0.5
    logits = jnp.where(named, dot(x_ref[...], wr_ref[...]), NEGATIVE)
    highest = jnp.max(logits, -1, keepdims=True)
    exponent = jnp.where(named, jnp.exp(logits - highest), 0.0)
    gates = exponent / jnp.sum(exponent, -1, keepdims=True)
    gate_ref[...] = gates
    arrive(cores + 1)
    leave(gm_ref, gm_out)
    grad_act = dot(gm_ref[...], wdn_ref[...], ((1,), (1,)))
    picked = jnp.zeros((total, LANES), F32)
    for c in range(cores):
        for e in range(own):
            j = c * own + e
            mine = lane == table_ref[j]
            gate = jnp.sum(jnp.where(mine, gates, 0.0), -1, keepdims=True)
            base = 2 * hidden * e
            gate_pre = pre[c][:, base : base + hidden]
            up_pre = pre[c][:, base + hidden : base + 2 * hidden]
            grad_one = grad_act[:, j * hidden : (j + 1) * hidden]
            sig = jax.nn.sigmoid(gate_pre)
            silu = gate_pre * sig
            activated = (silu * up_pre).astype(BF16).astype(F32)
            found = jnp.sum(activated * grad_one, -1, keepdims=True)
            picked = jnp.where(mine, found, picked)
            act_ref[c, :, e * hidden : (e + 1) * hidden] = (activated * gate).astype(BF16)
            grad_one = grad_one * gate
            base = 2 * hidden * j
            dgu_ref[:, base : base + hidden] = (
                grad_one * up_pre * sig * (1.0 + gate_pre * (1.0 - sig))
            ).astype(BF16)
            dgu_ref[:, base + hidden : base + 2 * hidden] = (grad_one * silu).astype(BF16)
        leave(dgu_ref.at[:, pl.ds(c * wide, wide)], dgu_outs[c])
        leave(act_ref.at[c], act_outs[c])

    coarse = picked.astype(BF16)
    back_ref[:, width : width + LANES] = coarse
    back_ref[:, width + LANES :] = (picked - coarse.astype(F32)).astype(BF16)
    back_ref[:, :width] = dot(dgu_ref[...], wgu_ref[...], ((1,), (1,))).astype(BF16)

    def leave_slots(source, goals):
        for i in range(slots):
            leave(source.at[pl.ds(i * rows, rows), :], goals[i])

    leave_slots(back_ref, back_outs)
    if tall % LANES == 0:
        acts = jnp.concatenate([act_ref[c] for c in range(cores)], 1)
        mixed = dot(acts, wdn_ref[...])
    else:
        mixed = sum(dot(act_ref[c], wdn_ref[c * tall : (c + 1) * tall, :]) for c in range(cores))
    mixed_ref[...] = mixed.astype(BF16)
    leave_slots(mixed_ref, mixed_outs)
    for copy in leaving:
        copy.wait()


def run_experts(shape, table, x_slots, beside, gu_parts, dn_parts, wr):
    rows, width = x_slots[0].shape[0], wr.shape[0]
    total = rows * len(x_slots)
    cores, own, hidden = shape["cores"], shape["own"], shape["hidden"]
    outs = [
        jax.ShapeDtypeStruct((total, LANES), F32),
        jax.ShapeDtypeStruct((total, width), BF16),
        jax.ShapeDtypeStruct((total, width), BF16),
    ]
    outs += [jax.ShapeDtypeStruct((rows, width + 2 * LANES), BF16) for _ in x_slots]
    outs += [jax.ShapeDtypeStruct((rows, width), BF16) for _ in x_slots]
    outs += [jax.ShapeDtypeStruct((total, own * hidden), BF16) for _ in range(cores)]
    outs += [jax.ShapeDtypeStruct((total, 2 * own * hidden), BF16) for _ in range(cores)]
    shape = dict(shape, slots=len(x_slots))
    copies = 3 * len(x_slots) + cores * shape["ys"] * (shape["zs"] + own)
    operands = x_slots + beside + gu_parts + dn_parts
    return pl.pallas_call(
        functools.partial(experts_kernel, shape),
        in_specs=[pl.BlockSpec(memory_space=pltpu.SMEM)] + [anywhere() for _ in operands] + [on_chip()],
        out_specs=[on_chip()] + [anywhere() for _ in outs[1:]],
        out_shape=outs,
        scratch_shapes=[
            pltpu.VMEM((total, width), BF16),
            pltpu.VMEM((total, width), BF16),
            pltpu.VMEM((total, LANES), BF16),
            pltpu.VMEM((width, cores * own * 2 * hidden), BF16),
            pltpu.VMEM((cores * own * hidden, width), BF16),
            pltpu.VMEM((cores, total, own * hidden), BF16),
            pltpu.VMEM((total, cores * own * 2 * hidden), BF16),
            pltpu.VMEM((total, width + 2 * LANES), BF16),
            pltpu.VMEM((total, width), BF16),
            pltpu.SemaphoreType.DMA((copies,)),
            pltpu.SemaphoreType.DMA((2 + 2 * cores + 2 * len(x_slots),)),
        ],
        compiler_params=pltpu.CompilerParams(vmem_limit_bytes=60 << 20),
        name="experts",
    )(table, *operands, wr)


def pack_kernel(hidden, gate_ref, up_ref, out_ref):
    for z in range(out_ref.shape[0]):
        out_ref[z, :, :hidden] = gate_ref[0, :, z * hidden : (z + 1) * hidden]
        out_ref[z, :, hidden:] = up_ref[0, :, z * hidden : (z + 1) * hidden]


def pack_experts(w_gate, w_up, zs):
    own, part, hidden_all = w_gate.shape
    hidden = hidden_all // zs
    return pl.pallas_call(
        functools.partial(pack_kernel, hidden),
        grid=(own,),
        in_specs=[pl.BlockSpec((1, part, hidden_all), lambda e: (e, 0, 0))] * 2,
        out_specs=pl.BlockSpec((zs, part, 2 * hidden), lambda e: (0, 0, e)),
        out_shape=jax.ShapeDtypeStruct((zs, part, own * 2 * hidden), BF16),
        name="pack_experts",
    )(w_gate, w_up)


def unpack_kernel(hidden, in_ref, gate_ref, up_ref):
    for z in range(in_ref.shape[0]):
        gate_ref[0, :, z * hidden : (z + 1) * hidden] = in_ref[z, :, :hidden].astype(F32)
        up_ref[0, :, z * hidden : (z + 1) * hidden] = in_ref[z, :, hidden:].astype(F32)


def unpack_experts(packed, own):
    zs, part, wide = packed.shape
    hidden = wide // own // 2
    out = jax.ShapeDtypeStruct((own, part, zs * hidden), F32)
    return pl.pallas_call(
        functools.partial(unpack_kernel, hidden),
        grid=(own,),
        in_specs=[pl.BlockSpec((zs, part, 2 * hidden), lambda e: (0, 0, e))],
        out_specs=[pl.BlockSpec((1, part, zs * hidden), lambda e: (e, 0, 0))] * 2,
        out_shape=[out, out],
        name="unpack_experts",
    )(packed)


def per_device(
    tokens,
    cotangent,
    attn_gain,
    mlp_gain,
    w_query,
    w_key,
    w_value,
    w_out,
    w_router,
    w_gate,
    w_up,
    w_down,
    shuffle,
    routes,
    lengths,
):
    micros, rows, width = tokens.shape
    dp_count, members = lax.axis_size("dp"), lax.axis_size("expert")
    devices = dp_count * members
    rings = Rings(dp_count, members)
    zn, yn, xn, cn = rings.z, rings.y, rings.x, rings.core
    group_rows = rows * members
    experts_all = w_router.shape[1]
    own_experts, model_part, hidden_all = w_gate.shape
    hidden_part = hidden_all // zn
    heads, kv_heads = HEADS // members, KV_HEADS // members
    weight_rows = w_query.shape[0]
    home_rows = micros * rows

    phases = Phases()

    def over_members(value):
        return phases.start(rings.gather_two(value, "c", "x"))

    def sum_members(parts):
        parts = [[parts[s * cn + t] for s in range(xn)] for t in range(cn)]
        return phases.start(rings.reduce_two(parts, "x", "c"))

    def line(columns):
        return [slot for column in columns for slot in column]

    def by_member(w):
        return w.reshape(weight_rows, members, w.shape[1] // members)

    small = jnp.concatenate([w_router, attn_gain[:, None], mlp_gain[:, None]], 1)
    small = jnp.pad(small, ((0, 0), (0, LANES - experts_all - 2)))
    small = jnp.broadcast_to(small[:, None, :], (weight_rows, members, LANES))
    mine = jnp.concatenate([by_member(w_query), by_member(w_key), by_member(w_value), small], 2)
    mine = lax.all_to_all(mine.transpose(1, 0, 2), "expert", 0, 0)
    small_at = mine.shape[2]
    qkv_columns = small_at - LANES
    pack_rows = members * weight_rows
    mine = mine.reshape(pack_rows, small_at)
    to_heads = [(s, (s % dp_count) * members + s // dp_count) for s in range(devices)]
    to_home = [(t, s) for s, t in to_heads]
    out_mine = lax.ppermute(w_out, ALL, to_heads)
    weights_started = []
    group_tokens = phases.start(paced(rings.gather_two(tokens, "c", "x"), weights_started))
    gate_up = pack_experts(w_gate, w_up, zn)
    begun = phases.start(make(lambda: (mine, gate_up, out_mine, routes)))
    phases.phase()
    (mine, gate_up, out_mine, routes) = begun.result
    merged_columns = width // members
    pack = jnp.concatenate(
        [out_mine[:, i * merged_columns : (i + 1) * merged_columns] for i in range(members)], 0
    )
    pack = jnp.concatenate([mine, pack], 1)
    whole = weight_rows % 16 != 0
    attention_shape = {
        "heads": heads,
        "kv_heads": kv_heads,
        "whole": whole,
        "pack_rows": pack_rows,
        "weight_rows": weight_rows,
        "qkv_columns": qkv_columns,
        "merged_columns": merged_columns,
        "slots": members,
        "gain_at": experts_all,
        "packs": 3 if whole else dp_count,
        "copies": micros * members + (3 if whole else dp_count * (2 + members)),
    }
    inputs = tokens.astype(F32)
    inv_first = lax.rsqrt(jnp.mean(inputs * inputs, -1, keepdims=True) + EPSILON)
    unit_first = inputs * inv_first

    grad_result = cotangent.astype(F32)
    grad_moe = (RESIDUAL_SCALE * grad_result).astype(BF16).reshape(home_rows, width)
    pack, routes, w_down, grad_moe = tie(pack, routes, w_down, grad_moe)
    packs = phases.start(rings.gather_two(pack, "z", "y"))
    weights_started.append(True)
    work = phases.start(make(lambda: grad_moe))
    phases.phase()
    beside = phases.start(rings.gather_two(work.result, "z", "x"))
    dealt = lax.all_to_all(
        routes.reshape(micros, dp_count, rows // dp_count, routes.shape[2]), "dp", 1, 1
    ).reshape(micros, rows, routes.shape[2])
    held = phases.start(make(lambda: dealt))
    phases.phase()
    dealt = held.result
    lane_ids = jnp.arange(LANES, dtype=jnp.int32)
    hot = jnp.sum((dealt[:, :, :, None] == lane_ids).astype(F32), 2).astype(BF16)
    place = (shuffle[:, 0, :, None] == jnp.arange(rows, dtype=jnp.int32)).astype(BF16)
    named = jnp.einsum("mir,mix->mrx", place, hot, preferred_element_type=F32).astype(BF16)

    row_at = jnp.concatenate(
        [
            (rings.origin("x", s) * cn + rings.origin("c", t)) * rows
            + jnp.arange(rows, dtype=jnp.int32)
            for s in range(xn)
            for t in range(cn)
        ]
    )
    row_at, dealt = tie(row_at, dealt)
    half = HEAD_DIM // 2
    lane = jnp.arange(LANES, dtype=jnp.int32)
    inverse = ROPE_BASE ** (-((lane % half).astype(F32) * 2.0) / HEAD_DIM)
    sign = jnp.where(lane % HEAD_DIM < half, -1.0, 1.0)
    doc_lengths = lengths[:, 0]
    doc_ends = jnp.cumsum(doc_lengths, 1)
    doc_starts = doc_ends - doc_lengths
    segment = jnp.sum((row_at[None, :, None] >= doc_ends[:, None, :]).astype(jnp.int32), 2)
    docs = jnp.arange(doc_lengths.shape[1], dtype=jnp.int32)
    start = jnp.sum(jnp.where(segment[:, :, None] == docs, doc_starts[:, None, :], 0), 2)
    position = row_at[None, :] - start
    angles = position.astype(F32)[:, :, None] * inverse
    cosine, sine = jnp.cos(angles), jnp.sin(angles) * sign
    allowed = segment[:, :, None] == segment[:, None, :]
    bias = jnp.where(allowed & (row_at[None, :] <= row_at[:, None]), 0.0, NEGATIVE)

    tables = phases.start(make(lambda: (cosine, sine, bias, named, gate_up, w_down)))
    phases.phase()
    cosine, sine, bias, named, gate_up, w_down = tables.result
    gate_up = lax.all_to_all(gate_up, "dp", 0, 0, axis_index_groups=rings.z_groups)
    held = phases.start(make(lambda: w_down))
    packs, group_tokens = phases.finish(packs, group_tokens)
    w_down = held.result
    spots = jnp.stack(
        [rings.origin("z", t) * yn + rings.origin("y", s) for s in range(yn) for t in range(zn)]
    )
    if whole:
        packs = [in_order(column, rings.at["z"], zn) for column in packs]
        packs = [in_order([packs[s][z] for s in range(yn)], rings.at["y"], yn) for z in range(zn)]
        packs = jnp.stack([packs[z][y] for z in range(zn) for y in range(yn)])
        w_merge = packs[:, :, small_at:].reshape(dp_count, members, weight_rows, merged_columns)
        w_merge = w_merge.transpose(0, 2, 1, 3).reshape(dp_count * weight_rows, width)
        w_small = packs[:, :, qkv_columns:small_at].reshape(width, LANES)
        packs = [packs[:, :, :qkv_columns].reshape(width, qkv_columns), w_merge, w_small]
    else:
        packs = line(packs)

    down = rings.gather(w_down, "y")
    attention = phases.start(
        make(
            attention_forward,
            attention_shape,
            spots,
            packs,
            line(group_tokens),
            cosine,
            sine,
            bias,
        )
    )
    down_task = phases.start(make(lambda: down))
    (_, beside) = phases.finish(attention, beside)
    down = phases.start(make(lambda: [rings.gather(part, "c") for part in down_task.result]))
    attn_parts, group_in, n1, router_columns, small_rows, qkv, merged, lse = attention.result
    gain_first = small_rows[experts_all]
    gain_second = small_rows[experts_all + 1]
    attended = sum_members(attn_parts)
    for _ in range(xn - 1):
        phases.phase()
    gate_up = phases.start(make(lambda: gate_up))
    attended, down, gate_up = phases.finish(attended, down, gate_up)
    hidden = inputs + RESIDUAL_SCALE * attended
    inv_second = lax.rsqrt(jnp.mean(hidden * hidden, -1, keepdims=True) + EPSILON)
    unit_second = hidden * inv_second
    normed_second = (unit_second * gain_second).astype(BF16).reshape(home_rows, width)

    together = jnp.concatenate([normed_second, named.reshape(home_rows, LANES)], 1)
    group_x = phases.start(rings.gather_two(together, "z", "x"))
    gate_up = rings.gather(gate_up, "y")
    phases.phase()
    phases.phase()
    mine_too = phases.start(make(lambda: rings.gather(gate_up[0], "c")))
    gate_up = phases.start(make(lambda: gate_up[1:]))
    phases.finish(mine_too, gate_up)
    gate_up = phases.start(make(lambda: [rings.gather(part, "c") for part in gate_up.result]))
    group_x, gate_up = phases.finish(group_x, gate_up)
    gate_up = [mine_too.result] + gate_up
    gu_parts = [gate_up[s][c] for c in range(cn) for s in range(yn)]
    dn_parts = [down[s][c] for c in range(cn) for s in range(yn)]

    slots = [(s, t) for s in range(xn) for t in range(zn)]
    x_slots = [group_x[s][t] for s, t in slots]
    beside = [beside[s][t] for s, t in slots]
    chunk = min(len(slots), 8)
    chunks = len(slots) // chunk
    table = [
        (rings.at["x"] * cn + rings.origin("c", s)) * own_experts
        + jnp.arange(own_experts, dtype=jnp.int32)
        for s in range(cn)
    ]
    table.append(jnp.stack([rings.origin("y", s) for s in range(yn)]))
    table = jnp.concatenate(table)
    experts_shape = {"cores": cn, "ys": yn, "zs": zn, "own": own_experts, "hidden": hidden_part}
    results = [
        run_experts(
            experts_shape,
            table,
            x_slots[i * chunk : (i + 1) * chunk],
            beside[i * chunk : (i + 1) * chunk],
            gu_parts,
            dn_parts,
            router_columns,
        )
        for i in range(chunks)
    ]
    back = [part for pieces in results for part in pieces[3 : 3 + chunk]]
    mixed = [part for pieces in results for part in pieces[3 + chunk : 3 + 2 * chunk]]
    results = [pieces[:3] + pieces[3 + 2 * chunk :] for pieces in results]
    results = [pieces[0] if chunks == 1 else jnp.concatenate(pieces, 0) for pieces in zip(*results)]
    gates, x_all, gm_all = results[:3]
    acts, dgus = results[3 : 3 + cn], results[3 + cn :]
    back = [back[i * zn : (i + 1) * zn] for i in range(xn)]
    mixed = [mixed[i * zn : (i + 1) * zn] for i in range(xn)]

    def by_y(value, axis):
        return [lax.dynamic_index_in_dim(value, rings.origin("y", s), axis, False) for s in range(yn)]

    def product(core, kind, x, gm, coming):
        if kind == 0:
            term = dot(x, dgus[core], ((0,), (0,)))
        else:
            term = dot(acts[core], gm, ((0,), (0,)))
        return (term if coming is None else term + coming.astype(F32)).astype(BF16)

    def own_gu(x, coming):
        return by_y(product(0, 0, x, None, coming).reshape(zn, yn, model_part, -1), 1)

    def own_dn(gm, coming):
        value = product(0, 1, None, gm, coming)
        return by_y(value.reshape(own_experts, yn, hidden_part // yn, width), 1)

    def held(*values):
        return phases.start(make(lambda: values))

    rows_back = phases.start(rings.reduce_two(back, "z", "x", two_part))
    x, gm, coming = x_all, gm_all, [None, None]
    if cn > 1:
        work = held(product(1, 0, x, None, None), x, gm)
        phases.phase()
        other, x, gm = work.result
        coming[0] = rings.step(other, "c")
    first = min(1, zn - 1)
    other = [product(1, 1, None, gm, None)] if cn > 1 else []
    work = held(own_gu(x, coming[0]), other, gm, [row[first] for row in mixed])
    phases.phase()
    made, other, gm, mixed_first = work.result
    if cn > 1:
        coming[1] = rings.step(other[0], "c")
    groups = [(0, 2), (2, 4), (4, 5)] if own_experts == 5 else [(0, own_experts)]
    wide = 2 * hidden_part
    waiting = [[part[:, :, low * wide : high * wide] for part in made] for low, high in groups]
    grad_gu = []

    def next_group(*keep):
        nonlocal waiting
        if waiting:
            grad_gu.append(phases.start(rings.reduce(waiting[0], "y")))
            waiting = waiting[1:]
        work = held(waiting, *keep)
        phases.phase()
        waiting, *keep = work.result
        return keep

    for row, value in zip(mixed, mixed_first):
        row[first] = value
    moe_rows = phases.start(rings.reduce_two(mixed, "z", "x"))
    (gm, *coming) = next_group(gm, *([coming[1]] if cn > 1 else []))
    (grad_dn,) = next_group(own_dn(gm, coming[0] if coming else None))
    phases.finish(rows_back)
    grad_dealt = rows_back.result[:, :width]
    grad_gates = rows_back.result[:, width:]
    grad_gates = grad_gates[:, :LANES] + grad_gates[:, LANES:]
    own_gates = gates[:home_rows]
    grad_picked = own_gates * (grad_gates - jnp.sum(own_gates * grad_gates, -1, keepdims=True))
    grad_logits = grad_picked.astype(BF16)
    router_rows = small_rows.astype(BF16)
    grad_dealt = (grad_dealt + dot(grad_logits[:, : LANES // 2], router_rows)).astype(BF16)
    grad_normed_second = grad_dealt.astype(F32).reshape(micros, rows, width)
    scaled_second = grad_normed_second * gain_second
    grad_hidden = grad_result + inv_second * (
        scaled_second - unit_second * jnp.mean(scaled_second * unit_second, -1, keepdims=True)
    )
    mlp_gain_grad = jnp.sum(grad_normed_second * unit_second, (0, 1))[None]
    grad_attn = (RESIDUAL_SCALE * grad_hidden).astype(BF16)

    grad_attn = over_members(grad_attn)
    while waiting:
        next_group()
    grad_gu = jnp.concatenate([part.astype(BF16) for part in phases.finish(*grad_gu)], 2)
    work = held(grad_gu, grad_dn)
    phases.finish(grad_attn, moe_rows, work)
    grad_gu, grad_dn = work.result
    grad_gu = lax.all_to_all(grad_gu, "dp", 0, 0, axis_index_groups=rings.z_groups)
    grad_dn = phases.start(rings.reduce(grad_dn, "y"))

    attention = phases.start(
        make(
            attention_backward,
            attention_shape,
            spots,
            packs,
            line(grad_attn.result),
            [cosine, sine, bias, qkv, lse, group_in],
            [n1, merged, normed_second, grad_logits, mlp_gain_grad],
        )
    )
    phases.finish(attention)
    first_parts, weight_grads = attention.result

    if whole:
        grad_qkv, grad_out, grad_small = weight_grads
        grad_out = grad_out.reshape(dp_count, weight_rows, members, merged_columns).transpose(0, 2, 1, 3)
        both = jnp.concatenate(
            [
                grad_qkv.reshape(dp_count, pack_rows, qkv_columns),
                grad_small.reshape(dp_count, pack_rows, LANES),
                grad_out.reshape(dp_count, pack_rows, merged_columns),
            ],
            2,
        )
        weight_grads = [
            lax.dynamic_index_in_dim(both, spots[i], 0, False) for i in range(dp_count)
        ]
    both = phases.start(
        rings.reduce_two([[weight_grads[s * zn + t] for t in range(zn)] for s in range(yn)], "z", "y")
    )
    phases.phase()
    grad_gu = held(grad_gu)
    grad_normed_first = sum_members(first_parts)
    both, grad_gu, grad_dn, grad_normed_first, moe_rows = phases.finish(
        both, grad_gu, grad_dn, grad_normed_first, moe_rows
    )
    grad_gate, grad_up = unpack_experts(grad_gu[0], own_experts)
    moe_rows = moe_rows.astype(BF16).reshape(micros, rows, width)
    output = (hidden + RESIDUAL_SCALE * moe_rows.astype(F32)).astype(BF16)
    scaled_first = grad_normed_first * gain_first
    grad_tokens = grad_hidden + inv_first * (
        scaled_first - unit_first * jnp.mean(scaled_first * unit_first, -1, keepdims=True)
    )
    grad_out = [
        both[i * weight_rows : (i + 1) * weight_rows, small_at:] for i in range(members)
    ]
    grad_out = lax.ppermute(jnp.concatenate(grad_out, 1).astype(BF16), ALL, to_home).astype(F32)
    home = both[:, :small_at].reshape(members, weight_rows, small_at)
    home = lax.all_to_all(home.astype(BF16), "expert", 0, 0).astype(F32)

    def columns(start, count):
        return jnp.concatenate([home[i, :, start : start + count] for i in range(members)], 1)

    query_columns, key_columns = heads * HEAD_DIM, kv_heads * HEAD_DIM
    grad_query = columns(0, query_columns)
    grad_key = columns(query_columns, key_columns)
    grad_value = columns(query_columns + key_columns, key_columns)

    small = jnp.sum(home[:, :, qkv_columns:], 0)
    grad_w_router = small[:, :experts_all]
    grad_attn_gain, grad_mlp_gain = small[:, experts_all], small[:, experts_all + 1]

    return (
        output,
        grad_tokens,
        grad_attn_gain,
        grad_mlp_gain,
        grad_query,
        grad_key,
        grad_value,
        grad_out,
        grad_w_router,
        grad_gate,
        grad_up,
        grad_dn,
    )


def solution(mesh):
    rows = P(None, ALL, None)
    placed = (rows, rows, P(ALL), P(ALL)) + (P(ALL, None),) * 5
    placed += (P("expert", "dp", None),) * 3 + (rows, rows, P(None, "dp", None))
    results = (rows, rows, P(ALL), P(ALL)) + (P(ALL, None),) * 5
    results += (P("expert", "dp", None),) * 3
    return jax.shard_map(per_device, mesh=mesh, in_specs=placed, out_specs=results, check_vma=False)
```

```python
import functools

import jax
import jax.numpy as jnp
from jax import lax
from jax.experimental import pallas as pl
from jax.experimental.pallas import tpu as pltpu
from jax.sharding import PartitionSpec as P

HEADS = 24
KV_HEADS = 8
HEAD_DIM = 64

EPSILON = 1e-06
ROPE_BASE = 10000.0
RESIDUAL_SCALE = 0.22
SCORE_SCALE = 1.0 / 64.0
NEGATIVE = -1e30
LANES = 128

BF16 = jnp.bfloat16
F32 = jnp.float32
ALL = ("dp", "expert")


def dot(a, b, dims=((1,), (0,))):
    return lax.dot_general(a, b, (dims, ((), ())), preferred_element_type=F32)


class Rings:
    def __init__(self, dp_count, expert_count):
        y_count = 1
        while dp_count % (2 * y_count) == 0 and 8 * y_count * y_count <= dp_count:
            y_count *= 2
        self.y, self.z = y_count, dp_count // y_count
        self.core = 2 if expert_count % 2 == 0 else 1
        self.x = expert_count // self.core
        zs, ys, xs, cs = range(self.z), range(self.y), range(self.x), range(self.core)
        self.z_groups = [[z * self.y + y for z in zs] for y in ys]
        self.token_groups = [
            [(z * self.y + y) * expert_count + x * self.core + c for z in zs for x in xs]
            for y in ys
            for c in cs
        ]
        self.table = {
            "z": ("dp", self.z, [(z * self.y + y, (z + 1) % self.z * self.y + y) for z in zs for y in ys]),
            "y": ("dp", self.y, [(z * self.y + y, z * self.y + (y + 1) % self.y) for z in zs for y in ys]),
            "x": (
                "expert",
                self.x,
                [(x * self.core + c, (x + 1) % self.x * self.core + c) for x in xs for c in cs],
            ),
            "c": (
                "expert",
                self.core,
                [(x * self.core + c, x * self.core + (c + 1) % self.core) for x in xs for c in cs],
            ),
        }
        d, e = lax.axis_index("dp"), lax.axis_index("expert")
        self.at = {"z": d // self.y, "y": d % self.y, "x": e // self.core, "c": e % self.core}

    def count(self, ring):
        return self.table[ring][1]

    def step(self, value, ring):
        axis, _, pairs = self.table[ring]
        return lax.ppermute(value, axis, pairs)

    def origin(self, ring, slot):
        return lax.rem(self.at[ring] + (self.count(ring) - slot), self.count(ring))

    def gather(self, value, ring):
        slots = [value]
        for _ in range(1, self.count(ring)):
            slots.append(self.step(slots[-1], ring))
        return slots

    def send(self, terms, ring, wire=None):
        running = None
        for term in terms[1:]:
            if running is None:
                term = term.astype(BF16)
            else:
                term = term.astype(F32) + running.astype(F32)
                term = term.astype(BF16) if wire is None else wire(term)
            running = self.step(term, ring)
        return running


    def gather_two(self, value, first, second, count=None):
        columns, slot = [], value
        count = self.count(first) if count is None else count
        for t in range(count):
            column = self.gather(slot, second)
            ahead = [self.step(slot, first)] if t + 1 < count else []
            tied = yield ahead + column[1:]
            columns.append([column[0]] + tied[len(ahead) :])
            slot = tied[0]
        return [[column[s] for column in columns] for s in range(self.count(second))]

    def reduce(self, parts, ring):
        running = self.send(parts, ring)
        own = parts[0]
        if running is not None:
            own, running = yield [own, running]
        return own.astype(F32) if running is None else own.astype(F32) + running.astype(F32)

    def reduce_two(self, parts, first, second, wire=None):
        count = self.count(first)
        parts = [list(row) for row in parts]
        arrived, running = {}, None
        order = list(range(1, count)) + [0]
        for phase in range(count + (count > 1)):
            made = []
            if phase > 0:
                t = order[phase - 1]
                term = self.partial(parts, arrived, t)
                if running is not None:
                    term = term + running.astype(F32)
                made.append(self.step(term.astype(BF16) if wire is None else wire(term), first))
            if phase < count:
                passing = self.send([row[order[phase]] for row in parts], second, wire)
                if passing is not None:
                    made.append(passing)
            after = [row[order[phase + 1]] for row in parts] if phase + 1 < count else []
            tied = yield made + after
            if after:
                for row, value in zip(parts, tied[len(made) :]):
                    row[order[phase + 1]] = value
            if phase < count and passing is not None:
                arrived[order[phase]] = tied[len(made) - 1]
            if phase > 0:
                running = tied[0]
            if phase == count - 1 and count > 1:
                break
        own = self.partial(parts, arrived, 0)
        return own if running is None else own + running.astype(F32)

    def partial(self, parts, arrived, t):
        own = parts[0][t].astype(F32)
        return own if t not in arrived else own + arrived[t].astype(F32)


def two_part(term):
    width = term.shape[1] - 2 * LANES
    value = term[:, width : width + LANES] + term[:, width + LANES :]
    coarse = value.astype(BF16)
    fine = (value - coarse.astype(F32)).astype(BF16)
    return jnp.concatenate([term[:, :width].astype(BF16), coarse, fine], 1)


class Task:
    def __init__(self, steps):
        self.steps, self.made, self.result, self.done = steps, [], None, False
        self.advance(None)

    def advance(self, values):
        try:
            self.made = list(self.steps.send(values))
        except StopIteration as stop:
            self.result, self.done, self.made = stop.value, True, []


class Phases:
    def __init__(self):
        self.tasks = []

    def start(self, steps):
        task = Task(steps)
        self.tasks.append(task)
        return task

    def phase(self):
        self.tasks = [task for task in self.tasks if not task.done]
        made = [value for task in self.tasks for value in task.made]
        tied = list(tie(*made)) if made else []
        for task in self.tasks:
            count = len(task.made)
            values, tied = tied[:count], tied[count:]
            task.advance(values)

    def finish(self, *tasks):
        while not all(task.done for task in tasks):
            self.phase()
        return [task.result for task in tasks]


def resumed(steps, made):
    while True:
        made = yield made
        try:
            made = steps.send(made)
        except StopIteration as stop:
            return stop.value


def paced(steps, ready):
    made = next(steps)
    while True:
        tied = yield made
        while not ready:
            tied = yield tied
        try:
            made = steps.send(tied)
        except StopIteration as stop:
            return stop.value


def make(function, *arguments):
    flat, tree = jax.tree.flatten(function(*arguments))
    flat = yield flat
    return jax.tree.unflatten(tree, flat)


def tie(*values):
    return lax.optimization_barrier(values)


def in_order(slots, position_of, count):
    stacked = jnp.stack(slots)
    return [
        lax.dynamic_index_in_dim(stacked, lax.rem(position_of + (count - i), count), 0, False)
        for i in range(count)
    ]


def fetch(copies, semaphores):
    started = [pltpu.make_async_copy(a, b, semaphores.at[i]) for i, (a, b) in enumerate(copies)]
    for copy in started:
        copy.start()
    for copy in started:
        copy.wait()


def anywhere():
    return pl.BlockSpec(memory_space=pl.ANY)


def on_chip():
    return pl.BlockSpec(memory_space=pltpu.VMEM)


def rotate_pairs(values, cosine, sine, direction):
    lane = lax.broadcasted_iota(jnp.int32, (values.shape[0], LANES), 1)
    low = (lane & (HEAD_DIM - 1)) < HEAD_DIM // 2
    pieces = []
    for start in range(0, values.shape[1], LANES):
        piece = values[:, start : start + LANES]
        partner = jnp.where(
            low,
            pltpu.roll(piece, LANES - HEAD_DIM // 2, 1),
            pltpu.roll(piece, HEAD_DIM // 2, 1),
        )
        turned = partner * sine
        pieces.append(piece * cosine + turned if direction > 0 else piece * cosine - turned)
    return jnp.concatenate(pieces, 1)


def weight_copies(shape, spots_ref, packs, w_ref, wo_ref, small_ref=None):
    if shape["whole"]:
        copies = [(packs[0], w_ref), (packs[1], wo_ref)]
        return copies if small_ref is None else copies + [(packs[2], small_ref)]
    copies = []
    rows, part, columns = shape["pack_rows"], shape["weight_rows"], shape["qkv_columns"]
    wide = shape["merged_columns"]
    for slot, pack in enumerate(packs):
        spot = spots_ref[slot]
        at = pl.multiple_of(spot * rows, rows)
        copies.append((pack.at[:, pl.ds(0, columns)], w_ref.at[pl.ds(at, rows), :]))
        if small_ref is not None:
            copies.append((pack.at[:, pl.ds(columns, LANES)], small_ref.at[pl.ds(at, rows), :]))
        at = pl.multiple_of(spot * part, part)
        for i in range(rows // part):
            copies.append(
                (
                    pack.at[pl.ds(i * part, part), pl.ds(columns + LANES, wide)],
                    wo_ref.at[pl.ds(at, part), pl.ds(i * wide, wide)],
                )
            )
    return copies


def row_copies(slots, into_ref):
    micros, rows, _ = slots[0].shape
    return [
        (slot.at[m], into_ref.at[m, pl.ds(i * rows, rows), :])
        for i, slot in enumerate(slots)
        for m in range(micros)
    ]


def attention_forward_kernel(shape, spots_ref, *refs):
    packs, refs = refs[: shape["packs"]], refs[shape["packs"] :]
    slots, refs = refs[: shape["slots"]], refs[shape["slots"] :]
    cos_ref, sin_ref, bias_ref = refs[:3]
    out_refs, refs = refs[3 : 3 + shape["slots"]], refs[3 + shape["slots"] :]
    x_ref, n1_ref, small_ref, rows_ref, qkv_ref, merged_ref, lse_ref = refs[:7]
    w_ref, wo_ref, semaphores = refs[7:]
    heads, kv_heads = shape["heads"], shape["kv_heads"]
    share = heads // kv_heads
    rotated = (heads + kv_heads) * HEAD_DIM
    micro = pl.program_id(0)

    @pl.when(micro == 0)
    def _():
        copies = weight_copies(shape, spots_ref, packs, w_ref, wo_ref, small_ref)
        fetch(row_copies(slots, x_ref) + copies, semaphores)
        count = rows_ref.shape[0]
        row = lax.broadcasted_iota(jnp.int32, (count, LANES), 0)
        column = lax.broadcasted_iota(jnp.int32, (count, LANES), 1)
        same = jnp.where(row == column, 1.0, 0.0).astype(BF16)
        rows_ref[...] = dot(same, small_ref[...], ((1,), (1,)))

    x = x_ref[micro].astype(F32)
    inverse = lax.rsqrt(jnp.mean(x * x, -1, keepdims=True) + EPSILON)
    at = shape["gain_at"]
    n1_ref[micro] = (x * inverse * rows_ref[at : at + 1, :]).astype(BF16)
    pre = dot(n1_ref[micro], w_ref[...])
    turned = rotate_pairs(pre[:, :rotated], cos_ref[0], sin_ref[0], 1)
    qkv_ref[0, :, :rotated] = turned.astype(BF16)
    qkv_ref[0, :, rotated:] = pre[:, rotated:].astype(BF16)
    bias = bias_ref[0]
    lane = lax.broadcasted_iota(jnp.int32, (pre.shape[0], LANES), 1)
    sums = jnp.zeros((pre.shape[0], LANES), F32)
    for head in range(heads):
        group = head // share
        key_at = (heads + group) * HEAD_DIM
        value_at = rotated + group * HEAD_DIM
        query = qkv_ref[0, :, head * HEAD_DIM : (head + 1) * HEAD_DIM]
        key = qkv_ref[0, :, key_at : key_at + HEAD_DIM]
        value = qkv_ref[0, :, value_at : value_at + HEAD_DIM]
        scores = dot(query * SCORE_SCALE, key, ((1,), (1,))) + bias
        highest = jnp.max(scores, -1, keepdims=True)
        exponent = jnp.exp(scores - highest)
        total = jnp.sum(exponent, -1, keepdims=True)
        weights = (exponent * (1.0 / total)).astype(BF16)
        merged_ref[0, :, head * HEAD_DIM : (head + 1) * HEAD_DIM] = dot(weights, value).astype(BF16)
        sums = jnp.where(lane == head, highest + jnp.log(total), sums)
    lse_ref[0] = sums
    rows = out_refs[0].shape[1]
    for i, out_ref in enumerate(out_refs):
        out_ref[0] = dot(merged_ref[0, i * rows : (i + 1) * rows, :], wo_ref[...]).astype(BF16)


def attention_backward_kernel(shape, spots_ref, *refs):
    packs, refs = refs[: shape["packs"]], refs[shape["packs"] :]
    slots, refs = refs[: shape["slots"]], refs[shape["slots"] :]
    cos_ref, sin_ref, bias_ref, qkv_ref, lse_ref, n1_ref, merged_ref = refs[:7]
    x_ref, n2_ref, logits_ref, mlp_ref = refs[7:11]
    refs = refs[11:]
    out_refs, refs = refs[: shape["slots"]], refs[shape["slots"] :]
    grads, refs = refs[: shape["packs"]], refs[shape["packs"] :]
    ga_ref, w_ref, wo_ref, dqkv_ref, turned_ref, gain_ref, dw_ref, dwo_ref, ds_ref, semaphores = refs
    heads, kv_heads = shape["heads"], shape["kv_heads"]
    share = heads // kv_heads
    rotated = (heads + kv_heads) * HEAD_DIM
    micro = pl.program_id(0)

    @pl.when(micro == 0)
    def _():
        copies = row_copies(slots, ga_ref) + weight_copies(shape, spots_ref, packs, w_ref, wo_ref)
        fetch(copies, semaphores)
        gain_ref[...] = jnp.zeros_like(gain_ref)
        gain_ref[1:2, :] = mlp_ref[...]

    grad_merged = dot(ga_ref[micro], wo_ref[...], ((1,), (1,))).astype(BF16)
    bias = bias_ref[0]
    for group in range(kv_heads):
        key_at = (heads + group) * HEAD_DIM
        value_at = rotated + group * HEAD_DIM
        key = qkv_ref[0, :, key_at : key_at + HEAD_DIM] * SCORE_SCALE
        value = qkv_ref[0, :, value_at : value_at + HEAD_DIM]
        grad_key, grad_value = None, None
        for head in range(group * share, (group + 1) * share):
            query = qkv_ref[0, :, head * HEAD_DIM : (head + 1) * HEAD_DIM]
            grad_rows = grad_merged[:, head * HEAD_DIM : (head + 1) * HEAD_DIM]
            scores = dot(query, key, ((1,), (1,))) + bias
            chance = jnp.exp(scores - lse_ref[0, :, head : head + 1])
            weights = chance.astype(BF16)
            grad_chance = dot(grad_rows, value, ((1,), (1,)))
            delta = jnp.sum(chance * grad_chance, -1, keepdims=True)
            grad_raw = (chance * (grad_chance - delta)).astype(BF16)
            turned_ref[:, head * HEAD_DIM : (head + 1) * HEAD_DIM] = dot(grad_raw, key)
            key_part = dot(grad_raw, query, ((0,), (0,)))
            value_part = dot(weights, grad_rows, ((0,), (0,)))
            grad_key = key_part if grad_key is None else grad_key + key_part
            grad_value = value_part if grad_value is None else grad_value + value_part
        turned_ref[:, key_at : key_at + HEAD_DIM] = grad_key * SCORE_SCALE
        dqkv_ref[micro, :, value_at : value_at + HEAD_DIM] = grad_value.astype(BF16)
    back = rotate_pairs(turned_ref[...], cos_ref[0], sin_ref[0], -1)
    dqkv_ref[micro, :, :rotated] = back.astype(BF16)
    rows = out_refs[0].shape[1]
    first = dot(dqkv_ref[micro], w_ref[...], ((1,), (1,)))
    for i, out_ref in enumerate(out_refs):
        out_ref[0] = first[i * rows : (i + 1) * rows, :].astype(BF16)
    x = x_ref[0].astype(F32)
    unit = x * lax.rsqrt(jnp.mean(x * x, -1, keepdims=True) + EPSILON)
    gain_ref[0:1, :] += jnp.sum(first * unit, 0, keepdims=True)

    @pl.when(micro == pl.num_programs(0) - 1)
    def _():
        def flat(ref):
            return ref[...].reshape(ref.shape[0] * ref.shape[1], ref.shape[2])

        dw = dot(flat(n1_ref), flat(dqkv_ref), ((0,), (0,))).astype(BF16)
        dwo = dot(flat(merged_ref), flat(ga_ref), ((0,), (0,))).astype(BF16)
        row = lax.broadcasted_iota(jnp.int32, (gain_ref.shape[0], LANES), 0)
        column = lax.broadcasted_iota(jnp.int32, (gain_ref.shape[0], LANES), 1)
        spread = jnp.where((row < 2) & (column == row + shape["gain_at"]), 1.0, 0.0)
        gains = lax.dot_general(
            gain_ref[...],
            spread,
            (((0,), (0,)), ((), ())),
            precision=lax.Precision.HIGHEST,
            preferred_element_type=F32,
        )
        ds = (gains + dot(n2_ref[...], logits_ref[...], ((0,), (0,)))).astype(BF16)
        if shape["whole"]:
            grads[0][...] = dw
            grads[1][...] = dwo
            grads[2][...] = ds
        else:
            dw_ref[...] = dw
            dwo_ref[...] = dwo
            ds_ref[...] = ds
            pack_rows, part, columns = shape["pack_rows"], shape["weight_rows"], shape["qkv_columns"]
            wide = shape["merged_columns"]
            for slot, grad_ref in enumerate(grads):
                spot = spots_ref[slot]
                at = pl.multiple_of(spot * pack_rows, pack_rows)
                grad_ref[:, :columns] = dw_ref[pl.ds(at, pack_rows), :]
                grad_ref[:, columns : columns + LANES] = ds_ref[pl.ds(at, pack_rows), :]
                at = pl.multiple_of(spot * part, part)
                for i in range(pack_rows // part):
                    grad_ref[i * part : (i + 1) * part, columns + LANES :] = dwo_ref[
                        pl.ds(at, part), i * wide : (i + 1) * wide
                    ]


def per_micro(shape):
    return pl.BlockSpec((1,) + tuple(shape[1:]), lambda m, s: (m,) + (0,) * (len(shape) - 1))


def fixed(shape):
    return pl.BlockSpec(tuple(shape), lambda m, s: (0,) * len(shape))


def attention_forward(shape, spots, packs, slots, cosine, sine, bias):
    micros, rows, width = slots[0].shape
    group = rows * len(slots)
    columns, merged = shape["qkv_columns"], shape["heads"] * HEAD_DIM
    outs = [jax.ShapeDtypeStruct((micros, rows, width), BF16) for _ in slots]
    specs = [per_micro(o.shape) for o in outs]
    more = [
        jax.ShapeDtypeStruct((micros, group, width), BF16),
        jax.ShapeDtypeStruct((micros, group, width), BF16),
        jax.ShapeDtypeStruct((width, LANES), BF16),
        jax.ShapeDtypeStruct((LANES // 2, width), F32),
        jax.ShapeDtypeStruct((micros, group, columns), BF16),
        jax.ShapeDtypeStruct((micros, group, merged), BF16),
        jax.ShapeDtypeStruct((micros, group, LANES), F32),
    ]
    specs += [fixed(o.shape) for o in more[:4]] + [per_micro(o.shape) for o in more[4:]]
    results = pl.pallas_call(
        functools.partial(attention_forward_kernel, shape),
        grid_spec=pltpu.PrefetchScalarGridSpec(
            num_scalar_prefetch=1,
            grid=(micros,),
            in_specs=[anywhere() for _ in packs + slots]
            + [per_micro(cosine.shape), per_micro(sine.shape), per_micro(bias.shape)],
            out_specs=specs,
            scratch_shapes=[
                pltpu.VMEM((width, columns), BF16),
                pltpu.VMEM((merged, width), BF16),
                pltpu.SemaphoreType.DMA((shape["copies"],)),
            ],
        ),
        out_shape=outs + more,
        name="attention_forward",
    )(spots, *packs, *slots, cosine, sine, bias)
    return (results[: len(slots)],) + tuple(results[len(slots) :])


def attention_backward(shape, spots, packs, slots, by_micro, at_once):
    micros, rows, width = slots[0].shape
    group = rows * len(slots)
    columns, merged_rows = shape["qkv_columns"], shape["heads"] * HEAD_DIM
    outs = [jax.ShapeDtypeStruct((micros, rows, width), BF16) for _ in slots]
    grads = [jax.ShapeDtypeStruct(pack.shape, BF16) for pack in packs]
    results = pl.pallas_call(
        functools.partial(attention_backward_kernel, shape),
        grid_spec=pltpu.PrefetchScalarGridSpec(
            num_scalar_prefetch=1,
            grid=(micros,),
            in_specs=[anywhere() for _ in packs + slots]
            + [per_micro(v.shape) for v in by_micro[:5]]
            + [fixed(v.shape) for v in at_once[:2]]
            + [per_micro(by_micro[5].shape)]
            + [fixed(v.shape) for v in at_once[2:]],
            out_specs=[per_micro(o.shape) for o in outs] + [fixed(g.shape) for g in grads],
            scratch_shapes=[
                pltpu.VMEM((micros, group, width), BF16),
                pltpu.VMEM((width, columns), BF16),
                pltpu.VMEM((merged_rows, width), BF16),
                pltpu.VMEM((micros, group, columns), BF16),
                pltpu.VMEM((group, (shape["heads"] + shape["kv_heads"]) * HEAD_DIM), F32),
                pltpu.VMEM((8, width), F32),
                pltpu.VMEM((width, columns), BF16),
                pltpu.VMEM((merged_rows, width), BF16),
                pltpu.VMEM((width, LANES), BF16),
                pltpu.SemaphoreType.DMA((shape["copies"],)),
            ],
        ),
        out_shape=outs + grads,
        name="attention_backward",
    )(spots, *packs, *slots, *by_micro[:5], *at_once[:2], by_micro[5], *at_once[2:])
    return list(results[: len(slots)]), list(results[len(slots) :])


def experts_kernel(shape, table_ref, *refs):
    slots, cores, ys, zs = shape["slots"], shape["cores"], shape["ys"], shape["zs"]
    own, hidden = shape["own"], shape["hidden"]
    x_slots, refs = refs[:slots], refs[slots:]
    beside, refs = refs[:slots], refs[slots:]
    gu_parts, refs = refs[: cores * ys], refs[cores * ys :]
    dn_parts, refs = refs[: cores * ys], refs[cores * ys :]
    wr_ref, gate_ref, x_out, gm_out = refs[:4]
    back_outs, refs = refs[4 : 4 + slots], refs[4 + slots :]
    mixed_outs, refs = refs[:slots], refs[slots:]
    act_outs, refs = refs[:cores], refs[cores:]
    dgu_outs, refs = refs[:cores], refs[cores:]
    x_ref, gm_ref, mask_ref, wgu_ref, wdn_ref, act_ref, dgu_ref, back_ref, mixed_ref = refs[:9]
    in_sems, out_sems = refs[9:]
    rows, width = x_slots[0].shape[0], x_ref.shape[1]
    part = width // (ys * zs)
    wide, tall = 2 * hidden * own, hidden * own
    local = cores * own

    fetched = [[] for _ in range(cores + 2)]
    for i in range(slots):
        at = pl.ds(i * rows, rows)
        fetched[0].append((x_slots[i].at[:, pl.ds(0, width)], x_ref.at[at, :]))
        fetched[cores].append((x_slots[i].at[:, pl.ds(width, LANES)], mask_ref.at[at, :]))
        fetched[cores + 1].append((beside[i], gm_ref.at[at, :]))
    step = hidden // ys
    for c in range(cores):
        for s in range(ys):
            y = table_ref[local + s]
            for z in range(zs):
                at = pl.multiple_of((z * ys + y) * part, part)
                goal = wgu_ref.at[pl.ds(at, part), pl.ds(c * wide, wide)]
                fetched[c].append((gu_parts[c * ys + s].at[z], goal))
            for e in range(own):
                at = pl.multiple_of((c * own + e) * hidden + y * step, step)
                goal = wdn_ref.at[pl.ds(at, step), :]
                fetched[cores + 1].append((dn_parts[c * ys + s].at[e], goal))
    used = 0
    for group in fetched:
        for i, (source, goal) in enumerate(group):
            group[i] = pltpu.make_async_copy(source, goal, in_sems.at[used])
            group[i].start()
            used += 1

    def arrive(group):
        for copy in fetched[group]:
            copy.wait()

    leaving = []

    def leave(source, goal):
        leaving.append(pltpu.make_async_copy(source, goal, out_sems.at[len(leaving)]))
        leaving[-1].start()

    pre = []
    for c in range(cores):
        arrive(c)
        if c == 0:
            leave(x_ref, x_out)
        pre.append(dot(x_ref[...], wgu_ref[:, c * wide : (c + 1) * wide]))
    arrive(cores)
    total = slots * rows
    lane = lax.broadcasted_iota(jnp.int32, (total, LANES), 1)
    named = mask_ref[...].astype(F32) > 0.5
    logits = jnp.where(named, dot(x_ref[...], wr_ref[...]), NEGATIVE)
    highest = jnp.max(logits, -1, keepdims=True)
    exponent = jnp.where(named, jnp.exp(logits - highest), 0.0)
    gates = exponent / jnp.sum(exponent, -1, keepdims=True)
    gate_ref[...] = gates
    arrive(cores + 1)
    leave(gm_ref, gm_out)
    grad_act = dot(gm_ref[...], wdn_ref[...], ((1,), (1,)))
    picked = jnp.zeros((total, LANES), F32)
    for c in range(cores):
        for e in range(own):
            j = c * own + e
            mine = lane == table_ref[j]
            gate = jnp.sum(jnp.where(mine, gates, 0.0), -1, keepdims=True)
            base = 2 * hidden * e
            gate_pre = pre[c][:, base : base + hidden]
            up_pre = pre[c][:, base + hidden : base + 2 * hidden]
            grad_one = grad_act[:, j * hidden : (j + 1) * hidden]
            sig = jax.nn.sigmoid(gate_pre)
            silu = gate_pre * sig
            activated = (silu * up_pre).astype(BF16).astype(F32)
            found = jnp.sum(activated * grad_one, -1, keepdims=True)
            picked = jnp.where(mine, found, picked)
            act_ref[c, :, e * hidden : (e + 1) * hidden] = (activated * gate).astype(BF16)
            grad_one = grad_one * gate
            base = 2 * hidden * j
            dgu_ref[:, base : base + hidden] = (
                grad_one * up_pre * sig * (1.0 + gate_pre * (1.0 - sig))
            ).astype(BF16)
            dgu_ref[:, base + hidden : base + 2 * hidden] = (grad_one * silu).astype(BF16)
        leave(dgu_ref.at[:, pl.ds(c * wide, wide)], dgu_outs[c])
        leave(act_ref.at[c], act_outs[c])

    coarse = picked.astype(BF16)
    back_ref[:, width : width + LANES] = coarse
    back_ref[:, width + LANES :] = (picked - coarse.astype(F32)).astype(BF16)
    back_ref[:, :width] = dot(dgu_ref[...], wgu_ref[...], ((1,), (1,))).astype(BF16)

    def leave_slots(source, goals):
        for i in range(slots):
            leave(source.at[pl.ds(i * rows, rows), :], goals[i])

    leave_slots(back_ref, back_outs)
    if tall % LANES == 0:
        acts = jnp.concatenate([act_ref[c] for c in range(cores)], 1)
        mixed = dot(acts, wdn_ref[...])
    else:
        mixed = sum(dot(act_ref[c], wdn_ref[c * tall : (c + 1) * tall, :]) for c in range(cores))
    mixed_ref[...] = mixed.astype(BF16)
    leave_slots(mixed_ref, mixed_outs)
    for copy in leaving:
        copy.wait()


def run_experts(shape, table, x_slots, beside, gu_parts, dn_parts, wr):
    rows, width = x_slots[0].shape[0], wr.shape[0]
    total = rows * len(x_slots)
    cores, own, hidden = shape["cores"], shape["own"], shape["hidden"]
    outs = [
        jax.ShapeDtypeStruct((total, LANES), F32),
        jax.ShapeDtypeStruct((total, width), BF16),
        jax.ShapeDtypeStruct((total, width), BF16),
    ]
    outs += [jax.ShapeDtypeStruct((rows, width + 2 * LANES), BF16) for _ in x_slots]
    outs += [jax.ShapeDtypeStruct((rows, width), BF16) for _ in x_slots]
    outs += [jax.ShapeDtypeStruct((total, own * hidden), BF16) for _ in range(cores)]
    outs += [jax.ShapeDtypeStruct((total, 2 * own * hidden), BF16) for _ in range(cores)]
    shape = dict(shape, slots=len(x_slots))
    copies = 3 * len(x_slots) + cores * shape["ys"] * (shape["zs"] + own)
    operands = x_slots + beside + gu_parts + dn_parts
    return pl.pallas_call(
        functools.partial(experts_kernel, shape),
        in_specs=[pl.BlockSpec(memory_space=pltpu.SMEM)] + [anywhere() for _ in operands] + [on_chip()],
        out_specs=[on_chip()] + [anywhere() for _ in outs[1:]],
        out_shape=outs,
        scratch_shapes=[
            pltpu.VMEM((total, width), BF16),
            pltpu.VMEM((total, width), BF16),
            pltpu.VMEM((total, LANES), BF16),
            pltpu.VMEM((width, cores * own * 2 * hidden), BF16),
            pltpu.VMEM((cores * own * hidden, width), BF16),
            pltpu.VMEM((cores, total, own * hidden), BF16),
            pltpu.VMEM((total, cores * own * 2 * hidden), BF16),
            pltpu.VMEM((total, width + 2 * LANES), BF16),
            pltpu.VMEM((total, width), BF16),
            pltpu.SemaphoreType.DMA((copies,)),
            pltpu.SemaphoreType.DMA((2 + 2 * cores + 2 * len(x_slots),)),
        ],
        compiler_params=pltpu.CompilerParams(vmem_limit_bytes=60 << 20),
        name="experts",
    )(table, *operands, wr)


def pack_kernel(hidden, gate_ref, up_ref, out_ref):
    for z in range(out_ref.shape[0]):
        out_ref[z, :, :hidden] = gate_ref[0, :, z * hidden : (z + 1) * hidden]
        out_ref[z, :, hidden:] = up_ref[0, :, z * hidden : (z + 1) * hidden]


def pack_experts(w_gate, w_up, zs):
    own, part, hidden_all = w_gate.shape
    hidden = hidden_all // zs
    return pl.pallas_call(
        functools.partial(pack_kernel, hidden),
        grid=(own,),
        in_specs=[pl.BlockSpec((1, part, hidden_all), lambda e: (e, 0, 0))] * 2,
        out_specs=pl.BlockSpec((zs, part, 2 * hidden), lambda e: (0, 0, e)),
        out_shape=jax.ShapeDtypeStruct((zs, part, own * 2 * hidden), BF16),
        name="pack_experts",
    )(w_gate, w_up)


def unpack_kernel(hidden, in_ref, gate_ref, up_ref):
    for z in range(in_ref.shape[0]):
        gate_ref[0, :, z * hidden : (z + 1) * hidden] = in_ref[z, :, :hidden].astype(F32)
        up_ref[0, :, z * hidden : (z + 1) * hidden] = in_ref[z, :, hidden:].astype(F32)


def unpack_experts(packed, own):
    zs, part, wide = packed.shape
    hidden = wide // own // 2
    out = jax.ShapeDtypeStruct((own, part, zs * hidden), F32)
    return pl.pallas_call(
        functools.partial(unpack_kernel, hidden),
        grid=(own,),
        in_specs=[pl.BlockSpec((zs, part, 2 * hidden), lambda e: (0, 0, e))],
        out_specs=[pl.BlockSpec((1, part, zs * hidden), lambda e: (e, 0, 0))] * 2,
        out_shape=[out, out],
        name="unpack_experts",
    )(packed)


def per_device(
    tokens,
    cotangent,
    attn_gain,
    mlp_gain,
    w_query,
    w_key,
    w_value,
    w_out,
    w_router,
    w_gate,
    w_up,
    w_down,
    shuffle,
    routes,
    lengths,
):
    micros, rows, width = tokens.shape
    dp_count, members = lax.axis_size("dp"), lax.axis_size("expert")
    devices = dp_count * members
    rings = Rings(dp_count, members)
    zn, yn, xn, cn = rings.z, rings.y, rings.x, rings.core
    group_rows = rows * members
    experts_all = w_router.shape[1]
    own_experts, model_part, hidden_all = w_gate.shape
    hidden_part = hidden_all // zn
    heads, kv_heads = HEADS // members, KV_HEADS // members
    weight_rows = w_query.shape[0]
    home_rows = micros * rows

    phases = Phases()

    def over_members(value):
        return phases.start(rings.gather_two(value, "c", "x"))

    def sum_members(parts):
        parts = [[parts[s * cn + t] for s in range(xn)] for t in range(cn)]
        return phases.start(rings.reduce_two(parts, "x", "c"))

    def line(columns):
        return [slot for column in columns for slot in column]

    def by_member(w):
        return w.reshape(weight_rows, members, w.shape[1] // members)

    small = jnp.concatenate([w_router, attn_gain[:, None], mlp_gain[:, None]], 1)
    small = jnp.pad(small, ((0, 0), (0, LANES - experts_all - 2)))
    small = jnp.broadcast_to(small[:, None, :], (weight_rows, members, LANES))
    mine = jnp.concatenate([by_member(w_query), by_member(w_key), by_member(w_value), small], 2)
    mine = lax.all_to_all(mine.transpose(1, 0, 2), "expert", 0, 0)
    small_at = mine.shape[2]
    qkv_columns = small_at - LANES
    pack_rows = members * weight_rows
    mine = mine.reshape(pack_rows, small_at)
    to_heads = [(s, (s % dp_count) * members + s // dp_count) for s in range(devices)]
    to_home = [(t, s) for s, t in to_heads]
    out_mine = lax.ppermute(w_out, ALL, to_heads)
    weights_started = []
    group_tokens = phases.start(paced(rings.gather_two(tokens, "c", "x"), weights_started))
    gate_up = pack_experts(w_gate, w_up, zn)
    begun = phases.start(make(lambda: (mine, gate_up, out_mine, routes)))
    phases.phase()
    (mine, gate_up, out_mine, routes) = begun.result
    merged_columns = width // members
    pack = jnp.concatenate(
        [out_mine[:, i * merged_columns : (i + 1) * merged_columns] for i in range(members)], 0
    )
    pack = jnp.concatenate([mine, pack], 1)
    whole = weight_rows % 16 != 0
    attention_shape = {
        "heads": heads,
        "kv_heads": kv_heads,
        "whole": whole,
        "pack_rows": pack_rows,
        "weight_rows": weight_rows,
        "qkv_columns": qkv_columns,
        "merged_columns": merged_columns,
        "slots": members,
        "gain_at": experts_all,
        "packs": 3 if whole else dp_count,
        "copies": micros * members + (3 if whole else dp_count * (2 + members)),
    }
    inputs = tokens.astype(F32)
    inv_first = lax.rsqrt(jnp.mean(inputs * inputs, -1, keepdims=True) + EPSILON)
    unit_first = inputs * inv_first

    grad_result = cotangent.astype(F32)
    grad_moe = (RESIDUAL_SCALE * grad_result).astype(BF16).reshape(home_rows, width)
    pack, routes, w_down, grad_moe = tie(pack, routes, w_down, grad_moe)
    packs = phases.start(rings.gather_two(pack, "z", "y"))
    weights_started.append(True)
    dealt = lax.all_to_all(
        routes.reshape(micros, dp_count, rows // dp_count, routes.shape[2]), "dp", 1, 1
    ).reshape(micros, rows, routes.shape[2])
    work = phases.start(make(lambda: (grad_moe, dealt)))
    phases.phase()
    grad_moe, dealt = work.result
    beside = phases.start(rings.gather_two(grad_moe, "z", "x"))
    work = phases.start(make(lambda: dealt))
    phases.phase()
    dealt = work.result
    lane_ids = jnp.arange(LANES, dtype=jnp.int32)
    hot = jnp.sum((dealt[:, :, :, None] == lane_ids).astype(F32), 2).astype(BF16)
    place = (shuffle[:, 0, :, None] == jnp.arange(rows, dtype=jnp.int32)).astype(BF16)
    named = jnp.einsum("mir,mix->mrx", place, hot, preferred_element_type=F32).astype(BF16)

    row_at = jnp.concatenate(
        [
            (rings.origin("x", s) * cn + rings.origin("c", t)) * rows
            + jnp.arange(rows, dtype=jnp.int32)
            for s in range(xn)
            for t in range(cn)
        ]
    )
    row_at, dealt = tie(row_at, dealt)
    half = HEAD_DIM // 2
    lane = jnp.arange(LANES, dtype=jnp.int32)
    inverse = ROPE_BASE ** (-((lane % half).astype(F32) * 2.0) / HEAD_DIM)
    sign = jnp.where(lane % HEAD_DIM < half, -1.0, 1.0)
    doc_lengths = lengths[:, 0]
    doc_ends = jnp.cumsum(doc_lengths, 1)
    doc_starts = doc_ends - doc_lengths
    segment = jnp.sum((row_at[None, :, None] >= doc_ends[:, None, :]).astype(jnp.int32), 2)
    docs = jnp.arange(doc_lengths.shape[1], dtype=jnp.int32)
    start = jnp.sum(jnp.where(segment[:, :, None] == docs, doc_starts[:, None, :], 0), 2)
    position = row_at[None, :] - start
    angles = position.astype(F32)[:, :, None] * inverse
    cosine, sine = jnp.cos(angles), jnp.sin(angles) * sign
    allowed = segment[:, :, None] == segment[:, None, :]
    bias = jnp.where(allowed & (row_at[None, :] <= row_at[:, None]), 0.0, NEGATIVE)

    tables = phases.start(make(lambda: (cosine, sine, bias, named, gate_up, w_down)))
    phases.phase()
    cosine, sine, bias, named, gate_up, w_down = tables.result
    gate_up = lax.all_to_all(gate_up, "dp", 0, 0, axis_index_groups=rings.z_groups)
    held = phases.start(make(lambda: w_down))
    packs, group_tokens = phases.finish(packs, group_tokens)
    w_down = held.result
    spots = jnp.stack(
        [rings.origin("z", t) * yn + rings.origin("y", s) for s in range(yn) for t in range(zn)]
    )
    if whole:
        packs = [in_order(column, rings.at["z"], zn) for column in packs]
        packs = [in_order([packs[s][z] for s in range(yn)], rings.at["y"], yn) for z in range(zn)]
        packs = jnp.stack([packs[z][y] for z in range(zn) for y in range(yn)])
        w_merge = packs[:, :, small_at:].reshape(dp_count, members, weight_rows, merged_columns)
        w_merge = w_merge.transpose(0, 2, 1, 3).reshape(dp_count * weight_rows, width)
        w_small = packs[:, :, qkv_columns:small_at].reshape(width, LANES)
        packs = [packs[:, :, :qkv_columns].reshape(width, qkv_columns), w_merge, w_small]
    else:
        packs = line(packs)

    down = rings.gather(w_down, "y")
    attention = phases.start(
        make(
            attention_forward,
            attention_shape,
            spots,
            packs,
            line(group_tokens),
            cosine,
            sine,
            bias,
        )
    )
    down_task = phases.start(make(lambda: down))
    (_, beside) = phases.finish(attention, beside)
    down = phases.start(make(lambda: [rings.gather(part, "c") for part in down_task.result]))
    attn_parts, group_in, n1, router_columns, small_rows, qkv, merged, lse = attention.result
    gain_first = small_rows[experts_all]
    gain_second = small_rows[experts_all + 1]
    attended = sum_members(attn_parts)
    for _ in range(xn - 1):
        phases.phase()
    gate_up = phases.start(make(lambda: gate_up))
    attended, down, gate_up = phases.finish(attended, down, gate_up)
    hidden = inputs + RESIDUAL_SCALE * attended
    inv_second = lax.rsqrt(jnp.mean(hidden * hidden, -1, keepdims=True) + EPSILON)
    unit_second = hidden * inv_second
    normed_second = (unit_second * gain_second).astype(BF16).reshape(home_rows, width)

    together = jnp.concatenate([normed_second, named.reshape(home_rows, LANES)], 1)
    group_x = phases.start(rings.gather_two(together, "z", "x"))
    gate_up = rings.gather(gate_up, "y")
    phases.phase()
    phases.phase()
    mine_too = phases.start(make(lambda: rings.gather(gate_up[0], "c")))
    gate_up = phases.start(make(lambda: gate_up[1:]))
    phases.finish(mine_too, gate_up)
    gate_up = phases.start(make(lambda: [rings.gather(part, "c") for part in gate_up.result]))
    group_x, gate_up = phases.finish(group_x, gate_up)
    gate_up = [mine_too.result] + gate_up
    gu_parts = [gate_up[s][c] for c in range(cn) for s in range(yn)]
    dn_parts = [down[s][c] for c in range(cn) for s in range(yn)]

    slots = [(s, t) for s in range(xn) for t in range(zn)]
    x_slots = [group_x[s][t] for s, t in slots]
    beside = [beside[s][t] for s, t in slots]
    chunk = min(len(slots), 8)
    chunks = len(slots) // chunk
    table = [
        (rings.at["x"] * cn + rings.origin("c", s)) * own_experts
        + jnp.arange(own_experts, dtype=jnp.int32)
        for s in range(cn)
    ]
    table.append(jnp.stack([rings.origin("y", s) for s in range(yn)]))
    table = jnp.concatenate(table)
    experts_shape = {"cores": cn, "ys": yn, "zs": zn, "own": own_experts, "hidden": hidden_part}
    results = [
        run_experts(
            experts_shape,
            table,
            x_slots[i * chunk : (i + 1) * chunk],
            beside[i * chunk : (i + 1) * chunk],
            gu_parts,
            dn_parts,
            router_columns,
        )
        for i in range(chunks)
    ]
    back = [part for pieces in results for part in pieces[3 : 3 + chunk]]
    mixed = [part for pieces in results for part in pieces[3 + chunk : 3 + 2 * chunk]]
    results = [pieces[:3] + pieces[3 + 2 * chunk :] for pieces in results]
    results = [pieces[0] if chunks == 1 else jnp.concatenate(pieces, 0) for pieces in zip(*results)]
    gates, x_all, gm_all = results[:3]
    acts, dgus = results[3 : 3 + cn], results[3 + cn :]
    back = [back[i * zn : (i + 1) * zn] for i in range(xn)]
    mixed = [mixed[i * zn : (i + 1) * zn] for i in range(xn)]

    def by_y(value, axis):
        return [lax.dynamic_index_in_dim(value, rings.origin("y", s), axis, False) for s in range(yn)]

    def product(core, kind, x, gm, coming):
        if kind == 0:
            term = dot(x, dgus[core], ((0,), (0,)))
        else:
            term = dot(acts[core], gm, ((0,), (0,)))
        return (term if coming is None else term + coming.astype(F32)).astype(BF16)

    def own_gu(x, coming):
        return by_y(product(0, 0, x, None, coming).reshape(zn, yn, model_part, -1), 1)

    def own_dn(gm, coming):
        value = product(0, 1, None, gm, coming)
        return by_y(value.reshape(own_experts, yn, hidden_part // yn, width), 1)

    def held(*values):
        return phases.start(make(lambda: values))

    rows_back = phases.start(rings.reduce_two(back, "z", "x", two_part))
    x, gm, coming = x_all, gm_all, [None, None]
    if cn > 1:
        work = held(product(1, 0, x, None, None), x, gm)
        phases.phase()
        other, x, gm = work.result
        coming[0] = rings.step(other, "c")
    first = min(1, zn - 1)
    other = [product(1, 1, None, gm, None)] if cn > 1 else []
    work = held(own_gu(x, coming[0]), other, gm, [row[first] for row in mixed])
    phases.phase()
    made, other, gm, mixed_first = work.result
    if cn > 1:
        coming[1] = rings.step(other[0], "c")
    groups = [(0, 2), (2, 4), (4, 5)] if own_experts == 5 else [(0, own_experts)]
    wide = 2 * hidden_part
    waiting = [[part[:, :, low * wide : high * wide] for part in made] for low, high in groups]
    grad_gu = []

    def next_group(*keep):
        nonlocal waiting
        if waiting:
            grad_gu.append(phases.start(rings.reduce(waiting[0], "y")))
            waiting = waiting[1:]
        work = held(waiting, *keep)
        phases.phase()
        waiting, *keep = work.result
        return keep

    for row, value in zip(mixed, mixed_first):
        row[first] = value
    moe_rows = phases.start(rings.reduce_two(mixed, "z", "x"))
    (gm, *coming) = next_group(gm, *([coming[1]] if cn > 1 else []))
    (grad_dn,) = next_group(own_dn(gm, coming[0] if coming else None))
    phases.finish(rows_back)
    grad_dealt = rows_back.result[:, :width]
    grad_gates = rows_back.result[:, width:]
    grad_gates = grad_gates[:, :LANES] + grad_gates[:, LANES:]
    own_gates = gates[:home_rows]
    grad_picked = own_gates * (grad_gates - jnp.sum(own_gates * grad_gates, -1, keepdims=True))
    grad_logits = grad_picked.astype(BF16)
    router_rows = small_rows.astype(BF16)
    grad_dealt = (grad_dealt + dot(grad_logits[:, : LANES // 2], router_rows)).astype(BF16)
    grad_normed_second = grad_dealt.astype(F32).reshape(micros, rows, width)
    scaled_second = grad_normed_second * gain_second
    grad_hidden = grad_result + inv_second * (
        scaled_second - unit_second * jnp.mean(scaled_second * unit_second, -1, keepdims=True)
    )
    mlp_gain_grad = jnp.sum(grad_normed_second * unit_second, (0, 1))[None]
    grad_attn = (RESIDUAL_SCALE * grad_hidden).astype(BF16)

    grad_attn = over_members(grad_attn)
    while waiting:
        next_group()
    grad_gu = jnp.concatenate([part.astype(BF16) for part in phases.finish(*grad_gu)], 2)
    work = held(grad_gu, grad_dn)
    phases.finish(grad_attn, moe_rows, work)
    grad_gu, grad_dn = work.result
    grad_gu = lax.all_to_all(grad_gu, "dp", 0, 0, axis_index_groups=rings.z_groups)
    grad_dn = phases.start(rings.reduce(grad_dn, "y"))

    attention = phases.start(
        make(
            attention_backward,
            attention_shape,
            spots,
            packs,
            line(grad_attn.result),
            [cosine, sine, bias, qkv, lse, group_in],
            [n1, merged, normed_second, grad_logits, mlp_gain_grad],
        )
    )
    phases.finish(attention)
    first_parts, weight_grads = attention.result

    if whole:
        grad_qkv, grad_out, grad_small = weight_grads
        grad_out = grad_out.reshape(dp_count, weight_rows, members, merged_columns).transpose(0, 2, 1, 3)
        both = jnp.concatenate(
            [
                grad_qkv.reshape(dp_count, pack_rows, qkv_columns),
                grad_small.reshape(dp_count, pack_rows, LANES),
                grad_out.reshape(dp_count, pack_rows, merged_columns),
            ],
            2,
        )
        weight_grads = [
            lax.dynamic_index_in_dim(both, spots[i], 0, False) for i in range(dp_count)
        ]
    both = phases.start(
        rings.reduce_two([[weight_grads[s * zn + t] for t in range(zn)] for s in range(yn)], "z", "y")
    )
    phases.phase()
    grad_gu = held(grad_gu)
    grad_normed_first = sum_members(first_parts)
    both, grad_gu, grad_dn, grad_normed_first, moe_rows = phases.finish(
        both, grad_gu, grad_dn, grad_normed_first, moe_rows
    )
    grad_gate, grad_up = unpack_experts(grad_gu[0], own_experts)
    moe_rows = moe_rows.astype(BF16).reshape(micros, rows, width)
    output = (hidden + RESIDUAL_SCALE * moe_rows.astype(F32)).astype(BF16)
    scaled_first = grad_normed_first * gain_first
    grad_tokens = grad_hidden + inv_first * (
        scaled_first - unit_first * jnp.mean(scaled_first * unit_first, -1, keepdims=True)
    )
    grad_out = [
        both[i * weight_rows : (i + 1) * weight_rows, small_at:] for i in range(members)
    ]
    grad_out = lax.ppermute(jnp.concatenate(grad_out, 1).astype(BF16), ALL, to_home).astype(F32)
    home = both[:, :small_at].reshape(members, weight_rows, small_at)
    home = lax.all_to_all(home.astype(BF16), "expert", 0, 0).astype(F32)

    def columns(start, count):
        return jnp.concatenate([home[i, :, start : start + count] for i in range(members)], 1)

    query_columns, key_columns = heads * HEAD_DIM, kv_heads * HEAD_DIM
    grad_query = columns(0, query_columns)
    grad_key = columns(query_columns, key_columns)
    grad_value = columns(query_columns + key_columns, key_columns)

    small = jnp.sum(home[:, :, qkv_columns:], 0)
    grad_w_router = small[:, :experts_all]
    grad_attn_gain, grad_mlp_gain = small[:, experts_all], small[:, experts_all + 1]

    return (
        output,
        grad_tokens,
        grad_attn_gain,
        grad_mlp_gain,
        grad_query,
        grad_key,
        grad_value,
        grad_out,
        grad_w_router,
        grad_gate,
        grad_up,
        grad_dn,
    )


def solution(mesh):
    rows = P(None, ALL, None)
    placed = (rows, rows, P(ALL), P(ALL)) + (P(ALL, None),) * 5
    placed += (P("expert", "dp", None),) * 3 + (rows, rows, P(None, "dp", None))
    results = (rows, rows, P(ALL), P(ALL)) + (P(ALL, None),) * 5
    results += (P("expert", "dp", None),) * 3
    return jax.shard_map(per_device, mesh=mesh, in_specs=placed, out_specs=results, check_vma=False)
```
